512 devices in a mesh: group: 2 (over y_lo), seq: 32 (over x, y_hi, core), mp: 8 (over z).
Axes of the slice: x: 4, y: 8 (y_hi: 4, y_lo: 2; y = y_hi * 2 + y_lo), z: 8, core: 2. Of those that a mesh axis runs over, the one named last changes fastest.
Arguments:
- student_hidden: bfloat16 [2, 4096, 3072], P('group', 'seq', 'mp'), may hold values from -6 to 6
- student_cond: float32 [2, 3072], P(None, 'seq'), may hold values from -6 to 6
- student_mod: bfloat16 [3072, 2, 3072], P('seq', 'group', 'mp'), may hold values from -0.109375 to 0.109375
- student_out: bfloat16 [3072, 64], P('mp'), may hold values from -0.109375 to 0.109375
- timestep: int32 [2], P('group'), may hold values from 0 to 999
- noise: bfloat16 [2, 4096, 64], P('group', 'seq'), may hold values from -6 to 6
- teacher_embed: bfloat16 [64, 3072], P(None, 'mp'), may hold values from -0.75 to 0.75
- teacher_mod: bfloat16 [256, 2, 3072], P(None, None, 'mp'), may hold values from -0.375 to 0.375
- up_weight: bfloat16 [3072, 6144], P('seq', 'mp'), may hold values from -0.109375 to 0.109375
- down_weight: bfloat16 [6144, 3072], P('mp', 'seq'), may hold values from -0.078125 to 0.078125
- head_proj: bfloat16 [4, 3072, 128], P(None, 'mp'), may hold values from -0.109375 to 0.109375
- head_kernel: float32 [4, 3, 3, 128], replicated, may hold values from -3 to 3
- head_out: float32 [4, 128], replicated, may hold values from -2 to 2
- disc_layer: int32 [2, 4], P('group'), may hold values from 0 to 1, as said below
Outputs:
- latents: bfloat16 [2, 4096, 64], P('group', 'seq')
- logits: float32 [2, 4, 4096], P('group', None, 'seq')
- latent_grad: float32 [2, 4096, 64], P('group', 'seq')
The draws below stay inside these ranges and needn't reach their ends.
Inputs may be any that keep to these rules, and one draw needn't show every extreme that they name: `disc_layer`: for every sample, exactly half of the 4 heads read layer 0 and the other half layer 1, in an order drawn afresh.
All inputs are finite; a program needn't handle non-finite values.
Results may differ from the reference program's by a relative error of at most 0.029.
Values may be sent and summed in bfloat16 or wider, within the bound.
No kernel may reach another device: no remote copies, remote signals or barrier semaphores. Data moves between devices by JAX's collectives and lax.ppermute only.
A program may use at most 64 MiB of HBM per device.

```python
import math
import jax
import jax.numpy as jnp
from jax import lax

D = 3072
FFW = 6144
C = 64
FREQ = 256
HC = 128
HEADS = 4
GRID_W = 64
TOKENS = 4096
SAMPLES = 2


def draw_disc_layer(key, part):
    keys = jax.random.split(jax.random.fold_in(key, 17), SAMPLES)
    base_row = jnp.arange(HEADS, dtype=jnp.int32) % 2
    return jax.vmap(lambda row_key: jax.random.permutation(row_key, base_row))(keys)


def block_levels(key, dims, shards, low, high):
    level = 1.0
    for dim, blocks in shards:
        steps = jax.random.uniform(jax.random.fold_in(jax.random.fold_in(key, 6), dim), (blocks,), jnp.float32, low / len(shards), high / len(shards))
        level = level * jnp.repeat(jnp.exp(steps), dims[dim] // blocks).reshape((-1,) + (1,) * (len(dims) - 1 - dim))
    return level


def normal_values(key, extent, deviation, limit, cuts=(), held_as=jnp.bfloat16):
    result = deviation * jax.random.normal(key, extent, jnp.float32)
    if cuts:
        result = result * block_levels(key, extent, cuts, -0.22, 0.18)
    return jnp.clip(result, -limit, limit).astype(held_as)


def setup_inputs(seed: int = 0) -> dict:
    key_list = jax.random.split(jax.random.key(seed), 15)
    return {
        "student_hidden": normal_values(key_list[0], (SAMPLES, TOKENS, D), 1.0, 6.0, ((0, 2), (1, 32), (2, 8))),
        "student_cond": normal_values(key_list[1], (SAMPLES, D), 1.0, 6.0, ((1, 32),), jnp.float32),
        "student_mod": normal_values(key_list[2], (D, 2, D), D ** -0.5, 0.109375, ((0, 32), (1, 2), (2, 8))),
        "student_out": normal_values(key_list[3], (D, C), D ** -0.5, 0.109375, ((0, 8),)),
        "timestep": jax.random.randint(key_list[4], (SAMPLES,), 0, 1000).astype(jnp.int32),
        "noise": normal_values(key_list[5], (SAMPLES, TOKENS, C), 1.0, 6.0, ((0, 2), (1, 32))),
        "teacher_embed": normal_values(key_list[6], (C, D), C ** -0.5, 0.75, ((1, 8),)),
        "teacher_mod": normal_values(key_list[7], (FREQ, 2, D), FREQ ** -0.5, 0.375, ((2, 8),)),
        "up_weight": normal_values(key_list[8], (D, FFW), D ** -0.5, 0.109375, ((0, 32), (1, 8))),
        "down_weight": normal_values(key_list[9], (FFW, D), FFW ** -0.5, 0.078125, ((0, 8), (1, 32))),
        "head_proj": normal_values(key_list[10], (HEADS, D, HC), D ** -0.5, 0.109375, ((1, 8),)),
        "head_kernel": normal_values(key_list[11], (HEADS, 3, 3, HC), 0.5, 3.0, (), jnp.float32),
        "head_out": normal_values(key_list[12], (HEADS, HC), 0.3, 2.0, (), jnp.float32),
        "disc_layer": draw_disc_layer(jax.random.fold_in(key_list[14], 71), 0),
    }


EPSILON = 1e-06
GELU_COEF = 0.7978845608028654

def gelu_tanh(values):
    inner = GELU_COEF * (values + 0.044715 * values * values * values)
    return 0.5 * values * (1.0 + jnp.tanh(inner))

def gelu_slope(values):
    inner = GELU_COEF * (values + 0.044715 * values * values * values)
    tangent = jnp.tanh(inner)
    return 0.5 * (1.0 + tangent) + 0.5 * values * (1.0 - tangent * tangent) * GELU_COEF * (1.0 + 3.0 * 0.044715 * values * values)

def time_features(timestep, width):
    half_width = width // 2
    index = jnp.arange(half_width, dtype=jnp.float32)
    freqs = jnp.exp(-math.log(10000.0) * index / half_width)
    angles = timestep.astype(jnp.float32)[:, None] * freqs[None, :]
    return jnp.concatenate([jnp.cos(angles), jnp.sin(angles)], axis=-1)

def reference(student_hidden, student_cond, student_mod, student_out, timestep, noise, teacher_embed, teacher_mod, up_weight, down_weight, head_proj, head_kernel, head_out, disc_layer):
    highest = lax.Precision.HIGHEST
    hidden = student_hidden.astype(jnp.float32)
    tok_mean = lax.optimization_barrier(jnp.mean(hidden, -1, keepdims=True))
    tok_var = lax.optimization_barrier(jnp.mean((hidden - tok_mean) ** 2, -1, keepdims=True))
    smod = jnp.einsum('sk,kjd->sjd', student_cond, student_mod.astype(jnp.float32), precision=highest)
    normed = ((hidden - tok_mean) * lax.rsqrt(tok_var + EPSILON) * (1.0 + smod[:, 1:2]) + smod[:, 0:1]).astype(jnp.bfloat16)
    latents = jnp.einsum('std,dc->stc', normed.astype(jnp.float32), student_out.astype(jnp.float32), precision=highest).astype(jnp.bfloat16)
    level = timestep.astype(jnp.float32) / 1000.0
    retain = (1.0 - level)[:, None, None]
    noised = (retain * latents.astype(jnp.float32) + level[:, None, None] * noise.astype(jnp.float32)).astype(jnp.bfloat16)
    embedded = jnp.einsum('stc,cd->std', noised.astype(jnp.float32), teacher_embed.astype(jnp.float32), precision=highest).astype(jnp.bfloat16)
    tmod = jnp.einsum('sf,fjd->sjd', time_features(timestep, FREQ), teacher_mod.astype(jnp.float32), precision=highest)
    emb_f = embedded.astype(jnp.float32)
    mean_t = lax.optimization_barrier(jnp.mean(emb_f, -1, keepdims=True))
    var_t = lax.optimization_barrier(jnp.mean((emb_f - mean_t) ** 2, -1, keepdims=True))
    inv_std = lax.rsqrt(var_t + EPSILON)
    centered = (emb_f - mean_t) * inv_std
    mod_gain = 1.0 + tmod[:, 1:2]
    modulated = (centered * mod_gain + tmod[:, 0:1]).astype(jnp.bfloat16)
    preact = jnp.einsum('std,df->stf', modulated.astype(jnp.float32), up_weight.astype(jnp.float32), precision=highest)
    activated = gelu_tanh(preact).astype(jnp.bfloat16)
    block_out = (emb_f + jnp.einsum('stf,fd->std', activated.astype(jnp.float32), down_weight.astype(jnp.float32), precision=highest)).astype(jnp.bfloat16)
    layer_pick = disc_layer == 1
    head_w = head_proj.astype(jnp.float32)
    proj_embed = jnp.einsum('std,kdc->sktc', embedded.astype(jnp.float32), head_w, precision=highest)
    proj_block = jnp.einsum('std,kdc->sktc', block_out.astype(jnp.float32), head_w, precision=highest)
    projected = jnp.where(layer_pick[:, :, None, None], proj_block, proj_embed)
    grid_rows = TOKENS // GRID_W
    samples = projected.shape[0]
    grid = projected.reshape(samples, HEADS, grid_rows, GRID_W, HC)
    padded = jnp.pad(grid, ((0, 0), (0, 0), (1, 1), (1, 1), (0, 0)))
    conv_field = jnp.zeros(grid.shape, jnp.float32)
    for row_off in range(3):
        for col_off in range(3):
            conv_field = conv_field + head_kernel[:, row_off, col_off][None, :, None, None, :] * padded[:, :, row_off:row_off + grid_rows, col_off:col_off + GRID_W, :]
    gating = jax.nn.sigmoid(conv_field)
    weights_out = head_out[None, :, None, None, :]
    logits = lax.optimization_barrier(jnp.sum(conv_field * gating * weights_out, -1)).reshape(samples, HEADS, TOKENS)
    slope_grad = -weights_out * gating * (1.0 + conv_field * (1.0 - gating))
    padded_grad = jnp.pad(slope_grad, ((0, 0), (0, 0), (1, 1), (1, 1), (0, 0)))
    field_grad = jnp.zeros(grid.shape, jnp.float32)
    for row_off in range(3):
        for col_off in range(3):
            field_grad = field_grad + head_kernel[:, row_off, col_off][None, :, None, None, :] * padded_grad[:, :, 2 - row_off:2 - row_off + grid_rows, 2 - col_off:2 - col_off + GRID_W, :]
    field_grad = field_grad.reshape(samples, HEADS, TOKENS, HC).astype(jnp.bfloat16)
    head_grads = jnp.einsum('sktc,kdc->sktd', field_grad.astype(jnp.float32), head_w, precision=highest)
    pick_f = layer_pick.astype(jnp.float32)[:, :, None, None]
    grad_out = lax.optimization_barrier(jnp.sum(pick_f * head_grads, 1))
    grad_embed = lax.optimization_barrier(jnp.sum((1.0 - pick_f) * head_grads, 1))
    hidden_grad = jnp.einsum('std,fd->stf', grad_out.astype(jnp.bfloat16).astype(jnp.float32), down_weight.astype(jnp.float32), precision=highest)
    preact_grad = (hidden_grad * gelu_slope(preact)).astype(jnp.bfloat16)
    input_grad = jnp.einsum('stf,df->std', preact_grad.astype(jnp.float32), up_weight.astype(jnp.float32), precision=highest)
    scaled = input_grad * mod_gain
    mean_one = lax.optimization_barrier(jnp.mean(scaled, -1, keepdims=True))
    mean_two = lax.optimization_barrier(jnp.mean(scaled * centered, -1, keepdims=True))
    embed_grad = (scaled - mean_one - centered * mean_two) * inv_std + grad_out + grad_embed
    latent_part = jnp.einsum('std,cd->stc', embed_grad.astype(jnp.bfloat16).astype(jnp.float32), teacher_embed.astype(jnp.float32), precision=highest)
    latent_grad = retain * latent_part
    return (latents, logits, latent_grad)
```

```python
import math

import jax
import jax.numpy as jnp
from jax import lax
from jax.experimental import pallas as pl
from jax.experimental.pallas import tpu as pltpu
from jax.sharding import PartitionSpec as P

GRID_W = 64
EPSILON = 1e-06
GELU_COEF = 0.7978845608028654
INTERPRET = False

F32 = jnp.float32
BF16 = jnp.bfloat16
HIGHEST = lax.Precision.HIGHEST


def contract(left, right, left_dim, right_dim, precision=None):
    return lax.dot_general(
        left,
        right,
        (((left_dim,), (right_dim,)), ((), ())),
        precision=precision,
        preferred_element_type=F32,
    )


def gelu_tanh(values):
    inner = GELU_COEF * (values + 0.044715 * values * values * values)
    return 0.5 * values * (1.0 + jnp.tanh(inner))


def gelu_slope(values):
    inner = GELU_COEF * (values + 0.044715 * values * values * values)
    tangent = jnp.tanh(inner)
    return 0.5 * (1.0 + tangent) + 0.5 * values * (1.0 - tangent * tangent) * GELU_COEF * (
        1.0 + 3.0 * 0.044715 * values * values
    )


def time_features(timestep, width):
    half_width = width // 2
    index = jnp.arange(half_width, dtype=F32)
    freqs = jnp.exp(-math.log(10000.0) * index / half_width)
    angles = timestep.astype(F32) * freqs
    return jnp.concatenate([jnp.cos(angles), jnp.sin(angles)], axis=-1)


def exchange(value, axes):
    return lax.all_to_all(value, axes, 0, 0, tiled=False)


def spread(value, count):
    return jnp.broadcast_to(value[None], (count,) + value.shape)


def conv_body(edge_ref, parts_ref, embed_ref, taps_ref, pay_ref, grad_ref):
    copies, block_channels, extent = parts_ref.shape
    channels = embed_ref.shape[0]
    own = extent // 3
    block_part = jnp.sum(parts_ref[...].astype(F32), axis=0)
    embed = embed_ref[...]
    field_in = jnp.concatenate([embed[:block_channels] + block_part, embed[block_channels:]], axis=0)
    lane = lax.broadcasted_iota(jnp.int32, (channels, extent), 1)
    first = edge_ref[0]
    last = edge_ref[1]
    inside = (lane >= first) & (lane < last)
    column = lane % GRID_W
    left_ok = column > 0
    right_ok = column < GRID_W - 1

    def tap(row, col):
        place = 3 * row + col
        return taps_ref[:, place : place + 1]

    def convolve(grid, flip):
        before = jnp.where(left_ok, pltpu.roll(grid, 1, 1), 0.0)
        after = jnp.where(right_ok, pltpu.roll(grid, extent - 1, 1), 0.0)
        rows = []
        for row in range(3):
            if flip:
                rows.append(tap(row, 2) * before + tap(row, 1) * grid + tap(row, 0) * after)
            else:
                rows.append(tap(row, 0) * before + tap(row, 1) * grid + tap(row, 2) * after)
        if flip:
            rows = rows[::-1]
        return pltpu.roll(rows[0], GRID_W, 1) + rows[1] + pltpu.roll(rows[2], extent - GRID_W, 1)

    field = convolve(jnp.where(inside, field_in, 0.0), False)
    gating = jax.nn.sigmoid(field)
    scale = taps_ref[:, 9:10]
    terms = field * gating * scale
    slope = -scale * gating * (1.0 + field * (1.0 - gating))
    grad = convolve(jnp.where(inside, slope, 0.0), True)[:, own : 2 * own]
    grad_ref[...] = grad.astype(BF16)
    block_sum = jnp.sum(terms[:block_channels, own : 2 * own], axis=0, keepdims=True)
    embed_sum = jnp.sum(terms[block_channels:, own : 2 * own], axis=0, keepdims=True)
    sums = jnp.concatenate([block_sum, embed_sum], axis=0)
    high = sums.astype(BF16).astype(F32)
    low = sums - high
    tail = jnp.concatenate([high, low, jnp.zeros((12, own), F32)], axis=0)
    pay = jnp.concatenate([grad[:block_channels], tail], axis=0).astype(BF16)
    for copy in range(copies):
        pay_ref[copy] = pay


def conv_stage(edges, parts, embed, taps):
    copies, block_channels, extent = parts.shape
    channels = embed.shape[0]
    own = extent // 3
    vmem = pl.BlockSpec(memory_space=pltpu.VMEM)
    return pl.pallas_call(
        conv_body,
        in_specs=[pl.BlockSpec(memory_space=pltpu.SMEM), vmem, vmem, vmem],
        out_specs=[vmem, vmem],
        out_shape=[
            jax.ShapeDtypeStruct((copies, block_channels + 16, own), BF16),
            jax.ShapeDtypeStruct((channels, own), BF16),
        ],
        interpret=INTERPRET,
    )(edges, parts, embed, taps)


def per_device(
    student_hidden,
    student_cond,
    student_mod,
    student_out,
    timestep,
    noise,
    teacher_embed,
    teacher_mod,
    up_weight,
    down_weight,
    head_proj,
    head_kernel,
    head_out,
    disc_layer,
):
    groups = lax.axis_size("group")
    seqs = lax.axis_size("seq")
    mps = lax.axis_size("mp")
    seq_at = lax.axis_index("seq")
    mp_at = lax.axis_index("mp")
    hidden = student_hidden[0].astype(F32)
    tokens, local_width = hidden.shape
    width = local_width * mps
    latent_width = teacher_embed.shape[0]
    hidden_units = down_weight.shape[0]
    channels = head_proj.shape[2]
    share = 2 * channels // mps
    level = timestep[0].astype(F32) / 1000.0
    retain = 1.0 - level

    picks = [disc_layer[0, k] for k in range(4)]

    def first_of(layer):
        return jnp.where(picks[0] == layer, 0, jnp.where(picks[1] == layer, 1, 2))

    def last_of(layer):
        return jnp.where(picks[3] == layer, 3, jnp.where(picks[2] == layer, 2, 1))

    block_heads = (first_of(1), last_of(1))
    embed_heads = (first_of(0), last_of(0))
    order = block_heads + embed_heads

    tmod = jnp.einsum(
        "f,fjd->jd",
        time_features(timestep[0], teacher_mod.shape[0]),
        teacher_mod.astype(F32),
        precision=HIGHEST,
    )
    gain = 1.0 + tmod[1:2]
    queries = jnp.concatenate(
        [
            teacher_embed.astype(F32) * gain,
            gain,
            tmod[0:1],
            jnp.zeros((128 - latent_width - 2, local_width), F32),
        ],
        axis=0,
    ).astype(BF16)
    sorted_proj = jnp.concatenate(
        [lax.dynamic_index_in_dim(head_proj, k, 0, keepdims=False) for k in order], axis=1
    )
    ratio = seqs // mps
    rows = local_width // ratio
    mixed = jnp.concatenate([sorted_proj[:, : 2 * channels], queries.T], axis=1)
    sent = lax.dynamic_slice_in_dim(mixed, (seq_at % ratio) * rows, rows, 0)
    swap = [
        (at * mps + m, (ratio * m + at % ratio) * mps + at // ratio)
        for at in range(seqs)
        for m in range(mps)
    ]
    got = lax.ppermute(sent, ("seq", "mp"), swap)
    value_terms = contract(down_weight, got[:, : 2 * channels], 1, 0)
    query_terms = contract(up_weight, got[:, 2 * channels :], 0, 0)
    weight_terms = jnp.concatenate([value_terms, query_terms], axis=1).astype(BF16)
    unit_rows = hidden_units // seqs
    weight_terms = exchange(weight_terms.reshape(seqs, unit_rows, -1), "seq")
    weight_sum = jnp.sum(weight_terms.astype(F32), axis=0).astype(BF16)
    weights = exchange(spread(weight_sum, seqs), "seq").reshape(hidden_units, -1)
    values = weights[:, : 2 * channels]
    raw_query = weights[:, 2 * channels : 2 * channels + latent_width].astype(F32)
    gain_query = weights[:, 2 * channels + latent_width : 2 * channels + latent_width + 1].astype(F32)
    shift_query = weights[:, 2 * channels + latent_width + 1 : 2 * channels + latent_width + 2].astype(F32)

    part_mean = jnp.mean(hidden, axis=1)
    part_square = jnp.sum(jnp.square(hidden - part_mean[:, None]), axis=1)
    embed_f = teacher_embed.astype(F32)
    embed_mean = jnp.mean(embed_f, axis=1)
    embed_dev = embed_f - embed_mean[:, None]
    gram_part = contract(embed_dev, embed_dev, 1, 1, HIGHEST)
    cross_part = contract(sorted_proj, teacher_embed, 0, 1).reshape(2, mps, share, latent_width)
    cross_part = jnp.swapaxes(cross_part, 0, 1).reshape(mps, 2 * share, latent_width)
    head_rows = jnp.stack(
        [part_mean, part_square, jnp.pad(embed_mean, (0, tokens - latent_width))]
        + [jnp.zeros((tokens,), F32)] * 5
    )
    stats = jnp.concatenate(
        [spread(head_rows, mps), jnp.concatenate([spread(gram_part, mps), cross_part], axis=2)],
        axis=1,
    )
    stats = exchange(stats, "mp")
    means = stats[:, 0]
    token_mean = jnp.mean(means, axis=0)
    token_var = (
        jnp.sum(stats[:, 1], axis=0)
        + local_width * jnp.sum(jnp.square(means - token_mean), axis=0)
    ) / width
    embed_means = stats[:, 2, :latent_width]
    center = jnp.mean(embed_means, axis=0)
    center_dev = embed_means - center
    stats_sum = jnp.sum(stats[:, 8:], axis=0)
    gram = stats_sum[:, :latent_width] + local_width * jnp.sum(
        center_dev[:, :, None] * center_dev[:, None, :], axis=0
    )
    cross = stats_sum[:, latent_width:].astype(BF16)

    half = jnp.einsum("sk,kd->sd", student_cond, student_mod[:, 0].astype(F32), precision=HIGHEST)
    half = half.reshape(groups, 1, local_width // 128, 128)
    half = jnp.broadcast_to(half, (groups, seqs) + half.shape[2:])
    half = exchange(half.reshape((groups * seqs,) + half.shape[2:]), ("group", "seq"))
    smod = jnp.sum(half.reshape((groups, seqs, local_width // 128, 128)), axis=1)
    smod = smod.reshape(groups, local_width)

    normed = (
        (hidden - token_mean[:, None])
        * lax.rsqrt(token_var + EPSILON)[:, None]
        * (1.0 + smod[1:2])
        + smod[0:1]
    ).astype(BF16)
    latent_part = contract(student_out, normed, 0, 1).astype(BF16)
    latent_part = exchange(spread(latent_part, mps), "mp")
    latents = jnp.sum(latent_part.astype(F32), axis=0).astype(BF16)
    noised = (retain * latents.astype(F32) + level * noise[0].T.astype(F32)).astype(BF16)
    up = [(i, i + 1) for i in range(seqs - 1)]
    down = [(i + 1, i) for i in range(seqs - 1)]
    noised = jnp.concatenate(
        [lax.ppermute(noised, "seq", up), noised, lax.ppermute(noised, "seq", down)], axis=1
    )
    extent = 3 * tokens
    own = slice(tokens, 2 * tokens)

    noised_f = noised.astype(F32)
    embed_avg = jnp.sum(noised_f * center[:, None], axis=0, keepdims=True)
    gram_noised = contract(gram, noised_f, 1, 0, HIGHEST)
    embed_var = jnp.sum(noised_f * gram_noised, axis=0, keepdims=True) / width
    inv_std = lax.rsqrt(embed_var + EPSILON)
    query = (raw_query - gain_query * center[None, :]).astype(BF16)
    preact = contract(query, noised, 1, 0) * inv_std + shift_query
    activated = gelu_tanh(preact).astype(BF16)
    proj_part = contract(values, activated, 0, 0).astype(BF16).reshape(mps, share, extent)
    proj_part = exchange(proj_part, "mp")

    edges = jnp.stack(
        [
            jnp.where(seq_at == 0, tokens, 0),
            jnp.where(seq_at == seqs - 1, 2 * tokens, extent),
        ]
    ).astype(jnp.int32)
    slot = (mp_at * share) // channels
    offset = (mp_at * share) % channels
    table = jnp.concatenate([head_kernel.reshape(4, 9, channels), head_out[:, None]], axis=1)
    taps = jnp.concatenate(
        [
            lax.dynamic_slice(table, (jnp.where(slot == 0, pair[0], pair[1]), 0, offset), (1, 10, share))[0]
            for pair in (block_heads, embed_heads)
        ],
        axis=1,
    ).T
    proj_embed = contract(cross, noised, 1, 0)
    pay, field_grad = conv_stage(edges, proj_part, proj_embed, taps)
    pay = exchange(pay, "mp")
    block_grad = pay[:, :share].reshape(2 * channels, tokens)
    sums = pay[:, share : share + 4].astype(F32)
    sums = (sums[:, 0:2] + sums[:, 2:4]).reshape(2, mps // 2, 2, tokens)
    sums = jnp.sum(sums, axis=1)
    logits = jnp.stack(
        [
            jnp.where(
                picks[k] == 1,
                jnp.where(block_heads[0] == k, sums[0, 0], sums[1, 0]),
                jnp.where(embed_heads[0] == k, sums[0, 1], sums[1, 1]),
            )
            for k in range(4)
        ]
    )

    hidden_grad = contract(values, block_grad, 1, 0)
    preact_grad = (hidden_grad * gelu_slope(preact[:, own])).astype(BF16)
    query_grad = contract(query, preact_grad, 0, 0)
    own_inv = inv_std[:, own]
    along = jnp.sum(noised_f[:, own] * query_grad, axis=0, keepdims=True)
    back_part = own_inv * (
        query_grad - (own_inv * own_inv / width) * along * gram_noised[:, own]
    ) + contract(cross, field_grad, 0, 0)
    back_part = exchange(spread(back_part.astype(BF16), mps), "mp")
    latent_grad = retain * jnp.sum(back_part.astype(F32), axis=0)
    return (latents.T[None], logits[None], latent_grad.T[None])


def solution(mesh):
    return jax.shard_map(
        per_device,
        mesh=mesh,
        in_specs=(
            P("group", "seq", "mp"),
            P(None, "seq"),
            P("seq", "group", "mp"),
            P("mp", None),
            P("group"),
            P("group", "seq", None),
            P(None, "mp"),
            P(None, None, "mp"),
            P("seq", "mp"),
            P("mp", "seq"),
            P(None, "mp", None),
            P(),
            P(),
            P("group", None),
        ),
        out_specs=(P("group", "seq", None), P("group", None, "seq"), P("group", "seq", None)),
        check_vma=False,
    )
```

```python
import functools
import math

import jax
import jax.numpy as jnp
from jax import lax
from jax.experimental import pallas as pl
from jax.experimental.pallas import tpu as pltpu
from jax.sharding import PartitionSpec as P

GRID_W = 64
EPSILON = 1e-06
GELU_COEF = 0.7978845608028654
INTERPRET = False

F32 = jnp.float32
BF16 = jnp.bfloat16
HIGHEST = lax.Precision.HIGHEST


def contract(left, right, left_dim, right_dim, precision=None):
    return lax.dot_general(
        left,
        right,
        (((left_dim,), (right_dim,)), ((), ())),
        precision=precision,
        preferred_element_type=F32,
    )


def gelu_tanh(values):
    inner = GELU_COEF * (values + 0.044715 * values * values * values)
    return 0.5 * values * (1.0 + jnp.tanh(inner))


def gelu_slope(values):
    inner = GELU_COEF * (values + 0.044715 * values * values * values)
    tangent = jnp.tanh(inner)
    return 0.5 * (1.0 + tangent) + 0.5 * values * (1.0 - tangent * tangent) * GELU_COEF * (
        1.0 + 3.0 * 0.044715 * values * values
    )


def time_features(timestep, width):
    half_width = width // 2
    index = jnp.arange(half_width, dtype=F32)
    freqs = jnp.exp(-math.log(10000.0) * index / half_width)
    angles = timestep.astype(F32)[:, None] * freqs[None, :]
    return jnp.concatenate([jnp.cos(angles), jnp.sin(angles)], axis=-1)


def exchange(value, axes):
    return lax.all_to_all(value, axes, 0, 0, tiled=False)


def call(body, name, outs, scalars, arrays, scratch=(), loose=()):
    smem = pl.BlockSpec(memory_space=pltpu.SMEM)
    vmem = pl.BlockSpec(memory_space=pltpu.VMEM)
    if INTERPRET:
        shapes = [jax.ShapeDtypeStruct(shape, dtype) for shape, dtype in outs]
    else:
        shapes = [
            jax.ShapeDtypeStruct(*out) if place in loose else pltpu.VMEM(*out)
            for place, out in enumerate(outs)
        ]
        arrays = [pltpu.with_memory_space_constraint(value, pltpu.VMEM) for value in arrays]
    return pl.pallas_call(
        body,
        name=name,
        in_specs=[smem] * len(scalars) + [vmem] * len(arrays),
        out_specs=[vmem] * len(outs),
        out_shape=shapes,
        scratch_shapes=[pltpu.VMEM(shape, dtype) for shape, dtype in scratch],
        interpret=INTERPRET,
    )(*scalars, *arrays)


def pick_heads(disc_ref):
    picks = [disc_ref[0, k] for k in range(4)]
    pairs = []
    for layer in (1, 0):
        first = jnp.where(picks[0] == layer, 0, jnp.where(picks[1] == layer, 1, 2))
        last = jnp.where(picks[3] == layer, 3, jnp.where(picks[2] == layer, 2, 1))
        pairs.append((first, last))
    return pairs


def level_of(time_ref):
    return time_ref[0].astype(F32) / 1000.0


def smod_body(cond_ref, mod_ref, out_ref):
    groups = cond_ref.shape[0]
    copies, pieces, lanes = out_ref.shape
    seqs = copies // groups
    half = contract(cond_ref[...], mod_ref[...].astype(F32), 1, 0, HIGHEST)
    for group in range(groups):
        row = half[group : group + 1]
        block = jnp.concatenate(
            [row[:, lanes * p : lanes * (p + 1)] for p in range(pieces)], axis=0
        )
        out_ref[seqs * group : seqs * (group + 1)] = jnp.broadcast_to(block[None], (seqs, pieces, lanes))


def prep_body(disc_ref, tmod_ref, embed_ref, proj_ref, out_ref, turned_ref):
    rows = out_ref.shape[0]
    channels = proj_ref.shape[2]
    width = embed_ref.shape[1]
    latent = embed_ref.shape[0]
    start = (lax.axis_index("seq") % (width // rows)) * rows
    gain = 1.0 + tmod_ref[1:2]
    queries = jnp.concatenate(
        [
            embed_ref[...].astype(F32) * gain,
            gain,
            tmod_ref[0:1],
            jnp.zeros((128 - latent - 2, width), F32),
        ],
        axis=0,
    )
    turned_ref[...] = queries.T
    out_ref[:, 2 * channels :] = turned_ref[pl.ds(start, rows), :].astype(BF16)
    for place, head in enumerate(pick_heads(disc_ref)[0]):
        out_ref[:, channels * place : channels * (place + 1)] = proj_ref[head, pl.ds(start, rows), :]


def weight_body(got_ref, down_ref, up_ref, order_ref, out_ref):
    del order_ref
    copies, rows, lanes = out_ref.shape
    split = lanes - 128
    terms = jnp.concatenate(
        [
            contract(down_ref[...], got_ref[:, :split], 0, 0),
            contract(up_ref[...], got_ref[:, split:], 0, 0),
        ],
        axis=1,
    )
    out_ref[...] = terms.astype(BF16).reshape(copies, rows, lanes)


def gather_body(parts_ref, order_ref, out_ref):
    del order_ref
    total = jnp.sum(parts_ref[...].astype(F32), axis=0).astype(BF16)
    out_ref[...] = jnp.broadcast_to(total[None], out_ref.shape)


def cross_body(disc_ref, proj_ref, embed_ref, table_ref, cross_ref, taps_ref, turned_ref):
    copies, share, lanes = cross_ref.shape
    channels = proj_ref.shape[2]
    per_head = channels // share
    begin = lax.axis_index("mp") * share
    slot = begin // channels
    offset = pl.multiple_of(begin % channels, 8)
    embed = embed_ref[...]
    block, other = pick_heads(disc_ref)
    for place in range(2):
        both = jnp.concatenate(
            [contract(proj_ref[head], embed, 0, 1) for head in (block[place], other[place])], axis=1
        )
        cross_ref[per_head * place : per_head * (place + 1)] = (
            both.astype(BF16).reshape(per_head, share, lanes)
        )
    for place, pair in enumerate((block, other)):
        turned_ref[...] = table_ref[jnp.where(slot == 0, pair[0], pair[1])].T
        taps_ref[share * place : share * (place + 1)] = turned_ref[pl.ds(offset, share), :]


def sums_body(hidden_ref, out_w_ref, embed_ref, mod_ref, sums_ref):
    copies, pieces, lanes = mod_ref.shape
    latent, width = out_w_ref.shape
    tokens = hidden_ref.shape[0]
    halves = []
    for half in range(2):
        total = jnp.sum(mod_ref[copies // 2 * half : copies // 2 * (half + 1)], axis=0)
        halves.append(jnp.concatenate([total[p : p + 1] for p in range(pieces)], axis=1))
    shift, scale = halves
    hidden = hidden_ref[...]
    embed = embed_ref[...]
    out_w = out_w_ref[...].astype(F32)
    scaled = (out_w * (1.0 + scale)).astype(BF16)
    ones = jnp.ones((8, width), BF16)
    square = jnp.square(hidden.astype(F32))
    high = square.astype(BF16)
    low = (square - high.astype(F32)).astype(BF16)
    sums_ref[0:latent] = contract(scaled, hidden, 1, 1)
    columns = jnp.concatenate(
        [
            contract(embed, embed, 1, 1),
            jnp.sum(scaled.astype(F32), axis=1, keepdims=True),
            jnp.sum(out_w * shift, axis=1, keepdims=True),
            jnp.sum(embed.astype(F32), axis=1, keepdims=True),
            jnp.zeros((latent, tokens - latent - 3), F32),
        ],
        axis=1,
    )
    sums_ref[latent : 2 * latent] = columns
    row = lax.broadcasted_iota(jnp.int32, (8, tokens), 0)
    firsts = contract(ones, hidden, 1, 1)
    squares = contract(ones, high, 1, 1) + contract(ones, low, 1, 1)
    embeds = jnp.concatenate(
        [contract(ones, embed, 1, 1), jnp.zeros((8, tokens - latent), F32)], axis=1
    )
    sums_ref[2 * latent :] = jnp.where(row == 0, firsts, jnp.where(row == 1, squares, embeds))


def noise_body(time_ref, sums_ref, noise_ref, latents_ref, noised_ref, *, width):
    latent = noise_ref.shape[0]
    mean = sums_ref[2 * latent : 2 * latent + 1] / width
    var = sums_ref[2 * latent + 1 : 2 * latent + 2] / width - mean * mean
    scaled_sum = sums_ref[latent : 2 * latent, latent : latent + 1]
    shifted_sum = sums_ref[latent : 2 * latent, latent + 1 : latent + 2]
    latents = lax.rsqrt(var + EPSILON) * (sums_ref[0:latent] - mean * scaled_sum) + shifted_sum
    latents = latents.astype(BF16)
    latents_ref[...] = latents
    level = level_of(time_ref)
    noised_ref[...] = (
        (1.0 - level) * latents.astype(F32) + level * noise_ref[...].astype(F32)
    ).astype(BF16)


def act_body(
    sums_ref,
    before_ref,
    noised_ref,
    after_ref,
    weights_ref,
    cross_ref,
    out_ref,
    pre_ref,
    query_ref,
    side_ref,
    act_ref,
    *,
    width,
):
    latent, tokens = noised_ref.shape
    units = weights_ref.shape[0]
    copies, share, lanes = out_ref.shape
    extent = 3 * tokens
    split = weights_ref.shape[1] - 128
    noised = jnp.concatenate([before_ref[...], noised_ref[...], after_ref[...]], axis=1)
    noised_f = noised.astype(F32)
    center_col = sums_ref[latent : 2 * latent, latent + 2 : latent + 3] / width
    center_row = sums_ref[2 * latent + 2 : 2 * latent + 3, :latent] / width
    gram = sums_ref[latent : 2 * latent, :latent] - width * (center_col * center_row)
    gram_noised = contract(gram, noised_f, 1, 0, HIGHEST)
    var = jnp.sum(noised_f * gram_noised, axis=0, keepdims=True) / width
    inv_std = lax.rsqrt(var + EPSILON)
    side_ref[0:latent] = gram_noised[:, tokens : 2 * tokens]
    side_ref[latent:] = jnp.broadcast_to(inv_std[:, tokens : 2 * tokens], (8, tokens))
    step = 128
    for begin in range(0, units, step):
        rows = slice(begin, begin + step)
        raw = weights_ref[rows, split : split + latent].astype(F32)
        gain = weights_ref[rows, split + latent : split + latent + 1].astype(F32)
        shift = weights_ref[rows, split + latent + 1 : split + latent + 2].astype(F32)
        query = (raw - gain * center_row).astype(BF16)
        query_ref[rows] = query
        pre = contract(query, noised, 1, 0) * inv_std + shift
        pre_ref[rows] = pre[:, tokens : 2 * tokens]
        act_ref[rows] = gelu_tanh(pre).astype(BF16)
    part = contract(weights_ref[:, :split], act_ref[...], 0, 0).astype(BF16)
    out_ref[:, :, :extent] = part.reshape(copies, share, extent)
    out_ref[:, :, extent:] = cross_ref[...]


def conv_body(
    parts_ref, before_ref, noised_ref, after_ref, taps_ref, pay_ref, back_ref, *, count
):
    copies, share, _ = parts_ref.shape
    latent, own = noised_ref.shape
    extent = 3 * own
    channels = 2 * share
    noised = jnp.concatenate([before_ref[...], noised_ref[...], after_ref[...]], axis=1)
    total = jnp.sum(parts_ref[...].astype(F32), axis=0)
    cross = jnp.concatenate(
        [total[:, extent : extent + latent], total[:, extent + latent :]], axis=0
    ).astype(BF16)
    embed = contract(cross, noised, 1, 0)
    field_in = jnp.concatenate([embed[:share] + total[:, :extent], embed[share:]], axis=0)
    lane = lax.broadcasted_iota(jnp.int32, (channels, extent), 1)
    at = lax.axis_index("seq")
    first = jnp.where(at == 0, own, 0)
    last = jnp.where(at == count - 1, 2 * own, extent)
    inside = (lane >= first) & (lane < last)
    column = lane % GRID_W
    left_ok = column > 0
    right_ok = column < GRID_W - 1

    def tap(row, col):
        place = 3 * row + col
        return taps_ref[:, place : place + 1]

    def convolve(grid, flip):
        before = jnp.where(left_ok, pltpu.roll(grid, 1, 1), 0.0)
        after = jnp.where(right_ok, pltpu.roll(grid, extent - 1, 1), 0.0)
        rows = []
        for row in range(3):
            if flip:
                rows.append(tap(row, 2) * before + tap(row, 1) * grid + tap(row, 0) * after)
            else:
                rows.append(tap(row, 0) * before + tap(row, 1) * grid + tap(row, 2) * after)
        if flip:
            rows = rows[::-1]
        return pltpu.roll(rows[0], GRID_W, 1) + rows[1] + pltpu.roll(rows[2], extent - GRID_W, 1)

    field = convolve(jnp.where(inside, field_in, 0.0), False)
    gating = jax.nn.sigmoid(field)
    scale = taps_ref[:, 9:10]
    terms = field * gating * scale
    slope = -scale * gating * (1.0 + field * (1.0 - gating))
    grad = convolve(jnp.where(inside, slope, 0.0), True)[:, own : 2 * own]
    block_sum = jnp.sum(terms[:share, own : 2 * own], axis=0, keepdims=True)
    embed_sum = jnp.sum(terms[share:, own : 2 * own], axis=0, keepdims=True)
    sums = jnp.concatenate([block_sum, embed_sum], axis=0)
    high = sums.astype(BF16).astype(F32)
    low = sums - high
    tail = jnp.concatenate([high, low, jnp.zeros((12, own), F32)], axis=0)
    pay = jnp.concatenate([grad[:share], tail], axis=0).astype(BF16)
    pay_ref[...] = jnp.broadcast_to(pay[None], pay_ref.shape)
    back_ref[...] = contract(cross, grad.astype(BF16), 0, 0)


def back_body(
    disc_ref,
    pay_ref,
    weights_ref,
    query_ref,
    slope_ref,
    side_ref,
    noised_ref,
    back_ref,
    out_ref,
    logits_ref,
    *,
    width,
):
    copies, rows, tokens = pay_ref.shape
    share = rows - 16
    latent = noised_ref.shape[0]
    split = copies * share
    grads = jnp.concatenate([pay_ref[copy, :share] for copy in range(copies)], axis=0)
    hidden_grad = contract(weights_ref[:, :split], grads, 1, 0)
    preact_grad = (hidden_grad * slope_ref[...]).astype(BF16)
    query_grad = contract(query_ref[...], preact_grad, 0, 0)
    inv_std = side_ref[latent : latent + 1]
    along = jnp.sum(noised_ref[...].astype(F32) * query_grad, axis=0, keepdims=True)
    result = (
        inv_std * (query_grad - (inv_std * inv_std / width) * along * side_ref[0:latent])
        + back_ref[...]
    )
    out_ref[...] = jnp.broadcast_to(result.astype(BF16)[None], out_ref.shape)
    sums = []
    for place in range(2):
        total = jnp.zeros((16, tokens), F32)
        for copy in range(copies // 2 * place, copies // 2 * (place + 1)):
            total = total + pay_ref[copy, share:].astype(F32)
        sums.append(total[0:2] + total[2:4])
    block, other = pick_heads(disc_ref)
    for k in range(4):
        chosen = jnp.where(block[0] == k, 0, jnp.where(block[1] == k, 1, jnp.where(other[0] == k, 2, 3)))
        options = [sums[0][0:1], sums[1][0:1], sums[0][1:2], sums[1][1:2]]
        value = options[3]
        for place in range(3):
            value = jnp.where(chosen == place, options[place], value)
        logits_ref[k : k + 1] = value


def final_body(time_ref, parts_ref, out_ref):
    retain = 1.0 - level_of(time_ref)
    out_ref[...] = retain * jnp.sum(parts_ref[...].astype(F32), axis=0)


def per_device(
    student_hidden,
    student_cond,
    student_mod,
    student_out,
    timestep,
    noise,
    teacher_embed,
    teacher_mod,
    up_weight,
    down_weight,
    head_proj,
    head_kernel,
    head_out,
    disc_layer,
):
    groups = lax.axis_size("group")
    seqs = lax.axis_size("seq")
    mps = lax.axis_size("mp")
    _, tokens, local_width = student_hidden.shape
    width = local_width * mps
    latent = teacher_embed.shape[0]
    units = down_weight.shape[0]
    channels = head_proj.shape[2]
    share = 2 * channels // mps
    lanes = 2 * channels + 128
    extent = 3 * tokens

    pieces = local_width // 128
    (mods,) = call(
        smod_body,
        "smod",
        [((groups * seqs, pieces, 128), F32)],
        [],
        [student_cond, student_mod[:, 0]],
    )
    with jax.named_scope("mod_exchange"):
        mods = exchange(mods, ("group", "seq"))

    tmod = jnp.einsum(
        "sf,fjd->sjd",
        time_features(timestep, teacher_mod.shape[0]),
        teacher_mod.astype(F32),
        precision=HIGHEST,
    )[0]
    ratio = seqs // mps
    rows = local_width // ratio
    (sent,) = call(
        prep_body,
        "prep",
        [((rows, lanes), BF16)],
        [disc_layer],
        [tmod, teacher_embed, head_proj],
        [((local_width, 128), F32)],
    )
    swap = [
        (at * mps + m, (ratio * m + at % ratio) * mps + at // ratio)
        for at in range(seqs)
        for m in range(mps)
    ]
    with jax.named_scope("row_swap"):
        got = lax.ppermute(sent, ("seq", "mp"), swap)
    (terms,) = call(
        weight_body,
        "weight",
        [((seqs, units // seqs, lanes), BF16)],
        [],
        [got, down_weight.T, up_weight, mods],
    )
    with jax.named_scope("weight_scatter"):
        terms = exchange(terms, "seq")
    table = jnp.concatenate(
        [head_kernel.reshape(4, 9, channels), head_out[:, None], jnp.zeros((4, 6, channels), F32)],
        axis=1,
    )
    cross, taps = call(
        cross_body,
        "cross",
        [((mps, share, 2 * latent), BF16), ((2 * share, 16), F32)],
        [disc_layer],
        [head_proj, teacher_embed, table],
        [((channels, 16), F32)],
    )

    (sums,) = call(
        sums_body,
        "sums",
        [((2 * latent + 8, tokens), F32)],
        [],
        [student_hidden[0], student_out.T, teacher_embed, mods],
    )
    stages = [sums]
    step = 1
    while step < mps:
        with jax.named_scope(f"pair_{step}"):
            sums = sums + lax.ppermute(sums, "mp", [(i, i ^ step) for i in range(mps)])
        step *= 2
        stages.append(sums)
    halfway = stages[-2]
    (terms,) = call(gather_body, "gather", [((seqs, units // seqs, lanes), BF16)], [], [terms, halfway])
    with jax.named_scope("weight_gather"):
        weights = exchange(terms, "seq").reshape(units, lanes)

    latents, noised = call(
        functools.partial(noise_body, width=float(width)),
        "noise",
        [((latent, tokens), BF16), ((latent, tokens), BF16)],
        [timestep],
        [sums, noise[0].T],
        loose=(0,),
    )
    with jax.named_scope("halo"):
        before = lax.ppermute(noised, "seq", [(i, i + 1) for i in range(seqs - 1)])
        after = lax.ppermute(noised, "seq", [(i + 1, i) for i in range(seqs - 1)])

    parts, preact, query, side = call(
        functools.partial(act_body, width=float(width)),
        "act",
        [
            ((mps, share, extent + 2 * latent), BF16),
            ((units, tokens), F32),
            ((units, latent), BF16),
            ((latent + 8, tokens), F32),
        ],
        [],
        [sums, before, noised, after, weights, cross],
        [((units, extent), BF16)],
    )
    with jax.named_scope("parts_exchange"):
        parts = exchange(parts, "mp")
    slope = gelu_slope(preact)
    pay, back = call(
        functools.partial(conv_body, count=seqs),
        "conv",
        [((mps, share + 16, tokens), BF16), ((latent, tokens), F32)],
        [],
        [parts, before, noised, after, taps],
    )
    with jax.named_scope("pay_exchange"):
        pay = exchange(pay, "mp")
    back, logits = call(
        functools.partial(back_body, width=float(width)),
        "back",
        [((mps, latent, tokens), BF16), ((4, tokens), F32)],
        [disc_layer],
        [pay, weights, query, slope, side, noised, back],
        loose=(1,),
    )
    with jax.named_scope("back_exchange"):
        back = exchange(back, "mp")
    (latent_grad,) = call(final_body, "final", [((latent, tokens), F32)], [timestep], [back], loose=(0,))
    return (latents.T[None], logits[None], latent_grad.T[None])


def solution(mesh):
    return jax.shard_map(
        per_device,
        mesh=mesh,
        in_specs=(
            P("group", "seq", "mp"),
            P(None, "seq"),
            P("seq", "group", "mp"),
            P("mp", None),
            P("group"),
            P("group", "seq", None),
            P(None, "mp"),
            P(None, None, "mp"),
            P("seq", "mp"),
            P("mp", "seq"),
            P(None, "mp", None),
            P(),
            P(),
            P("group", None),
        ),
        out_specs=(P("group", "seq", None), P("group", None, "seq"), P("group", "seq", None)),
        check_vma=False,
    )
```

```python
import functools
import math

import jax
import jax.numpy as jnp
from jax import lax
from jax.experimental import pallas as pl
from jax.experimental.pallas import tpu as pltpu
from jax.sharding import PartitionSpec as P


GRID_W = 64
EPSILON = 1e-06
GELU_COEF = 0.7978845608028654
INTERPRET = False

F32 = jnp.float32
BF16 = jnp.bfloat16
HIGHEST = lax.Precision.HIGHEST


def contract(left, right, left_dim, right_dim, precision=None):
    return lax.dot_general(
        left,
        right,
        (((left_dim,), (right_dim,)), ((), ())),
        precision=precision,
        preferred_element_type=F32,
    )


def gelu_tanh(values):
    inner = GELU_COEF * (values + 0.044715 * values * values * values)
    return 0.5 * values * (1.0 + jnp.tanh(inner))


def gelu_slope(values):
    inner = GELU_COEF * (values + 0.044715 * values * values * values)
    tangent = jnp.tanh(inner)
    return 0.5 * (1.0 + tangent) + 0.5 * values * (1.0 - tangent * tangent) * GELU_COEF * (
        1.0 + 3.0 * 0.044715 * values * values
    )


def time_features(timestep, width):
    half_width = width // 2
    index = jnp.arange(half_width, dtype=F32)
    freqs = jnp.exp(-math.log(10000.0) * index / half_width)
    angles = timestep.astype(F32)[:, None] * freqs[None, :]
    return jnp.concatenate([jnp.cos(angles), jnp.sin(angles)], axis=-1)


def exchange(value, axes):
    return lax.all_to_all(value, axes, 0, 0, tiled=False)


def call(body, outs, scalars, arrays, scratch=(), loose=()):
    smem = pl.BlockSpec(memory_space=pltpu.SMEM)
    vmem = pl.BlockSpec(memory_space=pltpu.VMEM)
    if INTERPRET:
        shapes = [jax.ShapeDtypeStruct(shape, dtype) for shape, dtype in outs]
    else:
        shapes = [
            jax.ShapeDtypeStruct(*out) if place in loose else pltpu.VMEM(*out)
            for place, out in enumerate(outs)
        ]
        arrays = [pltpu.with_memory_space_constraint(value, pltpu.VMEM) for value in arrays]
    return pl.pallas_call(
        body,
        in_specs=[smem] * len(scalars) + [vmem] * len(arrays),
        out_specs=[vmem] * len(outs),
        out_shape=shapes,
        scratch_shapes=[pltpu.VMEM(shape, dtype) for shape, dtype in scratch],
        interpret=INTERPRET,
    )(*scalars, *arrays)


def pick_heads(disc_ref):
    picks = [disc_ref[0, k] for k in range(4)]
    pairs = []
    for layer in (1, 0):
        first = jnp.where(picks[0] == layer, 0, jnp.where(picks[1] == layer, 1, 2))
        last = jnp.where(picks[3] == layer, 3, jnp.where(picks[2] == layer, 2, 1))
        pairs.append((first, last))
    return pairs


def level_of(time_ref):
    return time_ref[0].astype(F32) / 1000.0


def smod_body(cond_ref, mod_ref, out_ref):
    groups = cond_ref.shape[0]
    copies, pieces, lanes = out_ref.shape
    seqs = copies // groups
    half = contract(cond_ref[...], mod_ref[...].astype(F32), 1, 0, HIGHEST)
    for group in range(groups):
        row = half[group : group + 1]
        block = jnp.concatenate(
            [row[:, lanes * p : lanes * (p + 1)] for p in range(pieces)], axis=0
        )
        out_ref[seqs * group : seqs * (group + 1)] = jnp.broadcast_to(block[None], (seqs, pieces, lanes))


def prep_body(disc_ref, tmod_ref, embed_ref, proj_ref, out_ref, turned_ref):
    rows = out_ref.shape[0]
    channels = proj_ref.shape[2]
    width = embed_ref.shape[1]
    latent = embed_ref.shape[0]
    start = (lax.axis_index("seq") % (width // rows)) * rows
    gain = 1.0 + tmod_ref[1:2]
    queries = jnp.concatenate(
        [
            embed_ref[...].astype(F32) * gain,
            gain,
            tmod_ref[0:1],
            jnp.zeros((128 - latent - 2, width), F32),
        ],
        axis=0,
    )
    turned_ref[...] = queries.T
    out_ref[:, 2 * channels :] = turned_ref[pl.ds(start, rows), :].astype(BF16)
    for place, head in enumerate(pick_heads(disc_ref)[0]):
        out_ref[:, channels * place : channels * (place + 1)] = proj_ref[head, pl.ds(start, rows), :]


def weight_body(got_ref, down_ref, up_ref, order_ref, out_ref):
    del order_ref
    copies, rows, lanes = out_ref.shape
    split = lanes - 128
    terms = jnp.concatenate(
        [
            contract(down_ref[...], got_ref[:, :split], 0, 0),
            contract(up_ref[...], got_ref[:, split:], 0, 0),
        ],
        axis=1,
    )
    out_ref[...] = terms.astype(BF16).reshape(copies, rows, lanes)


def gather_body(parts_ref, order_ref, out_ref):
    del order_ref
    total = jnp.sum(parts_ref[...].astype(F32), axis=0).astype(BF16)
    out_ref[...] = jnp.broadcast_to(total[None], out_ref.shape)


def cross_body(disc_ref, proj_ref, embed_ref, table_ref, cross_ref, taps_ref, turned_ref):
    _, share, lanes = cross_ref.shape
    channels = proj_ref.shape[2]
    per_head = channels // share
    begin = lax.axis_index("mp") * share
    slot = begin // channels
    offset = pl.multiple_of(begin % channels, 8)
    embed = embed_ref[...]
    block, other = pick_heads(disc_ref)
    for place in range(2):
        both = jnp.concatenate(
            [contract(proj_ref[head], embed, 0, 1) for head in (block[place], other[place])], axis=1
        )
        cross_ref[per_head * place : per_head * (place + 1)] = (
            both.astype(BF16).reshape(per_head, share, lanes)
        )
    for place, pair in enumerate((block, other)):
        turned_ref[...] = table_ref[jnp.where(slot == 0, pair[0], pair[1])].T
        taps_ref[share * place : share * (place + 1)] = turned_ref[pl.ds(offset, share), :]


def sums_body(hidden_ref, out_w_ref, embed_ref, mod_ref, sums_ref):
    copies, pieces, _ = mod_ref.shape
    latent, width = out_w_ref.shape
    tokens = hidden_ref.shape[0]
    halves = []
    for half in range(2):
        total = jnp.sum(mod_ref[copies // 2 * half : copies // 2 * (half + 1)], axis=0)
        halves.append(jnp.concatenate([total[p : p + 1] for p in range(pieces)], axis=1))
    shift, scale = halves
    hidden = hidden_ref[...]
    embed = embed_ref[...]
    out_w = out_w_ref[...].astype(F32)
    scaled = (out_w * (1.0 + scale)).astype(BF16)
    ones = jnp.ones((8, width), BF16)
    square = jnp.square(hidden.astype(F32))
    high = square.astype(BF16)
    low = (square - high.astype(F32)).astype(BF16)
    sums_ref[0:latent] = contract(scaled, hidden, 1, 1)
    columns = jnp.concatenate(
        [
            contract(embed, embed, 1, 1),
            jnp.sum(scaled.astype(F32), axis=1, keepdims=True),
            jnp.sum(out_w * shift, axis=1, keepdims=True),
            jnp.sum(embed.astype(F32), axis=1, keepdims=True),
            jnp.zeros((latent, tokens - latent - 3), F32),
        ],
        axis=1,
    )
    sums_ref[latent : 2 * latent] = columns
    row = lax.broadcasted_iota(jnp.int32, (8, tokens), 0)
    firsts = contract(ones, hidden, 1, 1)
    squares = contract(ones, high, 1, 1) + contract(ones, low, 1, 1)
    embeds = jnp.concatenate(
        [contract(ones, embed, 1, 1), jnp.zeros((8, tokens - latent), F32)], axis=1
    )
    sums_ref[2 * latent :] = jnp.where(row == 0, firsts, jnp.where(row == 1, squares, embeds))


def noise_body(time_ref, sums_ref, noise_ref, latents_ref, noised_ref, *, width):
    latent = noise_ref.shape[0]
    mean = sums_ref[2 * latent : 2 * latent + 1] / width
    var = sums_ref[2 * latent + 1 : 2 * latent + 2] / width - mean * mean
    scaled_sum = sums_ref[latent : 2 * latent, latent : latent + 1]
    shifted_sum = sums_ref[latent : 2 * latent, latent + 1 : latent + 2]
    latents = lax.rsqrt(var + EPSILON) * (sums_ref[0:latent] - mean * scaled_sum) + shifted_sum
    latents = latents.astype(BF16)
    latents_ref[...] = latents
    level = level_of(time_ref)
    noised_ref[...] = (
        (1.0 - level) * latents.astype(F32) + level * noise_ref[...].astype(F32)
    ).astype(BF16)


def act_body(
    sums_ref,
    before_ref,
    noised_ref,
    after_ref,
    weights_ref,
    cross_ref,
    out_ref,
    pre_ref,
    query_ref,
    side_ref,
    act_ref,
    *,
    width,
):
    latent, tokens = noised_ref.shape
    units = weights_ref.shape[0]
    copies, share, _ = out_ref.shape
    extent = 3 * tokens
    split = weights_ref.shape[1] - 128
    noised = jnp.concatenate([before_ref[...], noised_ref[...], after_ref[...]], axis=1)
    noised_f = noised.astype(F32)
    center_col = sums_ref[latent : 2 * latent, latent + 2 : latent + 3] / width
    center_row = sums_ref[2 * latent + 2 : 2 * latent + 3, :latent] / width
    gram = sums_ref[latent : 2 * latent, :latent] - width * (center_col * center_row)
    gram_noised = contract(gram, noised_f, 1, 0, HIGHEST)
    var = jnp.sum(noised_f * gram_noised, axis=0, keepdims=True) / width
    inv_std = lax.rsqrt(var + EPSILON)
    side_ref[0:latent] = gram_noised[:, tokens : 2 * tokens]
    side_ref[latent:] = jnp.broadcast_to(inv_std[:, tokens : 2 * tokens], (8, tokens))
    step = 128
    for begin in range(0, units, step):
        rows = slice(begin, begin + step)
        raw = weights_ref[rows, split : split + latent].astype(F32)
        gain = weights_ref[rows, split + latent : split + latent + 1].astype(F32)
        shift = weights_ref[rows, split + latent + 1 : split + latent + 2].astype(F32)
        query = (raw - gain * center_row).astype(BF16)
        query_ref[rows] = query
        pre = contract(query, noised, 1, 0) * inv_std + shift
        pre_ref[rows] = pre[:, tokens : 2 * tokens]
        act_ref[rows] = gelu_tanh(pre).astype(BF16)
    part = contract(weights_ref[:, :split], act_ref[...], 0, 0).astype(BF16)
    out_ref[:, :, :extent] = part.reshape(copies, share, extent)
    out_ref[:, :, extent:] = cross_ref[...]


def conv_body(
    parts_ref, before_ref, noised_ref, after_ref, taps_ref, pay_ref, back_ref, *, count
):
    _, share, _ = parts_ref.shape
    latent, own = noised_ref.shape
    extent = 3 * own
    channels = 2 * share
    noised = jnp.concatenate([before_ref[...], noised_ref[...], after_ref[...]], axis=1)
    total = jnp.sum(parts_ref[...].astype(F32), axis=0)
    cross = jnp.concatenate(
        [total[:, extent : extent + latent], total[:, extent + latent :]], axis=0
    ).astype(BF16)
    embed = contract(cross, noised, 1, 0)
    field_in = jnp.concatenate([embed[:share] + total[:, :extent], embed[share:]], axis=0)
    lane = lax.broadcasted_iota(jnp.int32, (channels, extent), 1)
    at = lax.axis_index("seq")
    first = jnp.where(at == 0, own, 0)
    last = jnp.where(at == count - 1, 2 * own, extent)
    inside = (lane >= first) & (lane < last)
    column = lane % GRID_W
    left_ok = column > 0
    right_ok = column < GRID_W - 1

    def tap(row, col):
        place = 3 * row + col
        return taps_ref[:, place : place + 1]

    def convolve(grid, flip):
        before = jnp.where(left_ok, pltpu.roll(grid, 1, 1), 0.0)
        after = jnp.where(right_ok, pltpu.roll(grid, extent - 1, 1), 0.0)
        rows = []
        for row in range(3):
            if flip:
                rows.append(tap(row, 2) * before + tap(row, 1) * grid + tap(row, 0) * after)
            else:
                rows.append(tap(row, 0) * before + tap(row, 1) * grid + tap(row, 2) * after)
        if flip:
            rows = rows[::-1]
        return pltpu.roll(rows[0], GRID_W, 1) + rows[1] + pltpu.roll(rows[2], extent - GRID_W, 1)

    field = convolve(jnp.where(inside, field_in, 0.0), False)
    gating = jax.nn.sigmoid(field)
    scale = taps_ref[:, 9:10]
    terms = field * gating * scale
    slope = -scale * gating * (1.0 + field * (1.0 - gating))
    grad = convolve(jnp.where(inside, slope, 0.0), True)[:, own : 2 * own]
    block_sum = jnp.sum(terms[:share, own : 2 * own], axis=0, keepdims=True)
    embed_sum = jnp.sum(terms[share:, own : 2 * own], axis=0, keepdims=True)
    sums = jnp.concatenate([block_sum, embed_sum], axis=0)
    high = sums.astype(BF16).astype(F32)
    low = sums - high
    tail = jnp.concatenate([high, low, jnp.zeros((12, own), F32)], axis=0)
    pay = jnp.concatenate([grad[:share], tail], axis=0).astype(BF16)
    pay_ref[...] = jnp.broadcast_to(pay[None], pay_ref.shape)
    back_ref[...] = contract(cross, grad.astype(BF16), 0, 0)


def back_body(
    disc_ref,
    pay_ref,
    weights_ref,
    query_ref,
    slope_ref,
    side_ref,
    noised_ref,
    back_ref,
    out_ref,
    logits_ref,
    *,
    width,
):
    copies, rows, tokens = pay_ref.shape
    share = rows - 16
    latent = noised_ref.shape[0]
    split = copies * share
    grads = jnp.concatenate([pay_ref[copy, :share] for copy in range(copies)], axis=0)
    hidden_grad = contract(weights_ref[:, :split], grads, 1, 0)
    preact_grad = (hidden_grad * slope_ref[...]).astype(BF16)
    query_grad = contract(query_ref[...], preact_grad, 0, 0)
    inv_std = side_ref[latent : latent + 1]
    along = jnp.sum(noised_ref[...].astype(F32) * query_grad, axis=0, keepdims=True)
    result = (
        inv_std * (query_grad - (inv_std * inv_std / width) * along * side_ref[0:latent])
        + back_ref[...]
    )
    out_ref[...] = jnp.broadcast_to(result.astype(BF16)[None], out_ref.shape)
    sums = []
    for place in range(2):
        total = jnp.zeros((16, tokens), F32)
        for copy in range(copies // 2 * place, copies // 2 * (place + 1)):
            total = total + pay_ref[copy, share:].astype(F32)
        sums.append(total[0:2] + total[2:4])
    block, other = pick_heads(disc_ref)
    for k in range(4):
        chosen = jnp.where(block[0] == k, 0, jnp.where(block[1] == k, 1, jnp.where(other[0] == k, 2, 3)))
        options = [sums[0][0:1], sums[1][0:1], sums[0][1:2], sums[1][1:2]]
        value = options[3]
        for place in range(3):
            value = jnp.where(chosen == place, options[place], value)
        logits_ref[k : k + 1] = value


def final_body(time_ref, parts_ref, out_ref):
    retain = 1.0 - level_of(time_ref)
    out_ref[...] = retain * jnp.sum(parts_ref[...].astype(F32), axis=0)


def per_device(
    student_hidden,
    student_cond,
    student_mod,
    student_out,
    timestep,
    noise,
    teacher_embed,
    teacher_mod,
    up_weight,
    down_weight,
    head_proj,
    head_kernel,
    head_out,
    disc_layer,
):
    groups = lax.axis_size("group")
    seqs = lax.axis_size("seq")
    mps = lax.axis_size("mp")
    _, tokens, local_width = student_hidden.shape
    width = local_width * mps
    latent = teacher_embed.shape[0]
    units = down_weight.shape[0]
    channels = head_proj.shape[2]
    share = 2 * channels // mps
    lanes = 2 * channels + 128
    extent = 3 * tokens

    pieces = local_width // 128
    (mods,) = call(
        smod_body, [((groups * seqs, pieces, 128), F32)], [], [student_cond, student_mod[:, 0]]
    )
    mods = exchange(mods, ("group", "seq"))

    tmod = jnp.einsum(
        "sf,fjd->sjd",
        time_features(timestep, teacher_mod.shape[0]),
        teacher_mod.astype(F32),
        precision=HIGHEST,
    )[0]
    ratio = seqs // mps
    rows = local_width // ratio
    (sent,) = call(
        prep_body,
        [((rows, lanes), BF16)],
        [disc_layer],
        [tmod, teacher_embed, head_proj],
        [((local_width, 128), F32)],
    )
    swap = [
        (at * mps + m, (ratio * m + at % ratio) * mps + at // ratio)
        for at in range(seqs)
        for m in range(mps)
    ]
    got = lax.ppermute(sent, ("seq", "mp"), swap)
    (terms,) = call(
        weight_body,
        [((seqs, units // seqs, lanes), BF16)],
        [],
        [got, down_weight.T, up_weight, mods],
    )
    terms = exchange(terms, "seq")
    table = jnp.concatenate(
        [head_kernel.reshape(4, 9, channels), head_out[:, None], jnp.zeros((4, 6, channels), F32)],
        axis=1,
    )
    cross, taps = call(
        cross_body,
        [((mps, share, 2 * latent), BF16), ((2 * share, 16), F32)],
        [disc_layer],
        [head_proj, teacher_embed, table],
        [((channels, 16), F32)],
    )

    (sums,) = call(
        sums_body,
        [((2 * latent + 8, tokens), F32)],
        [],
        [student_hidden[0], student_out.T, teacher_embed, mods],
    )
    stages = [sums]
    step = 1
    while step < mps:
        sums = sums + lax.ppermute(sums, "mp", [(i, i ^ step) for i in range(mps)])
        step *= 2
        stages.append(sums)
    halfway = stages[-2]
    (terms,) = call(gather_body, [((seqs, units // seqs, lanes), BF16)], [], [terms, halfway])
    weights = exchange(terms, "seq").reshape(units, lanes)

    latents, noised = call(
        functools.partial(noise_body, width=float(width)),
        [((latent, tokens), BF16), ((latent, tokens), BF16)],
        [timestep],
        [sums, noise[0].T],
        loose=(0,),
    )
    before = lax.ppermute(noised, "seq", [(i, i + 1) for i in range(seqs - 1)])
    after = lax.ppermute(noised, "seq", [(i + 1, i) for i in range(seqs - 1)])

    parts, preact, query, side = call(
        functools.partial(act_body, width=float(width)),
        [
            ((mps, share, extent + 2 * latent), BF16),
            ((units, tokens), F32),
            ((units, latent), BF16),
            ((latent + 8, tokens), F32),
        ],
        [],
        [sums, before, noised, after, weights, cross],
        [((units, extent), BF16)],
    )
    parts = exchange(parts, "mp")
    slope = gelu_slope(preact)
    pay, back = call(
        functools.partial(conv_body, count=seqs),
        [((mps, share + 16, tokens), BF16), ((latent, tokens), F32)],
        [],
        [parts, before, noised, after, taps],
    )
    pay = exchange(pay, "mp")
    back, logits = call(
        functools.partial(back_body, width=float(width)),
        [((mps, latent, tokens), BF16), ((4, tokens), F32)],
        [disc_layer],
        [pay, weights, query, slope, side, noised, back],
        loose=(1,),
    )
    back = exchange(back, "mp")
    (latent_grad,) = call(final_body, [((latent, tokens), F32)], [timestep], [back], loose=(0,))
    return (latents.T[None], logits[None], latent_grad.T[None])


def solution(mesh):
    return jax.shard_map(
        per_device,
        mesh=mesh,
        in_specs=(
            P("group", "seq", "mp"),
            P(None, "seq"),
            P("seq", "group", "mp"),
            P("mp", None),
            P("group"),
            P("group", "seq", None),
            P(None, "mp"),
            P(None, None, "mp"),
            P("seq", "mp"),
            P("mp", "seq"),
            P(None, "mp", None),
            P(),
            P(),
            P("group", None),
        ),
        out_specs=(P("group", "seq", None), P("group", None, "seq"), P("group", "seq", None)),
        check_vma=False,
    )
```

```python
import functools
import math

import jax
import jax.numpy as jnp
from jax import lax
from jax.experimental import pallas as pl
from jax.experimental.pallas import tpu as pltpu
from jax.sharding import Mesh
from jax.sharding import PartitionSpec as P


GRID_W = 64
EPSILON = 1e-06
GELU_COEF = 0.7978845608028654
INTERPRET = False

F32 = jnp.float32
BF16 = jnp.bfloat16
HIGHEST = lax.Precision.HIGHEST


def contract(left, right, left_dim, right_dim, precision=None):
    return lax.dot_general(
        left,
        right,
        (((left_dim,), (right_dim,)), ((), ())),
        precision=precision,
        preferred_element_type=F32,
    )


def gelu_tanh(values):
    inner = GELU_COEF * (values + 0.044715 * values * values * values)
    return 0.5 * values * (1.0 + jnp.tanh(inner))


def gelu_slope(values):
    inner = GELU_COEF * (values + 0.044715 * values * values * values)
    tangent = jnp.tanh(inner)
    return 0.5 * (1.0 + tangent) + 0.5 * values * (1.0 - tangent * tangent) * GELU_COEF * (
        1.0 + 3.0 * 0.044715 * values * values
    )


def time_features(timestep, width):
    half_width = width // 2
    index = jnp.arange(half_width, dtype=F32)
    freqs = jnp.exp(-math.log(10000.0) * index / half_width)
    angles = timestep.astype(F32)[:, None] * freqs[None, :]
    return jnp.concatenate([jnp.cos(angles), jnp.sin(angles)], axis=-1)


SEQ = ("plane", "core")


def seq_index():
    return lax.axis_index("plane") * 2 + lax.axis_index("core")


def exchange(value, axes):
    return lax.all_to_all(value, axes, 0, 0, tiled=False)


def call(body, outs, scalars, arrays, scratch=(), loose=()):
    smem = pl.BlockSpec(memory_space=pltpu.SMEM)
    vmem = pl.BlockSpec(memory_space=pltpu.VMEM)
    if INTERPRET:
        shapes = [jax.ShapeDtypeStruct(shape, dtype) for shape, dtype in outs]
    else:
        shapes = [
            jax.ShapeDtypeStruct(*out) if place in loose else pltpu.VMEM(*out)
            for place, out in enumerate(outs)
        ]
        arrays = [pltpu.with_memory_space_constraint(value, pltpu.VMEM) for value in arrays]
    return pl.pallas_call(
        body,
        in_specs=[smem] * len(scalars) + [vmem] * len(arrays),
        out_specs=[vmem] * len(outs),
        out_shape=shapes,
        scratch_shapes=[pltpu.VMEM(shape, dtype) for shape, dtype in scratch],
        interpret=INTERPRET,
    )(*scalars, *arrays)


def pick_heads(disc_ref):
    picks = [disc_ref[0, k] for k in range(4)]
    pairs = []
    for layer in (1, 0):
        first = jnp.where(picks[0] == layer, 0, jnp.where(picks[1] == layer, 1, 2))
        last = jnp.where(picks[3] == layer, 3, jnp.where(picks[2] == layer, 2, 1))
        pairs.append((first, last))
    return pairs


def level_of(time_ref):
    return time_ref[0].astype(F32) / 1000.0


def smod_body(cond_ref, mod_ref, out_ref):
    groups = cond_ref.shape[0]
    copies, pieces, lanes = out_ref.shape
    seqs = copies // groups
    half = contract(cond_ref[...], mod_ref[...].astype(F32), 1, 0, HIGHEST)
    for group in range(groups):
        row = half[group : group + 1]
        block = jnp.concatenate(
            [row[:, lanes * p : lanes * (p + 1)] for p in range(pieces)], axis=0
        )
        out_ref[seqs * group : seqs * (group + 1)] = jnp.broadcast_to(
            block.astype(BF16)[None], (seqs, pieces, lanes)
        )


def prep_body(disc_ref, tmod_ref, embed_ref, proj_ref, out_ref, turned_ref):
    rows = out_ref.shape[0]
    channels = proj_ref.shape[2]
    width = embed_ref.shape[1]
    latent = embed_ref.shape[0]
    start = (seq_index() % (width // rows)) * rows
    gain = 1.0 + tmod_ref[1:2]
    queries = jnp.concatenate(
        [
            embed_ref[...].astype(F32) * gain,
            gain,
            tmod_ref[0:1],
            jnp.zeros((128 - latent - 2, width), F32),
        ],
        axis=0,
    )
    turned_ref[...] = queries.T
    out_ref[:, 2 * channels :] = turned_ref[pl.ds(start, rows), :].astype(BF16)
    for place, head in enumerate(pick_heads(disc_ref)[0]):
        out_ref[:, channels * place : channels * (place + 1)] = proj_ref[head, pl.ds(start, rows), :]


def weight_body(got_ref, down_ref, up_ref, order_ref, out_ref):
    del order_ref
    copies, rows, lanes = out_ref.shape
    split = lanes - 128
    half = pl.ds(pl.multiple_of(lax.axis_index("core") * (copies * rows), 128), copies * rows)
    terms = jnp.concatenate(
        [
            contract(down_ref[:, half], got_ref[:, :split], 0, 0),
            contract(up_ref[:, half], got_ref[:, split:], 0, 0),
        ],
        axis=1,
    )
    out_ref[...] = terms.astype(BF16).reshape(copies, rows, lanes)


def gather_body(parts_ref, order_ref, out_ref):
    del order_ref
    total = jnp.sum(parts_ref[...].astype(F32), axis=0).astype(BF16)
    out_ref[...] = jnp.broadcast_to(total[None], out_ref.shape)


def cross_body(disc_ref, proj_ref, embed_ref, table_ref, cross_ref, taps_ref, turned_ref):
    _, share, lanes = cross_ref.shape
    channels = proj_ref.shape[2]
    per_head = channels // share
    begin = lax.axis_index("mp") * share
    slot = begin // channels
    offset = pl.multiple_of(begin % channels, 8)
    embed = embed_ref[...]
    block, other = pick_heads(disc_ref)
    for place in range(2):
        both = jnp.concatenate(
            [contract(proj_ref[head], embed, 0, 1) for head in (block[place], other[place])], axis=1
        )
        cross_ref[per_head * place : per_head * (place + 1)] = (
            both.astype(BF16).reshape(per_head, share, lanes)
        )
    for place, pair in enumerate((block, other)):
        turned_ref[...] = table_ref[jnp.where(slot == 0, pair[0], pair[1])].T
        taps_ref[share * place : share * (place + 1)] = turned_ref[pl.ds(offset, share), :]


def sums_body(hidden_ref, out_w_ref, embed_ref, mod_ref, sums_ref):
    copies, pieces, _ = mod_ref.shape
    latent, width = out_w_ref.shape
    tokens = hidden_ref.shape[0]
    halves = []
    for half in range(2):
        total = jnp.sum(mod_ref[copies // 2 * half : copies // 2 * (half + 1)].astype(F32), axis=0)
        halves.append(jnp.concatenate([total[p : p + 1] for p in range(pieces)], axis=1))
    shift, scale = halves
    hidden = hidden_ref[...]
    embed = embed_ref[...]
    out_w = out_w_ref[...].astype(F32)
    scaled = (out_w * (1.0 + scale)).astype(BF16)
    ones = jnp.ones((8, width), BF16)
    square = jnp.square(hidden.astype(F32))
    high = square.astype(BF16)
    low = (square - high.astype(F32)).astype(BF16)
    sums_ref[0:latent] = contract(scaled, hidden, 1, 1)
    gram = contract(embed, embed, 1, 1)
    fold = latent // 2
    sums_ref[latent : latent + fold] = jnp.concatenate([gram[:fold], gram[fold:]], axis=1)
    row = lax.broadcasted_iota(jnp.int32, (8, tokens), 0)
    firsts = contract(ones, hidden, 1, 1)
    squares = contract(ones, high, 1, 1) + contract(ones, low, 1, 1)
    pairs = jnp.concatenate([contract(ones, embed, 1, 1), contract(ones, scaled, 1, 1)], axis=1)
    shifted = contract(jnp.broadcast_to(shift, (8, width)), out_w, 1, 1, HIGHEST)
    shifted = jnp.concatenate([shifted, shifted], axis=1)
    sums_ref[latent + fold :] = jnp.where(
        row == 0, firsts, jnp.where(row == 1, squares, jnp.where(row == 2, pairs, shifted))
    )


def noise_body(time_ref, sums_ref, noise_ref, latents_ref, noised_ref, *, width):
    latent, tokens = noise_ref.shape
    base = latent + latent // 2
    mean = sums_ref[base : base + 1] / width
    var = sums_ref[base + 1 : base + 2] / width - mean * mean
    inv_std = lax.rsqrt(var + EPSILON)
    scaled_sum = sums_ref[base + 2 : base + 3, latent:]
    shifted_sum = sums_ref[base + 3 : base + 4, :latent]
    ones = jnp.ones((1, tokens), F32)
    centered = sums_ref[0:latent] - contract(scaled_sum, mean, 0, 0, HIGHEST)
    latents = inv_std * centered + contract(shifted_sum, ones, 0, 0, HIGHEST)
    latents = latents.astype(BF16)
    latents_ref[...] = latents
    level = level_of(time_ref)
    noised_ref[...] = (
        (1.0 - level) * latents.astype(F32) + level * noise_ref[...].astype(F32)
    ).astype(BF16)


def act_body(
    sums_ref,
    cross_noised_ref,
    pair_ref,
    weights_ref,
    cross_ref,
    out_ref,
    pre_ref,
    query_ref,
    side_ref,
    wide_ref,
    act_ref,
    *,
    width,
):
    latent, extent = wide_ref.shape
    tokens = extent // 3
    units = weights_ref.shape[0]
    copies, share, _ = out_ref.shape
    split = weights_ref.shape[1] - 128
    edge = cross_noised_ref[...]
    first = pair_ref[0:latent]
    second = pair_ref[latent:]
    noised_f = jnp.where(
        lax.axis_index("core") == 0,
        jnp.concatenate([edge, first, second], axis=1).astype(F32),
        jnp.concatenate([first, second, edge], axis=1).astype(F32),
    )
    noised = noised_f.astype(BF16)
    wide_ref[...] = noised
    base = latent + latent // 2
    center_row = sums_ref[base + 2 : base + 3, :latent] / width
    gram = jnp.concatenate([sums_ref[latent:base, :latent], sums_ref[latent:base, latent:]], axis=0)
    gram = gram - width * contract(center_row, center_row, 0, 0, HIGHEST)
    gram_noised = contract(gram, noised_f, 1, 0, HIGHEST)
    var = jnp.sum(noised_f * gram_noised, axis=0, keepdims=True) / width
    inv_std = lax.rsqrt(var + EPSILON)
    side_ref[0:latent] = gram_noised[:, tokens : 2 * tokens]
    side_ref[latent:] = jnp.broadcast_to(inv_std[:, tokens : 2 * tokens], (8, tokens))
    step = 128
    for begin in range(0, units, step):
        rows = slice(begin, begin + step)
        raw = weights_ref[rows, split : split + latent].astype(F32)
        gain = weights_ref[rows, split + latent : split + latent + 1].astype(F32)
        shift = weights_ref[rows, split + latent + 1 : split + latent + 2].astype(F32)
        query = (raw - gain * center_row).astype(BF16)
        query_ref[rows] = query
        pre = contract(query, noised, 1, 0) * inv_std + shift
        pre_ref[rows] = pre[:, tokens : 2 * tokens]
        act_ref[rows] = gelu_tanh(pre).astype(BF16)
    part = contract(weights_ref[:, :split], act_ref[...], 0, 0).astype(BF16)
    out_ref[:, :, :extent] = part.reshape(copies, share, extent)
    out_ref[:, :, extent:] = cross_ref[...]


def conv_body(
    parts_ref, wide_ref, taps_ref, pay_ref, back_ref, *, count
):
    _, share, _ = parts_ref.shape
    latent, extent = wide_ref.shape
    own = extent // 3
    channels = 2 * share
    noised = wide_ref[...]
    total = jnp.sum(parts_ref[...].astype(F32), axis=0)
    cross = jnp.concatenate(
        [total[:, extent : extent + latent], total[:, extent + latent :]], axis=0
    ).astype(BF16)
    embed = contract(cross, noised, 1, 0)
    field_in = jnp.concatenate([embed[:share] + total[:, :extent], embed[share:]], axis=0)
    lane = lax.broadcasted_iota(jnp.int32, (channels, extent), 1)
    at = seq_index()
    first = jnp.where(at == 0, own, 0)
    last = jnp.where(at == count - 1, 2 * own, extent)
    inside = (lane >= first) & (lane < last)
    column = lane % GRID_W
    left_ok = column > 0
    right_ok = column < GRID_W - 1

    def tap(row, col):
        place = 3 * row + col
        return taps_ref[:, place : place + 1]

    def convolve(grid, flip):
        before = jnp.where(left_ok, pltpu.roll(grid, 1, 1), 0.0)
        after = jnp.where(right_ok, pltpu.roll(grid, extent - 1, 1), 0.0)
        rows = []
        for row in range(3):
            if flip:
                rows.append(tap(row, 2) * before + tap(row, 1) * grid + tap(row, 0) * after)
            else:
                rows.append(tap(row, 0) * before + tap(row, 1) * grid + tap(row, 2) * after)
        if flip:
            rows = rows[::-1]
        return pltpu.roll(rows[0], GRID_W, 1) + rows[1] + pltpu.roll(rows[2], extent - GRID_W, 1)

    field = convolve(jnp.where(inside, field_in, 0.0), False)
    gating = jax.nn.sigmoid(field)
    scale = taps_ref[:, 9:10]
    terms = field * gating * scale
    slope = -scale * gating * (1.0 + field * (1.0 - gating))
    grad = convolve(jnp.where(inside, slope, 0.0), True)[:, own : 2 * own]
    block_sum = jnp.sum(terms[:share, own : 2 * own], axis=0, keepdims=True)
    embed_sum = jnp.sum(terms[share:, own : 2 * own], axis=0, keepdims=True)
    sums = jnp.concatenate([block_sum, embed_sum], axis=0)
    high = sums.astype(BF16).astype(F32)
    low = sums - high
    tail = jnp.concatenate([high, low, jnp.zeros((12, own), F32)], axis=0)
    pay = jnp.concatenate([grad[:share], tail], axis=0).astype(BF16)
    pay_ref[...] = jnp.broadcast_to(pay[None], pay_ref.shape)
    back_ref[...] = contract(cross, grad.astype(BF16), 0, 0)


def back_body(
    disc_ref,
    pay_ref,
    weights_ref,
    query_ref,
    slope_ref,
    side_ref,
    noised_ref,
    back_ref,
    out_ref,
    logits_ref,
    *,
    width,
):
    copies, rows, tokens = pay_ref.shape
    share = rows - 16
    latent = noised_ref.shape[0]
    split = copies * share
    grads = jnp.concatenate([pay_ref[copy, :share] for copy in range(copies)], axis=0)
    hidden_grad = contract(weights_ref[:, :split], grads, 1, 0)
    preact_grad = (hidden_grad * slope_ref[...]).astype(BF16)
    query_grad = contract(query_ref[...], preact_grad, 0, 0)
    inv_std = side_ref[latent : latent + 1]
    along = jnp.sum(noised_ref[...].astype(F32) * query_grad, axis=0, keepdims=True)
    result = (
        inv_std * (query_grad - (inv_std * inv_std / width) * along * side_ref[0:latent])
        + back_ref[...]
    )
    out_ref[...] = jnp.broadcast_to(result.astype(BF16)[None], out_ref.shape)
    sums = []
    for place in range(2):
        total = jnp.zeros((16, tokens), F32)
        for copy in range(copies // 2 * place, copies // 2 * (place + 1)):
            total = total + pay_ref[copy, share:].astype(F32)
        sums.append(total[0:2] + total[2:4])
    block, other = pick_heads(disc_ref)
    for k in range(4):
        chosen = jnp.where(block[0] == k, 0, jnp.where(block[1] == k, 1, jnp.where(other[0] == k, 2, 3)))
        options = [sums[0][0:1], sums[1][0:1], sums[0][1:2], sums[1][1:2]]
        value = options[3]
        for place in range(3):
            value = jnp.where(chosen == place, options[place], value)
        logits_ref[k : k + 1] = value


def final_body(time_ref, parts_ref, out_ref):
    retain = 1.0 - level_of(time_ref)
    out_ref[...] = retain * jnp.sum(parts_ref[...].astype(F32), axis=0)


def per_device(
    student_hidden,
    student_cond,
    student_mod,
    student_out,
    timestep,
    noise,
    teacher_embed,
    teacher_mod,
    up_weight,
    down_weight,
    head_proj,
    head_kernel,
    head_out,
    disc_layer,
):
    groups = lax.axis_size("group")
    planes = lax.axis_size("plane")
    seqs = 2 * planes
    mps = lax.axis_size("mp")
    _, tokens, local_width = student_hidden.shape
    width = local_width * mps
    latent = teacher_embed.shape[0]
    units = down_weight.shape[0]
    channels = head_proj.shape[2]
    share = 2 * channels // mps
    lanes = 2 * channels + 128
    extent = 3 * tokens

    pieces = local_width // 128
    (mods,) = call(
        smod_body, [((groups * seqs, pieces, 128), BF16)], [], [student_cond, student_mod[:, 0]]
    )
    mods = exchange(mods, ("group",) + SEQ)

    tmod = jnp.einsum(
        "sf,fjd->sjd",
        time_features(timestep, teacher_mod.shape[0]),
        teacher_mod.astype(F32),
        precision=HIGHEST,
    )[0]
    ratio = seqs // mps
    rows = local_width // ratio
    (sent,) = call(
        prep_body,
        [((rows, lanes), BF16)],
        [disc_layer],
        [tmod, teacher_embed, head_proj],
        [((local_width, 128), F32)],
    )
    swap = [
        (at * mps + m, (ratio * m + at % ratio) * mps + at // ratio)
        for at in range(seqs)
        for m in range(mps)
    ]
    got = lax.ppermute(sent, SEQ + ("mp",), swap)
    down_pair = lax.all_gather(down_weight.T, "core", axis=0, tiled=True)
    up_pair = lax.all_gather(up_weight, "core", axis=0, tiled=True)
    got = lax.all_gather(got, "core", axis=0, tiled=True)
    (terms,) = call(
        weight_body, [((planes, units // seqs, lanes), BF16)], [], [got, down_pair, up_pair, mods]
    )
    terms = exchange(terms, "plane")
    table = jnp.concatenate(
        [head_kernel.reshape(4, 9, channels), head_out[:, None], jnp.zeros((4, 6, channels), F32)],
        axis=1,
    )
    cross, taps = call(
        cross_body,
        [((mps, share, 2 * latent), BF16), ((2 * share, 16), F32)],
        [disc_layer],
        [head_proj, teacher_embed, table],
        [((channels, 16), F32)],
    )

    (sums,) = call(
        sums_body,
        [((latent + latent // 2 + 8, tokens), F32)],
        [],
        [student_hidden[0], student_out.T, teacher_embed, mods],
    )
    stages = [sums]
    step = 1
    while step < mps:
        sums = sums + lax.ppermute(sums, "mp", [(i, i ^ step) for i in range(mps)])
        step *= 2
        stages.append(sums)
    halfway = stages[-2]
    (terms,) = call(gather_body, [((planes, units // seqs, lanes), BF16)], [], [terms, halfway])
    weights = exchange(terms, "plane").reshape(units // 2, lanes)
    weights = lax.all_gather(weights, "core", axis=0, tiled=True)

    latents, noised = call(
        functools.partial(noise_body, width=float(width)),
        [((latent, tokens), BF16), ((latent, tokens), BF16)],
        [timestep],
        [sums, noise[0].T],
        loose=(0,),
    )
    swap = [(i, i + 1 if i % 2 else i - 1) for i in range(1, seqs - 1)]
    edge = lax.ppermute(noised, SEQ, swap)
    pair = lax.all_gather(noised, "core", axis=0, tiled=True)

    parts, preact, query, side, wide = call(
        functools.partial(act_body, width=float(width)),
        [
            ((mps, share, extent + 2 * latent), BF16),
            ((units, tokens), F32),
            ((units, latent), BF16),
            ((latent + 8, tokens), F32),
            ((latent, extent), BF16),
        ],
        [],
        [sums, edge, pair, weights, cross],
        [((units, extent), BF16)],
    )
    parts = exchange(parts, "mp")
    slope = gelu_slope(preact)
    pay, back = call(
        functools.partial(conv_body, count=seqs),
        [((mps, share + 16, tokens), BF16), ((latent, tokens), F32)],
        [],
        [parts, wide, taps],
    )
    pay = exchange(pay, "mp")
    back, logits = call(
        functools.partial(back_body, width=float(width)),
        [((mps, latent, tokens), BF16), ((4, tokens), F32)],
        [disc_layer],
        [pay, weights, query, slope, side, noised, back],
        loose=(1,),
    )
    back = exchange(back, "mp")
    (latent_grad,) = call(final_body, [((latent, tokens), F32)], [timestep], [back], loose=(0,))
    return (latents.T[None], logits[None], latent_grad.T[None])


def solution(mesh):
    groups, seqs, mps = mesh.devices.shape
    split = Mesh(
        mesh.devices.reshape(groups, seqs // 2, 2, mps), ("group", "plane", "core", "mp")
    )
    return jax.shard_map(
        per_device,
        mesh=split,
        in_specs=(
            P("group", SEQ, "mp"),
            P(None, SEQ),
            P(SEQ, "group", "mp"),
            P("mp", None),
            P("group"),
            P("group", SEQ, None),
            P(None, "mp"),
            P(None, None, "mp"),
            P(SEQ, "mp"),
            P("mp", SEQ),
            P(None, "mp", None),
            P(),
            P(),
            P("group", None),
        ),
        out_specs=(P("group", SEQ, None), P("group", None, SEQ), P("group", SEQ, None)),
        check_vma=False,
    )
```

```python
import functools
import math

import jax
import jax.numpy as jnp
from jax import lax
from jax.experimental import pallas as pl
from jax.experimental.pallas import tpu as pltpu
from jax.sharding import Mesh
from jax.sharding import PartitionSpec as P


GRID_W = 64
EPSILON = 1e-06
GELU_COEF = 0.7978845608028654
INTERPRET = False

F32 = jnp.float32
BF16 = jnp.bfloat16
HIGHEST = lax.Precision.HIGHEST


def contract(left, right, left_dim, right_dim, precision=None):
    return lax.dot_general(
        left,
        right,
        (((left_dim,), (right_dim,)), ((), ())),
        precision=precision,
        preferred_element_type=F32,
    )


def gelu_tanh(values):
    inner = GELU_COEF * (values + 0.044715 * values * values * values)
    return 0.5 * values * (1.0 + jnp.tanh(inner))


def gelu_slope(values):
    inner = GELU_COEF * (values + 0.044715 * values * values * values)
    tangent = jnp.tanh(inner)
    return 0.5 * (1.0 + tangent) + 0.5 * values * (1.0 - tangent * tangent) * GELU_COEF * (
        1.0 + 3.0 * 0.044715 * values * values
    )


def time_features(timestep, width):
    half_width = width // 2
    index = jnp.arange(half_width, dtype=F32)
    freqs = jnp.exp(-math.log(10000.0) * index / half_width)
    angles = timestep.astype(F32)[:, None] * freqs[None, :]
    return jnp.concatenate([jnp.cos(angles), jnp.sin(angles)], axis=-1)


SEQ = ("plane", "core")


def seq_index():
    return lax.axis_index("plane") * 2 + lax.axis_index("core")


def exchange(value, axes):
    return lax.all_to_all(value, axes, 0, 0, tiled=False)


def call(body, outs, scalars, arrays, scratch=(), loose=(), distant=(), plain=()):
    smem = pl.BlockSpec(memory_space=pltpu.SMEM)
    vmem = pl.BlockSpec(memory_space=pltpu.VMEM)
    if INTERPRET:
        shapes = [jax.ShapeDtypeStruct(shape, dtype) for shape, dtype in outs]
    else:
        shapes = [
            jax.ShapeDtypeStruct(*out) if place in loose else pltpu.VMEM(*out)
            for place, out in enumerate(outs)
        ]
        arrays = [
            value if place in plain else pltpu.with_memory_space_constraint(value, pltpu.VMEM)
            for place, value in enumerate(arrays)
        ]
    return pl.pallas_call(
        body,
        in_specs=[smem] * len(scalars)
        + [vmem] * len(arrays)
        + [pl.BlockSpec(memory_space=pl.ANY)] * len(distant),
        out_specs=[vmem] * len(outs),
        out_shape=shapes,
        scratch_shapes=[pltpu.VMEM(shape, dtype) for shape, dtype in scratch]
        + [pltpu.SemaphoreType.DMA] * len(distant),
        interpret=INTERPRET,
    )(*scalars, *arrays, *distant)


def pick_heads(disc_ref):
    picks = [disc_ref[0, k] for k in range(4)]
    pairs = []
    for layer in (1, 0):
        first = jnp.where(picks[0] == layer, 0, jnp.where(picks[1] == layer, 1, 2))
        last = jnp.where(picks[3] == layer, 3, jnp.where(picks[2] == layer, 2, 1))
        pairs.append((first, last))
    return pairs


def level_of(time_ref):
    return time_ref[0].astype(F32) / 1000.0


def open_body(
    disc_ref,
    cond_ref,
    mod_ref,
    tmod_ref,
    embed_ref,
    proj_ref,
    taps_in_ref,
    head_out_ref,
    noise_in_ref,
    sent_ref,
    mods_ref,
    cross_ref,
    taps_ref,
    noise_ref,
    queries_ref,
    turned_ref,
    noise_sem,
):
    fetch = pltpu.make_async_copy(noise_in_ref, noise_ref, noise_sem)
    fetch.start()
    block, other = pick_heads(disc_ref)
    channels = proj_ref.shape[2]
    latent, width = embed_ref.shape

    rows = sent_ref.shape[0]
    start = pl.multiple_of((seq_index() % (width // rows)) * rows, rows)
    embed = embed_ref[...]
    gain = 1.0 + tmod_ref[1:2]
    queries = jnp.concatenate(
        [
            embed.astype(F32) * gain,
            gain,
            tmod_ref[0:1],
            jnp.zeros((128 - latent - 2, width), F32),
        ],
        axis=0,
    )
    queries_ref[...] = queries.T
    sent_ref[:, 2 * channels :] = queries_ref[pl.ds(start, rows), :].astype(BF16)
    for place, head in enumerate(block):
        sent_ref[:, channels * place : channels * (place + 1)] = proj_ref[head, pl.ds(start, rows), :]

    groups = cond_ref.shape[0]
    copies, pieces, lanes = mods_ref.shape
    seqs = copies // groups
    half = contract(cond_ref[...], mod_ref[...].astype(F32), 1, 0, HIGHEST)
    for group in range(groups):
        row = half[group : group + 1]
        pieces_of = jnp.concatenate(
            [row[:, lanes * p : lanes * (p + 1)] for p in range(pieces)], axis=0
        )
        mods_ref[seqs * group : seqs * (group + 1)] = jnp.broadcast_to(
            pieces_of.astype(BF16)[None], (seqs, pieces, lanes)
        )

    _, share, pair_lanes = cross_ref.shape
    per_head = channels // share
    begin = lax.axis_index("mp") * share
    slot = begin // channels
    offset = pl.multiple_of(begin % channels, 8)
    for place in range(2):
        both = jnp.concatenate(
            [contract(proj_ref[head], embed, 0, 1) for head in (block[place], other[place])], axis=1
        )
        cross_ref[per_head * place : per_head * (place + 1)] = (
            both.astype(BF16).reshape(per_head, share, pair_lanes)
        )
    for place, pair in enumerate((block, other)):
        head = jnp.where(slot == 0, pair[0], pair[1])
        table = jnp.concatenate(
            [taps_in_ref[tap, pl.ds(head, 1), :] for tap in range(9)]
            + [head_out_ref[pl.ds(head, 1), :], jnp.zeros((6, channels), F32)],
            axis=0,
        )
        turned_ref[...] = table.T
        taps_ref[share * place : share * (place + 1)] = turned_ref[pl.ds(offset, share), :]
    fetch.wait()


def weight_body(got_ref, pair_ref, order_ref, out_ref):
    del order_ref
    copies, rows, lanes = out_ref.shape
    split = lanes - 128
    depth = got_ref.shape[0] // 2
    half = pl.ds(pl.multiple_of(lax.axis_index("core") * (copies * rows), 128), copies * rows)
    down = jnp.concatenate([pair_ref[0:depth, half], pair_ref[2 * depth : 3 * depth, half]], axis=0)
    up = jnp.concatenate([pair_ref[depth : 2 * depth, half], pair_ref[3 * depth :, half]], axis=0)
    terms = jnp.concatenate(
        [contract(down, got_ref[:, :split], 0, 0), contract(up, got_ref[:, split:], 0, 0)], axis=1
    )
    out_ref[...] = terms.astype(BF16).reshape(copies, rows, lanes)


def gather_body(parts_ref, order_ref, out_ref):
    del order_ref
    total = jnp.sum(parts_ref[...].astype(F32), axis=0).astype(BF16)
    out_ref[...] = jnp.broadcast_to(total[None], out_ref.shape)


def sums_body(hidden_ref, out_w_ref, embed_ref, mod_ref, sums_ref):
    copies, pieces, _ = mod_ref.shape
    latent, width = out_w_ref.shape
    tokens = hidden_ref.shape[0]
    halves = []
    for half in range(2):
        total = jnp.sum(mod_ref[copies // 2 * half : copies // 2 * (half + 1)].astype(F32), axis=0)
        halves.append(jnp.concatenate([total[p : p + 1] for p in range(pieces)], axis=1))
    shift, scale = halves
    hidden = hidden_ref[...]
    embed = embed_ref[...]
    out_w = out_w_ref[...].astype(F32)
    scaled = (out_w * (1.0 + scale)).astype(BF16)
    ones = jnp.ones((8, width), BF16)
    square = jnp.square(hidden.astype(F32))
    high = square.astype(BF16)
    low = (square - high.astype(F32)).astype(BF16)
    sums_ref[0:latent] = contract(scaled, hidden, 1, 1)
    gram = contract(embed, embed, 1, 1)
    fold = latent // 2
    sums_ref[latent : latent + fold] = jnp.concatenate([gram[:fold], gram[fold:]], axis=1)
    row = lax.broadcasted_iota(jnp.int32, (8, tokens), 0)
    firsts = contract(ones, hidden, 1, 1)
    squares = contract(ones, high, 1, 1) + contract(ones, low, 1, 1)
    pairs = jnp.concatenate([contract(ones, embed, 1, 1), contract(ones, scaled, 1, 1)], axis=1)
    shifted = contract(jnp.broadcast_to(shift, (8, width)), out_w, 1, 1, HIGHEST)
    shifted = jnp.concatenate([shifted, shifted], axis=1)
    sums_ref[latent + fold :] = jnp.where(
        row == 0, firsts, jnp.where(row == 1, squares, jnp.where(row == 2, pairs, shifted))
    )


def noise_body(time_ref, sums_ref, noise_ref, latents_ref, noised_ref, *, width):
    latent, tokens = noise_ref.shape
    base = latent + latent // 2
    mean = sums_ref[base : base + 1] / width
    var = sums_ref[base + 1 : base + 2] / width - mean * mean
    inv_std = lax.rsqrt(var + EPSILON)
    scaled_sum = sums_ref[base + 2 : base + 3, latent:]
    shifted_sum = sums_ref[base + 3 : base + 4, :latent]
    ones = jnp.ones((1, tokens), F32)
    centered = sums_ref[0:latent] - contract(scaled_sum, mean, 0, 0, HIGHEST)
    latents = inv_std * centered + contract(shifted_sum, ones, 0, 0, HIGHEST)
    latents = latents.astype(BF16)
    latents_ref[...] = latents
    level = level_of(time_ref)
    noised_ref[...] = (
        (1.0 - level) * latents.astype(F32) + level * noise_ref[...].astype(F32)
    ).astype(BF16)


def act_body(
    sums_ref,
    cross_noised_ref,
    pair_ref,
    weights_ref,
    cross_ref,
    out_ref,
    pre_ref,
    query_ref,
    side_ref,
    wide_ref,
    act_ref,
    *,
    width,
):
    latent, extent = wide_ref.shape
    tokens = extent // 3
    units = weights_ref.shape[0]
    copies, share, _ = out_ref.shape
    split = weights_ref.shape[1] - 128
    edge = cross_noised_ref[...]
    first = pair_ref[0:latent]
    second = pair_ref[latent:]
    noised_f = jnp.where(
        lax.axis_index("core") == 0,
        jnp.concatenate([edge, first, second], axis=1).astype(F32),
        jnp.concatenate([first, second, edge], axis=1).astype(F32),
    )
    noised = noised_f.astype(BF16)
    wide_ref[...] = noised
    base = latent + latent // 2
    center_row = sums_ref[base + 2 : base + 3, :latent] / width
    gram = jnp.concatenate([sums_ref[latent:base, :latent], sums_ref[latent:base, latent:]], axis=0)
    gram = gram - width * contract(center_row, center_row, 0, 0, HIGHEST)
    gram_noised = contract(gram, noised_f, 1, 0, HIGHEST)
    var = jnp.sum(noised_f * gram_noised, axis=0, keepdims=True) / width
    inv_std = lax.rsqrt(var + EPSILON)
    side_ref[0:latent] = gram_noised[:, tokens : 2 * tokens]
    side_ref[latent:] = jnp.broadcast_to(inv_std[:, tokens : 2 * tokens], (8, tokens))
    step = 128
    for begin in range(0, units, step):
        rows = slice(begin, begin + step)
        raw = weights_ref[rows, split : split + latent].astype(F32)
        gain = weights_ref[rows, split + latent : split + latent + 1].astype(F32)
        shift = weights_ref[rows, split + latent + 1 : split + latent + 2].astype(F32)
        query = (raw - gain * center_row).astype(BF16)
        query_ref[rows] = query
        pre = contract(query, noised, 1, 0) * inv_std + shift
        pre_ref[rows] = pre[:, tokens : 2 * tokens]
        act_ref[rows] = gelu_tanh(pre).astype(BF16)
    part = contract(weights_ref[:, :split], act_ref[...], 0, 0).astype(BF16)
    out_ref[:, :, :extent] = part.reshape(copies, share, extent)
    out_ref[:, :, extent:] = cross_ref[...]


def conv_body(
    parts_ref, wide_ref, taps_ref, pay_ref, back_ref, *, count
):
    _, share, _ = parts_ref.shape
    latent, extent = wide_ref.shape
    own = extent // 3
    channels = 2 * share
    noised = wide_ref[...]
    total = jnp.sum(parts_ref[...].astype(F32), axis=0)
    cross = jnp.concatenate(
        [total[:, extent : extent + latent], total[:, extent + latent :]], axis=0
    ).astype(BF16)
    embed = contract(cross, noised, 1, 0)
    field_in = jnp.concatenate([embed[:share] + total[:, :extent], embed[share:]], axis=0)
    lane = lax.broadcasted_iota(jnp.int32, (channels, extent), 1)
    at = seq_index()
    first = jnp.where(at == 0, own, 0)
    last = jnp.where(at == count - 1, 2 * own, extent)
    inside = (lane >= first) & (lane < last)
    column = lane % GRID_W
    left_ok = column > 0
    right_ok = column < GRID_W - 1

    def tap(row, col):
        place = 3 * row + col
        return taps_ref[:, place : place + 1]

    def convolve(grid, flip):
        before = jnp.where(left_ok, pltpu.roll(grid, 1, 1), 0.0)
        after = jnp.where(right_ok, pltpu.roll(grid, extent - 1, 1), 0.0)
        rows = []
        for row in range(3):
            if flip:
                rows.append(tap(row, 2) * before + tap(row, 1) * grid + tap(row, 0) * after)
            else:
                rows.append(tap(row, 0) * before + tap(row, 1) * grid + tap(row, 2) * after)
        if flip:
            rows = rows[::-1]
        return pltpu.roll(rows[0], GRID_W, 1) + rows[1] + pltpu.roll(rows[2], extent - GRID_W, 1)

    field = convolve(jnp.where(inside, field_in, 0.0), False)
    gating = jax.nn.sigmoid(field)
    scale = taps_ref[:, 9:10]
    terms = field * gating * scale
    slope = -scale * gating * (1.0 + field * (1.0 - gating))
    grad = convolve(jnp.where(inside, slope, 0.0), True)[:, own : 2 * own]
    block_sum = jnp.sum(terms[:share, own : 2 * own], axis=0, keepdims=True)
    embed_sum = jnp.sum(terms[share:, own : 2 * own], axis=0, keepdims=True)
    sums = jnp.concatenate([block_sum, embed_sum], axis=0)
    high = sums.astype(BF16).astype(F32)
    low = sums - high
    tail = jnp.concatenate([high, low, jnp.zeros((12, own), F32)], axis=0)
    pay = jnp.concatenate([grad[:share], tail], axis=0).astype(BF16)
    pay_ref[...] = jnp.broadcast_to(pay[None], pay_ref.shape)
    back_ref[...] = contract(cross, grad.astype(BF16), 0, 0)


def back_body(
    disc_ref,
    pay_ref,
    weights_ref,
    query_ref,
    slope_ref,
    side_ref,
    noised_ref,
    back_ref,
    out_ref,
    logits_ref,
    *,
    width,
):
    copies, rows, tokens = pay_ref.shape
    share = rows - 16
    latent = noised_ref.shape[0]
    split = copies * share
    grads = jnp.concatenate([pay_ref[copy, :share] for copy in range(copies)], axis=0)
    hidden_grad = contract(weights_ref[:, :split], grads, 1, 0)
    preact_grad = (hidden_grad * slope_ref[...]).astype(BF16)
    query_grad = contract(query_ref[...], preact_grad, 0, 0)
    inv_std = side_ref[latent : latent + 1]
    along = jnp.sum(noised_ref[...].astype(F32) * query_grad, axis=0, keepdims=True)
    result = (
        inv_std * (query_grad - (inv_std * inv_std / width) * along * side_ref[0:latent])
        + back_ref[...]
    )
    out_ref[...] = jnp.broadcast_to(result.astype(BF16)[None], out_ref.shape)
    sums = []
    for place in range(2):
        total = jnp.zeros((16, tokens), F32)
        for copy in range(copies // 2 * place, copies // 2 * (place + 1)):
            total = total + pay_ref[copy, share:].astype(F32)
        sums.append(total[0:2] + total[2:4])
    block, other = pick_heads(disc_ref)
    for k in range(4):
        chosen = jnp.where(block[0] == k, 0, jnp.where(block[1] == k, 1, jnp.where(other[0] == k, 2, 3)))
        options = [sums[0][0:1], sums[1][0:1], sums[0][1:2], sums[1][1:2]]
        value = options[3]
        for place in range(3):
            value = jnp.where(chosen == place, options[place], value)
        logits_ref[k : k + 1] = value


def final_body(time_ref, parts_ref, out_ref):
    retain = 1.0 - level_of(time_ref)
    out_ref[...] = retain * jnp.sum(parts_ref[...].astype(F32), axis=0)


def per_device(
    student_hidden,
    student_cond,
    student_mod,
    student_out,
    timestep,
    noise,
    teacher_embed,
    teacher_mod,
    up_weight,
    down_weight,
    head_proj,
    head_kernel,
    head_out,
    disc_layer,
):
    groups = lax.axis_size("group")
    planes = lax.axis_size("plane")
    seqs = 2 * planes
    mps = lax.axis_size("mp")
    _, tokens, local_width = student_hidden.shape
    width = local_width * mps
    latent = teacher_embed.shape[0]
    units = down_weight.shape[0]
    channels = head_proj.shape[2]
    share = 2 * channels // mps
    lanes = 2 * channels + 128
    extent = 3 * tokens

    tmod = jnp.einsum(
        "sf,fjd->sjd",
        time_features(timestep, teacher_mod.shape[0]),
        teacher_mod.astype(F32),
        precision=HIGHEST,
    )[0]
    ratio = seqs // mps
    rows = local_width // ratio
    pieces = local_width // 128
    sent, mods, cross, taps, noise_t = call(
        open_body,
        [
            ((rows, lanes), BF16),
            ((groups * seqs, pieces, 128), BF16),
            ((mps, share, 2 * latent), BF16),
            ((2 * share, 16), F32),
            ((latent, tokens), BF16),
        ],
        [disc_layer],
        [
            student_cond,
            student_mod[:, 0],
            tmod,
            teacher_embed,
            head_proj,
            jnp.transpose(head_kernel, (1, 2, 0, 3)).reshape(9, 4, channels),
            head_out,
        ],
        [((local_width, 128), F32), ((channels, 16), F32)],
        distant=[noise[0].T],
        plain=(0, 1, 3, 5, 6),
    )

    swap = [
        (at * mps + m, (ratio * m + at % ratio) * mps + at // ratio)
        for at in range(seqs)
        for m in range(mps)
    ]
    got = lax.ppermute(sent, SEQ + ("mp",), swap)

    mods = exchange(mods, ("group",) + SEQ)
    slices = jnp.concatenate([down_weight.T, up_weight], axis=0)
    slices = lax.all_gather(slices, "core", axis=0, tiled=True)
    got = lax.all_gather(got, "core", axis=0, tiled=True)
    (terms,) = call(weight_body, [((planes, units // seqs, lanes), BF16)], [], [got, slices, mods])
    terms = exchange(terms, "plane")
    (sums,) = call(
        sums_body,
        [((latent + latent // 2 + 8, tokens), F32)],
        [],
        [student_hidden[0], student_out.T, teacher_embed, mods],
    )
    stages = [sums]
    step = 1
    while step < mps:
        sums = sums + lax.ppermute(sums, "mp", [(i, i ^ step) for i in range(mps)])
        step *= 2
        stages.append(sums)
    halfway = stages[-2]
    (terms,) = call(gather_body, [((planes, units // seqs, lanes), BF16)], [], [terms, halfway])
    weights = exchange(terms, "plane").reshape(units // 2, lanes)
    weights = lax.all_gather(weights, "core", axis=0, tiled=True)

    latents, noised = call(
        functools.partial(noise_body, width=float(width)),
        [((latent, tokens), BF16), ((latent, tokens), BF16)],
        [timestep],
        [sums, noise_t],
        loose=(0,),
    )
    swap = [(i, i + 1 if i % 2 else i - 1) for i in range(1, seqs - 1)]
    edge = lax.ppermute(noised, SEQ, swap)
    pair = lax.all_gather(noised, "core", axis=0, tiled=True)

    parts, preact, query, side, wide = call(
        functools.partial(act_body, width=float(width)),
        [
            ((mps, share, extent + 2 * latent), BF16),
            ((units, tokens), F32),
            ((units, latent), BF16),
            ((latent + 8, tokens), F32),
            ((latent, extent), BF16),
        ],
        [],
        [sums, edge, pair, weights, cross],
        [((units, extent), BF16)],
    )
    parts = exchange(parts, "mp")
    slope = gelu_slope(preact)
    pay, back = call(
        functools.partial(conv_body, count=seqs),
        [((mps, share + 16, tokens), BF16), ((latent, tokens), F32)],
        [],
        [parts, wide, taps],
    )
    pay = exchange(pay, "mp")
    back, logits = call(
        functools.partial(back_body, width=float(width)),
        [((mps, latent, tokens), BF16), ((4, tokens), F32)],
        [disc_layer],
        [pay, weights, query, slope, side, noised, back],
        loose=(1,),
    )
    back = exchange(back, "mp")
    (latent_grad,) = call(final_body, [((latent, tokens), F32)], [timestep], [back], loose=(0,))
    return (latents.T[None], logits[None], latent_grad.T[None])


def solution(mesh):
    groups, seqs, mps = mesh.devices.shape
    split = Mesh(
        mesh.devices.reshape(groups, seqs // 2, 2, mps), ("group", "plane", "core", "mp")
    )
    return jax.shard_map(
        per_device,
        mesh=split,
        in_specs=(
            P("group", SEQ, "mp"),
            P(None, SEQ),
            P(SEQ, "group", "mp"),
            P("mp", None),
            P("group"),
            P("group", SEQ, None),
            P(None, "mp"),
            P(None, None, "mp"),
            P(SEQ, "mp"),
            P("mp", SEQ),
            P(None, "mp", None),
            P(),
            P(),
            P("group", None),
        ),
        out_specs=(P("group", SEQ, None), P("group", None, SEQ), P("group", SEQ, None)),
        check_vma=False,
    )
```

```python
import functools
import math

import jax
import jax.numpy as jnp
from jax import lax
from jax.experimental import pallas as pl
from jax.experimental.pallas import tpu as pltpu
from jax.sharding import Mesh
from jax.sharding import PartitionSpec as P


GRID_W = 64
EPSILON = 1e-06
GELU_COEF = 0.7978845608028654
INTERPRET = False

F32 = jnp.float32
BF16 = jnp.bfloat16
HIGHEST = lax.Precision.HIGHEST


def contract(left, right, left_dim, right_dim, precision=None):
    return lax.dot_general(
        left,
        right,
        (((left_dim,), (right_dim,)), ((), ())),
        precision=precision,
        preferred_element_type=F32,
    )


def gelu_tanh(values):
    inner = GELU_COEF * (values + 0.044715 * values * values * values)
    return 0.5 * values * (1.0 + jnp.tanh(inner))


def gelu_slope(values):
    inner = GELU_COEF * (values + 0.044715 * values * values * values)
    tangent = jnp.tanh(inner)
    return 0.5 * (1.0 + tangent) + 0.5 * values * (1.0 - tangent * tangent) * GELU_COEF * (
        1.0 + 3.0 * 0.044715 * values * values
    )


def time_features(timestep, width):
    half_width = width // 2
    index = jnp.arange(half_width, dtype=F32)
    freqs = jnp.exp(-math.log(10000.0) * index / half_width)
    angles = timestep.astype(F32)[:, None] * freqs[None, :]
    return jnp.concatenate([jnp.cos(angles), jnp.sin(angles)], axis=-1)


SEQ = ("plane", "core")


def seq_index():
    return lax.axis_index("plane") * 2 + lax.axis_index("core")


def exchange(value, axes):
    return lax.all_to_all(value, axes, 0, 0, tiled=False)


def call(body, outs, scalars, arrays, scratch=(), loose=(), distant=(), plain=(), away=()):
    smem = pl.BlockSpec(memory_space=pltpu.SMEM)
    vmem = pl.BlockSpec(memory_space=pltpu.VMEM)
    if INTERPRET:
        shapes = [jax.ShapeDtypeStruct(shape, dtype) for shape, dtype in outs]
    else:
        shapes = [
            jax.ShapeDtypeStruct(*out) if place in loose + away else pltpu.VMEM(*out)
            for place, out in enumerate(outs)
        ]
        arrays = [
            value if place in plain else pltpu.with_memory_space_constraint(value, pltpu.VMEM)
            for place, value in enumerate(arrays)
        ]
    return pl.pallas_call(
        body,
        in_specs=[smem] * len(scalars)
        + [vmem] * len(arrays)
        + [pl.BlockSpec(memory_space=pl.ANY)] * len(distant),
        out_specs=[
            pl.BlockSpec(memory_space=pl.ANY) if place in away else vmem for place in range(len(outs))
        ],
        out_shape=shapes,
        scratch_shapes=[pltpu.VMEM(shape, dtype) for shape, dtype in scratch]
        + [pltpu.SemaphoreType.DMA] * (len(distant) + len(away)),
        interpret=INTERPRET,
    )(*scalars, *arrays, *distant)


def pick_heads(disc_ref):
    picks = [disc_ref[0, k] for k in range(4)]
    pairs = []
    for layer in (1, 0):
        first = jnp.where(picks[0] == layer, 0, jnp.where(picks[1] == layer, 1, 2))
        last = jnp.where(picks[3] == layer, 3, jnp.where(picks[2] == layer, 2, 1))
        pairs.append((first, last))
    return pairs


def level_of(time_ref):
    return time_ref[0:1] / 1000.0


def open_body(
    disc_ref,
    cond_ref,
    mod_ref,
    tmod_ref,
    embed_ref,
    proj_ref,
    taps_in_ref,
    head_out_ref,
    noise_in_ref,
    sent_ref,
    mods_ref,
    cross_ref,
    taps_ref,
    noise_ref,
    queries_ref,
    turned_ref,
    terms_ref,
    noise_sem,
    terms_sem,
):
    fetch = pltpu.make_async_copy(noise_in_ref, noise_ref, noise_sem)
    fetch.start()
    block, other = pick_heads(disc_ref)
    channels = proj_ref.shape[2]
    latent, width = embed_ref.shape

    groups = cond_ref.shape[0]
    copies, pieces, lanes = mods_ref.shape
    seqs = copies // groups
    half = contract(cond_ref[...], mod_ref[...].astype(F32), 1, 0, HIGHEST)
    for group in range(groups):
        row = half[group : group + 1]
        pieces_of = jnp.concatenate(
            [row[:, lanes * p : lanes * (p + 1)] for p in range(pieces)], axis=0
        )
        terms_ref[seqs * group : seqs * (group + 1)] = jnp.broadcast_to(
            pieces_of.astype(BF16)[None], (seqs, pieces, lanes)
        )
    store = pltpu.make_async_copy(terms_ref, mods_ref, terms_sem)
    store.start()

    rows = sent_ref.shape[0]
    start = pl.multiple_of((seq_index() % (width // rows)) * rows, rows)
    embed = embed_ref[...]
    gain = 1.0 + tmod_ref[1:2]
    queries = jnp.concatenate(
        [
            embed.astype(F32) * gain,
            gain,
            tmod_ref[0:1],
            jnp.zeros((128 - latent - 2, width), F32),
        ],
        axis=0,
    )
    queries_ref[...] = queries.T
    sent_ref[:, 2 * channels :] = queries_ref[pl.ds(start, rows), :].astype(BF16)
    for place, head in enumerate(block):
        sent_ref[:, channels * place : channels * (place + 1)] = proj_ref[head, pl.ds(start, rows), :]

    _, share, pair_lanes = cross_ref.shape
    per_head = channels // share
    begin = lax.axis_index("mp") * share
    slot = begin // channels
    offset = pl.multiple_of(begin % channels, 8)
    for place in range(2):
        both = jnp.concatenate(
            [contract(proj_ref[head], embed, 0, 1) for head in (block[place], other[place])], axis=1
        )
        cross_ref[per_head * place : per_head * (place + 1)] = (
            both.astype(BF16).reshape(per_head, share, pair_lanes)
        )
    for place, pair in enumerate((block, other)):
        head = jnp.where(slot == 0, pair[0], pair[1])
        table = jnp.concatenate(
            [taps_in_ref[tap, pl.ds(head, 1), :] for tap in range(9)]
            + [head_out_ref[pl.ds(head, 1), :], jnp.zeros((6, channels), F32)],
            axis=0,
        )
        turned_ref[...] = table.T
        taps_ref[share * place : share * (place + 1)] = turned_ref[pl.ds(offset, share), :]
    store.wait()
    fetch.wait()


def weight_body(got_ref, pair_ref, order_ref, out_ref):
    del order_ref
    copies, rows, lanes = out_ref.shape
    split = lanes - 128
    depth = got_ref.shape[0] // 2
    half = pl.ds(pl.multiple_of(lax.axis_index("core") * (copies * rows), 128), copies * rows)
    down = jnp.concatenate([pair_ref[0:depth, half], pair_ref[2 * depth : 3 * depth, half]], axis=0)
    up = jnp.concatenate([pair_ref[depth : 2 * depth, half], pair_ref[3 * depth :, half]], axis=0)
    terms = jnp.concatenate(
        [contract(down, got_ref[:, :split], 0, 0), contract(up, got_ref[:, split:], 0, 0)], axis=1
    )
    out_ref[...] = terms.astype(BF16).reshape(copies, rows, lanes)


def gather_body(parts_ref, order_ref, out_ref):
    del order_ref
    total = jnp.sum(parts_ref[...].astype(F32), axis=0).astype(BF16)
    out_ref[...] = jnp.broadcast_to(total[None], out_ref.shape)


def sums_body(hidden_ref, out_w_ref, embed_ref, mod_ref, sums_ref):
    copies, pieces, _ = mod_ref.shape
    latent, width = out_w_ref.shape
    tokens = hidden_ref.shape[0]
    halves = []
    for half in range(2):
        total = jnp.sum(mod_ref[copies // 2 * half : copies // 2 * (half + 1)].astype(F32), axis=0)
        halves.append(jnp.concatenate([total[p : p + 1] for p in range(pieces)], axis=1))
    shift, scale = halves
    hidden = hidden_ref[...]
    embed = embed_ref[...]
    out_w = out_w_ref[...].astype(F32)
    scaled = (out_w * (1.0 + scale)).astype(BF16)
    ones = jnp.ones((8, width), BF16)
    square = jnp.square(hidden.astype(F32))
    high = square.astype(BF16)
    low = (square - high.astype(F32)).astype(BF16)
    sums_ref[0:latent] = contract(scaled, hidden, 1, 1)
    gram = contract(embed, embed, 1, 1)
    fold = latent // 2
    sums_ref[latent : latent + fold] = jnp.concatenate([gram[:fold], gram[fold:]], axis=1)
    row = lax.broadcasted_iota(jnp.int32, (8, tokens), 0)
    firsts = contract(ones, hidden, 1, 1)
    squares = contract(ones, high, 1, 1) + contract(ones, low, 1, 1)
    pairs = jnp.concatenate([contract(ones, embed, 1, 1), contract(ones, scaled, 1, 1)], axis=1)
    shifted = contract(jnp.broadcast_to(shift, (8, width)), out_w, 1, 1, HIGHEST)
    shifted = jnp.concatenate([shifted, shifted], axis=1)
    sums_ref[latent + fold :] = jnp.where(
        row == 0, firsts, jnp.where(row == 1, squares, jnp.where(row == 2, pairs, shifted))
    )


def noise_body(time_ref, sums_ref, noise_ref, latents_ref, noised_ref, *, width):
    latent, tokens = noise_ref.shape
    base = latent + latent // 2
    mean = sums_ref[base : base + 1] / width
    var = sums_ref[base + 1 : base + 2] / width - mean * mean
    inv_std = lax.rsqrt(var + EPSILON)
    scaled_sum = sums_ref[base + 2 : base + 3, latent:]
    shifted_sum = sums_ref[base + 3 : base + 4, :latent]
    ones = jnp.ones((1, tokens), F32)
    centered = sums_ref[0:latent] - contract(scaled_sum, mean, 0, 0, HIGHEST)
    latents = inv_std * centered + contract(shifted_sum, ones, 0, 0, HIGHEST)
    latents = latents.astype(BF16)
    latents_ref[...] = latents
    level = level_of(time_ref)
    noised_ref[...] = (
        (1.0 - level) * latents.astype(F32) + level * noise_ref[...].astype(F32)
    ).astype(BF16)


def act_body(
    sums_ref,
    cross_noised_ref,
    pair_ref,
    weights_ref,
    cross_ref,
    out_ref,
    pre_ref,
    query_ref,
    side_ref,
    wide_ref,
    act_ref,
    *,
    width,
):
    latent, extent = wide_ref.shape
    tokens = extent // 3
    units = weights_ref.shape[0]
    copies, share, _ = out_ref.shape
    split = weights_ref.shape[1] - 128
    edge = cross_noised_ref[...]
    first = pair_ref[0:latent]
    second = pair_ref[latent:]
    noised_f = jnp.where(
        lax.axis_index("core") == 0,
        jnp.concatenate([edge, first, second], axis=1).astype(F32),
        jnp.concatenate([first, second, edge], axis=1).astype(F32),
    )
    noised = noised_f.astype(BF16)
    wide_ref[...] = noised
    base = latent + latent // 2
    center_row = sums_ref[base + 2 : base + 3, :latent] / width
    gram = jnp.concatenate([sums_ref[latent:base, :latent], sums_ref[latent:base, latent:]], axis=0)
    gram = gram - width * contract(center_row, center_row, 0, 0, HIGHEST)
    gram_noised = contract(gram, noised_f, 1, 0, HIGHEST)
    var = jnp.sum(noised_f * gram_noised, axis=0, keepdims=True) / width
    inv_std = lax.rsqrt(var + EPSILON)
    side_ref[0:latent] = gram_noised[:, tokens : 2 * tokens]
    side_ref[latent:] = jnp.broadcast_to(inv_std[:, tokens : 2 * tokens], (8, tokens))
    step = 128
    for begin in range(0, units, step):
        rows = slice(begin, begin + step)
        raw = weights_ref[rows, split : split + latent].astype(F32)
        gain = weights_ref[rows, split + latent : split + latent + 1].astype(F32)
        shift = weights_ref[rows, split + latent + 1 : split + latent + 2].astype(F32)
        query = (raw - gain * center_row).astype(BF16)
        query_ref[rows] = query
        pre = contract(query, noised, 1, 0) * inv_std + shift
        pre_ref[rows] = pre[:, tokens : 2 * tokens]
        act_ref[rows] = gelu_tanh(pre).astype(BF16)
    part = contract(weights_ref[:, :split], act_ref[...], 0, 0).astype(BF16)
    out_ref[:, :, :extent] = part.reshape(copies, share, extent)
    out_ref[:, :, extent:] = cross_ref[...]


def conv_body(
    parts_ref, wide_ref, taps_ref, pay_ref, back_ref, *, count
):
    _, share, _ = parts_ref.shape
    latent, extent = wide_ref.shape
    own = extent // 3
    channels = 2 * share
    noised = wide_ref[...]
    total = jnp.sum(parts_ref[...].astype(F32), axis=0)
    cross = jnp.concatenate(
        [total[:, extent : extent + latent], total[:, extent + latent :]], axis=0
    ).astype(BF16)
    embed = contract(cross, noised, 1, 0)
    field_in = jnp.concatenate([embed[:share] + total[:, :extent], embed[share:]], axis=0)
    lane = lax.broadcasted_iota(jnp.int32, (channels, extent), 1)
    at = seq_index()
    first = jnp.where(at == 0, own, 0)
    last = jnp.where(at == count - 1, 2 * own, extent)
    inside = (lane >= first) & (lane < last)
    column = lane % GRID_W
    left_ok = column > 0
    right_ok = column < GRID_W - 1

    def tap(row, col):
        place = 3 * row + col
        return taps_ref[:, place : place + 1]

    def convolve(grid, flip):
        before = jnp.where(left_ok, pltpu.roll(grid, 1, 1), 0.0)
        after = jnp.where(right_ok, pltpu.roll(grid, extent - 1, 1), 0.0)
        rows = []
        for row in range(3):
            if flip:
                rows.append(tap(row, 2) * before + tap(row, 1) * grid + tap(row, 0) * after)
            else:
                rows.append(tap(row, 0) * before + tap(row, 1) * grid + tap(row, 2) * after)
        if flip:
            rows = rows[::-1]
        return pltpu.roll(rows[0], GRID_W, 1) + rows[1] + pltpu.roll(rows[2], extent - GRID_W, 1)

    field = convolve(jnp.where(inside, field_in, 0.0), False)
    gating = jax.nn.sigmoid(field)
    scale = taps_ref[:, 9:10]
    terms = field * gating * scale
    slope = -scale * gating * (1.0 + field * (1.0 - gating))
    grad = convolve(jnp.where(inside, slope, 0.0), True)[:, own : 2 * own]
    block_sum = jnp.sum(terms[:share, own : 2 * own], axis=0, keepdims=True)
    embed_sum = jnp.sum(terms[share:, own : 2 * own], axis=0, keepdims=True)
    sums = jnp.concatenate([block_sum, embed_sum], axis=0)
    high = sums.astype(BF16).astype(F32)
    low = sums - high
    tail = jnp.concatenate([high, low, jnp.zeros((12, own), F32)], axis=0)
    pay = jnp.concatenate([grad[:share], tail], axis=0).astype(BF16)
    pay_ref[...] = jnp.broadcast_to(pay[None], pay_ref.shape)
    back_ref[...] = contract(cross, grad.astype(BF16), 0, 0)


def back_body(
    disc_ref,
    pay_ref,
    weights_ref,
    query_ref,
    pre_ref,
    side_ref,
    noised_ref,
    back_ref,
    out_ref,
    logits_ref,
    *,
    width,
):
    copies, rows, tokens = pay_ref.shape
    share = rows - 16
    latent = noised_ref.shape[0]
    split = copies * share
    grads = jnp.concatenate([pay_ref[copy, :share] for copy in range(copies)], axis=0)
    hidden_grad = contract(weights_ref[:, :split], grads, 1, 0)
    preact_grad = (hidden_grad * gelu_slope(pre_ref[...])).astype(BF16)
    query_grad = contract(query_ref[...], preact_grad, 0, 0)
    inv_std = side_ref[latent : latent + 1]
    along = jnp.sum(noised_ref[...].astype(F32) * query_grad, axis=0, keepdims=True)
    result = (
        inv_std * (query_grad - (inv_std * inv_std / width) * along * side_ref[0:latent])
        + back_ref[...]
    )
    out_ref[...] = jnp.broadcast_to(result.astype(BF16)[None], out_ref.shape)
    sums = []
    for place in range(2):
        total = jnp.zeros((16, tokens), F32)
        for copy in range(copies // 2 * place, copies // 2 * (place + 1)):
            total = total + pay_ref[copy, share:].astype(F32)
        sums.append(total[0:2] + total[2:4])
    block, other = pick_heads(disc_ref)
    for k in range(4):
        chosen = jnp.where(block[0] == k, 0, jnp.where(block[1] == k, 1, jnp.where(other[0] == k, 2, 3)))
        options = [sums[0][0:1], sums[1][0:1], sums[0][1:2], sums[1][1:2]]
        value = options[3]
        for place in range(3):
            value = jnp.where(chosen == place, options[place], value)
        logits_ref[k : k + 1] = value


def final_body(time_ref, parts_ref, latents_ref, logits_ref, out_ref, latents_out_ref, logits_out_ref):
    retain = 1.0 - level_of(time_ref)
    out_ref[...] = retain * jnp.sum(parts_ref[...].astype(F32), axis=0)
    latents_out_ref[...] = latents_ref[...]
    logits_out_ref[...] = logits_ref[...]


def per_device(
    student_hidden,
    student_cond,
    student_mod,
    student_out,
    timestep,
    noise,
    teacher_embed,
    teacher_mod,
    up_weight,
    down_weight,
    head_proj,
    head_kernel,
    head_out,
    disc_layer,
):
    groups = lax.axis_size("group")
    planes = lax.axis_size("plane")
    seqs = 2 * planes
    mps = lax.axis_size("mp")
    _, tokens, local_width = student_hidden.shape
    width = local_width * mps
    latent = teacher_embed.shape[0]
    units = down_weight.shape[0]
    channels = head_proj.shape[2]
    share = 2 * channels // mps
    lanes = 2 * channels + 128
    extent = 3 * tokens

    tmod = jnp.einsum(
        "sf,fjd->sjd",
        time_features(timestep, teacher_mod.shape[0]),
        teacher_mod.astype(F32),
        precision=HIGHEST,
    )[0]
    time_row = jnp.broadcast_to(timestep.astype(F32)[:, None], (8, tokens))
    ratio = seqs // mps
    rows = local_width // ratio
    pieces = local_width // 128
    sent, mods, cross, taps, noise_t = call(
        open_body,
        [
            ((rows, lanes), BF16),
            ((groups * seqs, pieces, 128), BF16),
            ((mps, share, 2 * latent), BF16),
            ((2 * share, 16), F32),
            ((latent, tokens), BF16),
        ],
        [disc_layer],
        [
            student_cond,
            student_mod[:, 0],
            tmod,
            teacher_embed,
            head_proj,
            jnp.transpose(head_kernel, (1, 2, 0, 3)).reshape(9, 4, channels),
            head_out,
        ],
        [
            ((local_width, 128), F32),
            ((channels, 16), F32),
            ((groups * seqs, pieces, 128), BF16),
        ],
        away=(1,),
        distant=[noise[0].T],
        plain=(0, 1, 3, 5, 6),
    )

    swap = [
        (at * mps + m, (ratio * m + at % ratio) * mps + at // ratio)
        for at in range(seqs)
        for m in range(mps)
    ]
    got = lax.ppermute(sent, SEQ + ("mp",), swap)

    mods = exchange(mods, ("group",) + SEQ)
    slices = jnp.concatenate([down_weight.T, up_weight], axis=0)
    slices = lax.all_gather(slices, "core", axis=0, tiled=True)
    got = lax.all_gather(got, "core", axis=0, tiled=True)
    (terms,) = call(weight_body, [((planes, units // seqs, lanes), BF16)], [], [got, slices, mods])
    terms = exchange(terms, "plane")
    (sums,) = call(
        sums_body,
        [((latent + latent // 2 + 8, tokens), F32)],
        [],
        [student_hidden[0], student_out.T, teacher_embed, mods],
    )
    stages = [sums]
    step = 1
    while step < mps:
        sums = sums + lax.ppermute(sums, "mp", [(i, i ^ step) for i in range(mps)])
        step *= 2
        stages.append(sums)
    halfway = stages[-2]
    (terms,) = call(gather_body, [((planes, units // seqs, lanes), BF16)], [], [terms, halfway])
    weights = exchange(terms, "plane").reshape(units // 2, lanes)
    weights = lax.all_gather(weights, "core", axis=0, tiled=True)

    latents, noised = call(
        functools.partial(noise_body, width=float(width)),
        [((latent, tokens), BF16), ((latent, tokens), BF16)],
        [],
        [time_row, sums, noise_t],
    )
    swap = [(i, i + 1 if i % 2 else i - 1) for i in range(1, seqs - 1)]
    edge = lax.ppermute(noised, SEQ, swap)
    pair = lax.all_gather(noised, "core", axis=0, tiled=True)

    parts, preact, query, side, wide = call(
        functools.partial(act_body, width=float(width)),
        [
            ((mps, share, extent + 2 * latent), BF16),
            ((units, tokens), F32),
            ((units, latent), BF16),
            ((latent + 8, tokens), F32),
            ((latent, extent), BF16),
        ],
        [],
        [sums, edge, pair, weights, cross],
        [((units, extent), BF16)],
    )
    parts = exchange(parts, "mp")
    pay, back = call(
        functools.partial(conv_body, count=seqs),
        [((mps, share + 16, tokens), BF16), ((latent, tokens), F32)],
        [],
        [parts, wide, taps],
    )
    pay = exchange(pay, "mp")
    back, logits = call(
        functools.partial(back_body, width=float(width)),
        [((mps, latent, tokens), BF16), ((4, tokens), F32)],
        [disc_layer],
        [pay, weights, query, preact, side, noised, back],
    )
    back = exchange(back, "mp")
    latent_grad, latents, logits = call(
        final_body,
        [((latent, tokens), F32), ((latent, tokens), BF16), ((4, tokens), F32)],
        [],
        [time_row, back, latents, logits],
        loose=(0, 1, 2),
    )
    return (latents.T[None], logits[None], latent_grad.T[None])


def solution(mesh):
    groups, seqs, mps = mesh.devices.shape
    split = Mesh(
        mesh.devices.reshape(groups, seqs // 2, 2, mps), ("group", "plane", "core", "mp")
    )
    return jax.shard_map(
        per_device,
        mesh=split,
        in_specs=(
            P("group", SEQ, "mp"),
            P(None, SEQ),
            P(SEQ, "group", "mp"),
            P("mp", None),
            P("group"),
            P("group", SEQ, None),
            P(None, "mp"),
            P(None, None, "mp"),
            P(SEQ, "mp"),
            P("mp", SEQ),
            P(None, "mp", None),
            P(),
            P(),
            P("group", None),
        ),
        out_specs=(P("group", SEQ, None), P("group", None, SEQ), P("group", SEQ, None)),
        check_vma=False,
    )
```

```python
import functools
import math

import jax
import jax.numpy as jnp
from jax import lax
from jax.experimental import pallas as pl
from jax.experimental.pallas import tpu as pltpu
from jax.sharding import Mesh
from jax.sharding import PartitionSpec as P


GRID_W = 64
EPSILON = 1e-06
GELU_COEF = 0.7978845608028654
INTERPRET = False

F32 = jnp.float32
BF16 = jnp.bfloat16
HIGHEST = lax.Precision.HIGHEST


def contract(left, right, left_dim, right_dim, precision=None):
    return lax.dot_general(
        left,
        right,
        (((left_dim,), (right_dim,)), ((), ())),
        precision=precision,
        preferred_element_type=F32,
    )


def gelu_tanh(values):
    inner = GELU_COEF * (values + 0.044715 * values * values * values)
    return 0.5 * values * (1.0 + jnp.tanh(inner))


def gelu_slope(values):
    inner = GELU_COEF * (values + 0.044715 * values * values * values)
    tangent = jnp.tanh(inner)
    return 0.5 * (1.0 + tangent) + 0.5 * values * (1.0 - tangent * tangent) * GELU_COEF * (
        1.0 + 3.0 * 0.044715 * values * values
    )


def time_features(timestep, width):
    half_width = width // 2
    index = jnp.arange(half_width, dtype=F32)
    freqs = jnp.exp(-math.log(10000.0) * index / half_width)
    angles = timestep.astype(F32)[:, None] * freqs[None, :]
    return jnp.concatenate([jnp.cos(angles), jnp.sin(angles)], axis=-1)


SEQ = ("plane", "core")


def seq_index():
    return lax.axis_index("plane") * 2 + lax.axis_index("core")


def exchange(value, axes):
    return lax.all_to_all(value, axes, 0, 0, tiled=False)


def call(body, outs, scalars, arrays, scratch=(), loose=(), distant=(), plain=(), away=()):
    smem = pl.BlockSpec(memory_space=pltpu.SMEM)
    vmem = pl.BlockSpec(memory_space=pltpu.VMEM)
    if INTERPRET:
        shapes = [jax.ShapeDtypeStruct(shape, dtype) for shape, dtype in outs]
    else:
        shapes = [
            jax.ShapeDtypeStruct(*out) if place in loose + away else pltpu.VMEM(*out)
            for place, out in enumerate(outs)
        ]
        arrays = [
            value if place in plain else pltpu.with_memory_space_constraint(value, pltpu.VMEM)
            for place, value in enumerate(arrays)
        ]
    return pl.pallas_call(
        body,
        in_specs=[smem] * len(scalars)
        + [vmem] * len(arrays)
        + [pl.BlockSpec(memory_space=pl.ANY)] * len(distant),
        out_specs=[
            pl.BlockSpec(memory_space=pl.ANY) if place in away else vmem for place in range(len(outs))
        ],
        out_shape=shapes,
        scratch_shapes=[pltpu.VMEM(shape, dtype) for shape, dtype in scratch]
        + [pltpu.SemaphoreType.DMA] * (len(distant) + len(away)),
        interpret=INTERPRET,
    )(*scalars, *arrays, *distant)


def pick_heads(disc_ref):
    picks = [disc_ref[0, k] for k in range(4)]
    pairs = []
    for layer in (1, 0):
        first = jnp.where(picks[0] == layer, 0, jnp.where(picks[1] == layer, 1, 2))
        last = jnp.where(picks[3] == layer, 3, jnp.where(picks[2] == layer, 2, 1))
        pairs.append((first, last))
    return pairs


def level_of(time_ref):
    return time_ref[0:1] / 1000.0


def open_body(
    disc_ref,
    cond_ref,
    mod_ref,
    tmod_ref,
    embed_ref,
    proj_ref,
    taps_in_ref,
    head_out_ref,
    noise_in_ref,
    sent_ref,
    mods_ref,
    cross_ref,
    taps_ref,
    noise_ref,
    queries_ref,
    turned_ref,
    terms_ref,
    noise_sem,
    terms_sem,
):
    fetch = pltpu.make_async_copy(noise_in_ref, noise_ref, noise_sem)
    fetch.start()
    block, other = pick_heads(disc_ref)
    channels = proj_ref.shape[2]
    latent, width = embed_ref.shape

    groups = cond_ref.shape[0]
    copies, pieces, lanes = mods_ref.shape
    seqs = copies // groups
    half = contract(cond_ref[...], mod_ref[...].astype(F32), 1, 0, HIGHEST)
    for group in range(groups):
        row = half[group : group + 1]
        pieces_of = jnp.concatenate(
            [row[:, lanes * p : lanes * (p + 1)] for p in range(pieces)], axis=0
        )
        terms_ref[seqs * group : seqs * (group + 1)] = jnp.broadcast_to(
            pieces_of.astype(BF16)[None], (seqs, pieces, lanes)
        )
    store = pltpu.make_async_copy(terms_ref, mods_ref, terms_sem)
    store.start()

    rows = sent_ref.shape[0]
    start = pl.multiple_of((seq_index() % (width // rows)) * rows, rows)
    embed = embed_ref[...]
    gain = 1.0 + tmod_ref[1:2]
    queries = jnp.concatenate(
        [
            embed.astype(F32) * gain,
            gain,
            tmod_ref[0:1],
            jnp.zeros((128 - latent - 2, width), F32),
        ],
        axis=0,
    )
    queries_ref[...] = queries.T
    sent_ref[:, 2 * channels :] = queries_ref[pl.ds(start, rows), :].astype(BF16)
    for place, head in enumerate(block):
        sent_ref[:, channels * place : channels * (place + 1)] = proj_ref[head, pl.ds(start, rows), :]

    _, share, pair_lanes = cross_ref.shape
    per_head = channels // share
    begin = lax.axis_index("mp") * share
    slot = begin // channels
    offset = pl.multiple_of(begin % channels, 8)
    for place in range(2):
        both = jnp.concatenate(
            [contract(proj_ref[head], embed, 0, 1) for head in (block[place], other[place])], axis=1
        )
        cross_ref[per_head * place : per_head * (place + 1)] = (
            both.astype(BF16).reshape(per_head, share, pair_lanes)
        )
    for place, pair in enumerate((block, other)):
        head = jnp.where(slot == 0, pair[0], pair[1])
        table = jnp.concatenate(
            [taps_in_ref[tap, pl.ds(head, 1), :] for tap in range(9)]
            + [head_out_ref[pl.ds(head, 1), :], jnp.zeros((6, channels), F32)],
            axis=0,
        )
        turned_ref[...] = table.T
        taps_ref[share * place : share * (place + 1)] = turned_ref[pl.ds(offset, share), :]
    store.wait()
    fetch.wait()


def weight_body(got_ref, pair_ref, order_ref, out_ref, *, latent):
    del order_ref
    copies, all_rows, lanes = out_ref.shape
    rows = all_rows - 8
    depth = got_ref.shape[0] // 2
    half = pl.ds(pl.multiple_of(lax.axis_index("core") * (copies * rows), 128), copies * rows)
    down = jnp.concatenate([pair_ref[0:depth, half], pair_ref[2 * depth : 3 * depth, half]], axis=0)
    up = jnp.concatenate([pair_ref[depth : 2 * depth, half], pair_ref[3 * depth :, half]], axis=0)
    value = contract(down, got_ref[:, :lanes], 0, 0)
    query = contract(up, got_ref[:, lanes:], 0, 0).reshape(copies, rows, 128)
    pieces = [query[:, 8 * fold : 8 * (fold + 1)] for fold in range(rows // 8)]
    tail = jnp.concatenate(
        [piece[:, :, :latent] for piece in pieces]
        + [piece[:, :, latent : latent + 2] for piece in pieces]
        + [jnp.zeros((copies, 8, lanes - len(pieces) * (latent + 2)), F32)],
        axis=2,
    )
    out_ref[:, :rows] = value.astype(BF16).reshape(copies, rows, lanes)
    out_ref[:, rows:] = tail.astype(BF16)


def gather_body(parts_ref, order_ref, out_ref):
    del order_ref
    total = jnp.sum(parts_ref[...].astype(F32), axis=0).astype(BF16)
    out_ref[...] = jnp.broadcast_to(total[None], out_ref.shape)


def sums_body(hidden_ref, out_w_ref, embed_ref, mod_ref, sums_ref):
    copies, pieces, _ = mod_ref.shape
    latent, width = out_w_ref.shape
    tokens = hidden_ref.shape[0]
    halves = []
    for half in range(2):
        total = jnp.sum(mod_ref[copies // 2 * half : copies // 2 * (half + 1)].astype(F32), axis=0)
        halves.append(jnp.concatenate([total[p : p + 1] for p in range(pieces)], axis=1))
    shift, scale = halves
    hidden = hidden_ref[...]
    embed = embed_ref[...]
    out_w = out_w_ref[...].astype(F32)
    scaled = (out_w * (1.0 + scale)).astype(BF16)
    ones = jnp.ones((8, width), BF16)
    square = jnp.square(hidden.astype(F32))
    high = square.astype(BF16)
    low = (square - high.astype(F32)).astype(BF16)
    sums_ref[0:latent] = contract(scaled, hidden, 1, 1)
    gram = contract(embed, embed, 1, 1)
    fold = latent // 2
    sums_ref[latent : latent + fold] = jnp.concatenate([gram[:fold], gram[fold:]], axis=1)
    row = lax.broadcasted_iota(jnp.int32, (8, tokens), 0)
    firsts = contract(ones, hidden, 1, 1)
    squares = contract(ones, high, 1, 1) + contract(ones, low, 1, 1)
    pairs = jnp.concatenate([contract(ones, embed, 1, 1), contract(ones, scaled, 1, 1)], axis=1)
    shifted = contract(jnp.broadcast_to(shift, (8, width)), out_w, 1, 1, HIGHEST)
    shifted = jnp.concatenate([shifted, shifted], axis=1)
    sums_ref[latent + fold :] = jnp.where(
        row == 0, firsts, jnp.where(row == 1, squares, jnp.where(row == 2, pairs, shifted))
    )


def noise_body(time_ref, sums_ref, noise_ref, latents_ref, noised_ref, *, width):
    latent, tokens = noise_ref.shape
    base = latent + latent // 2
    mean = sums_ref[base : base + 1] / width
    var = sums_ref[base + 1 : base + 2] / width - mean * mean
    inv_std = lax.rsqrt(jnp.maximum(var, 0.0) + EPSILON)
    scaled_sum = sums_ref[base + 2 : base + 3, latent:]
    shifted_sum = sums_ref[base + 3 : base + 4, :latent]
    ones = jnp.ones((1, tokens), F32)
    centered = sums_ref[0:latent] - contract(scaled_sum, mean, 0, 0, HIGHEST)
    latents = inv_std * centered + contract(shifted_sum, ones, 0, 0, HIGHEST)
    latents = latents.astype(BF16)
    latents_ref[...] = latents
    level = level_of(time_ref)
    noised_ref[...] = (
        (1.0 - level) * latents.astype(F32) + level * noise_ref[...].astype(F32)
    ).astype(BF16)


def act_body(
    sums_ref,
    cross_noised_ref,
    pair_ref,
    weights_ref,
    cross_ref,
    out_ref,
    pre_ref,
    query_ref,
    side_ref,
    wide_ref,
    values_ref,
    act_ref,
    *,
    width,
):
    latent, extent = wide_ref.shape
    tokens = extent // 3
    chunks, all_rows, split = weights_ref.shape
    unit_rows = all_rows - 8
    copies, share, _ = out_ref.shape
    edge = cross_noised_ref[...]
    first = pair_ref[0:latent]
    second = pair_ref[latent:]
    noised_f = jnp.where(
        lax.axis_index("core") == 0,
        jnp.concatenate([edge, first, second], axis=1).astype(F32),
        jnp.concatenate([first, second, edge], axis=1).astype(F32),
    )
    noised = noised_f.astype(BF16)
    wide_ref[...] = noised
    base = latent + latent // 2
    center_row = sums_ref[base + 2 : base + 3, :latent] / width
    gram = jnp.concatenate([sums_ref[latent:base, :latent], sums_ref[latent:base, latent:]], axis=0)
    gram = gram - width * contract(center_row, center_row, 0, 0, HIGHEST)
    gram_noised = contract(gram, noised_f, 1, 0, HIGHEST)
    var = jnp.sum(noised_f * gram_noised, axis=0, keepdims=True) / width
    inv_std = lax.rsqrt(jnp.maximum(var, 0.0) + EPSILON)
    side_ref[0:latent] = gram_noised[:, tokens : 2 * tokens]
    side_ref[latent:] = jnp.broadcast_to(inv_std[:, tokens : 2 * tokens], (8, tokens))
    folds = unit_rows // 8
    base = folds * latent
    step = 4
    for begin in range(0, chunks, step):
        rows = slice(begin * unit_rows, (begin + step) * unit_rows)
        tail = weights_ref[begin : begin + step, unit_rows:].astype(F32)

        def unfold(start, stride, size):
            parts = [tail[:, :, start + stride * f : start + stride * f + size] for f in range(folds)]
            return jnp.concatenate(parts, axis=1).reshape(step * unit_rows, size)

        query = (unfold(0, latent, latent) - unfold(base, 2, 1) * center_row).astype(BF16)
        query_ref[rows] = query
        pre = contract(query, noised, 1, 0) * inv_std + unfold(base + 1, 2, 1)
        pre_ref[rows] = pre[:, tokens : 2 * tokens]
        act_ref[rows] = gelu_tanh(pre).astype(BF16)
        values_ref[rows] = weights_ref[begin : begin + step, :unit_rows].reshape(
            step * unit_rows, split
        )
    part = contract(values_ref[...], act_ref[...], 0, 0).astype(BF16)
    out_ref[:, :, :extent] = part.reshape(copies, share, extent)
    out_ref[:, :, extent:] = cross_ref[...]


def conv_body(
    parts_ref, wide_ref, taps_ref, pay_ref, back_ref, *, count
):
    _, share, _ = parts_ref.shape
    latent, extent = wide_ref.shape
    own = extent // 3
    channels = 2 * share
    noised = wide_ref[...]
    total = jnp.sum(parts_ref[...].astype(F32), axis=0)
    cross = jnp.concatenate(
        [total[:, extent : extent + latent], total[:, extent + latent :]], axis=0
    ).astype(BF16)
    embed = contract(cross, noised, 1, 0)
    field_in = jnp.concatenate([embed[:share] + total[:, :extent], embed[share:]], axis=0)
    lane = lax.broadcasted_iota(jnp.int32, (channels, extent), 1)
    at = seq_index()
    first = jnp.where(at == 0, own, 0)
    last = jnp.where(at == count - 1, 2 * own, extent)
    inside = (lane >= first) & (lane < last)
    column = lane % GRID_W
    left_ok = column > 0
    right_ok = column < GRID_W - 1

    def tap(row, col):
        place = 3 * row + col
        return taps_ref[:, place : place + 1]

    def convolve(grid, flip):
        before = jnp.where(left_ok, pltpu.roll(grid, 1, 1), 0.0)
        after = jnp.where(right_ok, pltpu.roll(grid, extent - 1, 1), 0.0)
        rows = []
        for row in range(3):
            if flip:
                rows.append(tap(row, 2) * before + tap(row, 1) * grid + tap(row, 0) * after)
            else:
                rows.append(tap(row, 0) * before + tap(row, 1) * grid + tap(row, 2) * after)
        if flip:
            rows = rows[::-1]
        return pltpu.roll(rows[0], GRID_W, 1) + rows[1] + pltpu.roll(rows[2], extent - GRID_W, 1)

    field = convolve(jnp.where(inside, field_in, 0.0), False)
    gating = jax.nn.sigmoid(field)
    scale = taps_ref[:, 9:10]
    terms = field * gating * scale
    slope = -scale * gating * (1.0 + field * (1.0 - gating))
    grad = convolve(jnp.where(inside, slope, 0.0), True)[:, own : 2 * own]
    block_sum = jnp.sum(terms[:share, own : 2 * own], axis=0, keepdims=True)
    embed_sum = jnp.sum(terms[share:, own : 2 * own], axis=0, keepdims=True)
    sums = jnp.concatenate([block_sum, embed_sum], axis=0)
    high = sums.astype(BF16).astype(F32)
    low = sums - high
    tail = jnp.concatenate([high, low, jnp.zeros((12, own), F32)], axis=0)
    pay = jnp.concatenate([grad[:share], tail], axis=0).astype(BF16)
    pay_ref[...] = jnp.broadcast_to(pay[None], pay_ref.shape)
    back_ref[...] = contract(cross, grad.astype(BF16), 0, 0)


def back_body(
    disc_ref,
    pay_ref,
    values_ref,
    query_ref,
    pre_ref,
    side_ref,
    noised_ref,
    back_ref,
    out_ref,
    logits_ref,
    *,
    width,
):
    copies, rows, tokens = pay_ref.shape
    share = rows - 16
    latent = noised_ref.shape[0]
    grads = jnp.concatenate([pay_ref[copy, :share] for copy in range(copies)], axis=0)
    hidden_grad = contract(values_ref[...], grads, 1, 0)
    preact_grad = (hidden_grad * gelu_slope(pre_ref[...])).astype(BF16)
    query_grad = contract(query_ref[...], preact_grad, 0, 0)
    inv_std = side_ref[latent : latent + 1]
    along = jnp.sum(noised_ref[...].astype(F32) * query_grad, axis=0, keepdims=True)
    result = (
        inv_std * (query_grad - (inv_std * inv_std / width) * along * side_ref[0:latent])
        + back_ref[...]
    )
    out_ref[...] = jnp.broadcast_to(result.astype(BF16)[None], out_ref.shape)
    sums = []
    for place in range(2):
        total = jnp.zeros((16, tokens), F32)
        for copy in range(copies // 2 * place, copies // 2 * (place + 1)):
            total = total + pay_ref[copy, share:].astype(F32)
        sums.append(total[0:2] + total[2:4])
    block, other = pick_heads(disc_ref)
    for k in range(4):
        chosen = jnp.where(block[0] == k, 0, jnp.where(block[1] == k, 1, jnp.where(other[0] == k, 2, 3)))
        options = [sums[0][0:1], sums[1][0:1], sums[0][1:2], sums[1][1:2]]
        value = options[3]
        for place in range(3):
            value = jnp.where(chosen == place, options[place], value)
        logits_ref[k : k + 1] = value


def final_body(time_ref, parts_ref, latents_ref, logits_ref, out_ref, latents_out_ref, logits_out_ref):
    retain = 1.0 - level_of(time_ref)
    out_ref[...] = retain * jnp.sum(parts_ref[...].astype(F32), axis=0)
    latents_out_ref[...] = latents_ref[...]
    logits_out_ref[...] = logits_ref[...]


def per_device(
    student_hidden,
    student_cond,
    student_mod,
    student_out,
    timestep,
    noise,
    teacher_embed,
    teacher_mod,
    up_weight,
    down_weight,
    head_proj,
    head_kernel,
    head_out,
    disc_layer,
):
    groups = lax.axis_size("group")
    planes = lax.axis_size("plane")
    seqs = 2 * planes
    mps = lax.axis_size("mp")
    _, tokens, local_width = student_hidden.shape
    width = local_width * mps
    latent = teacher_embed.shape[0]
    units = down_weight.shape[0]
    channels = head_proj.shape[2]
    share = 2 * channels // mps
    lanes = 2 * channels + 128
    extent = 3 * tokens

    tmod = jnp.einsum(
        "sf,fjd->sjd",
        time_features(timestep, teacher_mod.shape[0]),
        teacher_mod.astype(F32),
        precision=HIGHEST,
    )[0]
    time_row = jnp.broadcast_to(timestep.astype(F32)[:, None], (8, tokens))
    ratio = seqs // mps
    rows = local_width // ratio
    pieces = local_width // 128
    sent, mods, cross, taps, noise_t = call(
        open_body,
        [
            ((rows, lanes), BF16),
            ((groups * seqs, pieces, 128), BF16),
            ((mps, share, 2 * latent), BF16),
            ((2 * share, 16), F32),
            ((latent, tokens), BF16),
        ],
        [disc_layer],
        [
            student_cond,
            student_mod[:, 0],
            tmod,
            teacher_embed,
            head_proj,
            jnp.transpose(head_kernel, (1, 2, 0, 3)).reshape(9, 4, channels),
            head_out,
        ],
        [
            ((local_width, 128), F32),
            ((channels, 16), F32),
            ((groups * seqs, pieces, 128), BF16),
        ],
        away=(1,),
        distant=[noise[0].T],
        plain=(0, 1, 3, 5, 6),
    )

    swap = [
        (at * mps + m, (ratio * m + at % ratio) * mps + at // ratio)
        for at in range(seqs)
        for m in range(mps)
    ]
    got = lax.ppermute(sent, SEQ + ("mp",), swap)

    mods = exchange(mods, ("group",) + SEQ)
    slices = jnp.concatenate([down_weight.T, up_weight], axis=0)
    slices = lax.all_gather(slices, "core", axis=0, tiled=True)
    got = lax.all_gather(got, "core", axis=0, tiled=True)
    (terms,) = call(
        functools.partial(weight_body, latent=latent),
        [((planes, units // seqs + 8, 2 * channels), BF16)],
        [],
        [got, slices, mods],
    )
    terms = exchange(terms, "plane")
    (sums,) = call(
        sums_body,
        [((latent + latent // 2 + 8, tokens), F32)],
        [],
        [student_hidden[0], student_out.T, teacher_embed, mods],
    )
    stages = [sums]
    step = 1
    while step < mps:
        sums = sums + lax.ppermute(sums, "mp", [(i, i ^ step) for i in range(mps)])
        step *= 2
        stages.append(sums)
    halfway = stages[-2]
    (terms,) = call(gather_body, [((planes, units // seqs + 8, 2 * channels), BF16)], [], [terms, halfway])
    weights = exchange(terms, "plane")
    weights = lax.all_gather(weights, "core", axis=0, tiled=True)

    latents, noised = call(
        functools.partial(noise_body, width=float(width)),
        [((latent, tokens), BF16), ((latent, tokens), BF16)],
        [],
        [time_row, sums, noise_t],
    )
    swap = [(i, i + 1 if i % 2 else i - 1) for i in range(1, seqs - 1)]
    edge = lax.ppermute(noised, SEQ, swap)
    pair = lax.all_gather(noised, "core", axis=0, tiled=True)

    parts, preact, query, side, wide, values = call(
        functools.partial(act_body, width=float(width)),
        [
            ((mps, share, extent + 2 * latent), BF16),
            ((units, tokens), F32),
            ((units, latent), BF16),
            ((latent + 8, tokens), F32),
            ((latent, extent), BF16),
            ((units, 2 * channels), BF16),
        ],
        [],
        [sums, edge, pair, weights, cross],
        [((units, extent), BF16)],
    )
    parts = exchange(parts, "mp")
    pay, back = call(
        functools.partial(conv_body, count=seqs),
        [((mps, share + 16, tokens), BF16), ((latent, tokens), F32)],
        [],
        [parts, wide, taps],
    )
    pay = exchange(pay, "mp")
    back, logits = call(
        functools.partial(back_body, width=float(width)),
        [((mps, latent, tokens), BF16), ((4, tokens), F32)],
        [disc_layer],
        [pay, values, query, preact, side, noised, back],
    )
    back = exchange(back, "mp")
    latent_grad, latents, logits = call(
        final_body,
        [((latent, tokens), F32), ((latent, tokens), BF16), ((4, tokens), F32)],
        [],
        [time_row, back, latents, logits],
        loose=(0, 1, 2),
    )
    return (latents.T[None], logits[None], latent_grad.T[None])


def solution(mesh):
    groups, seqs, mps = mesh.devices.shape
    split = Mesh(
        mesh.devices.reshape(groups, seqs // 2, 2, mps), ("group", "plane", "core", "mp")
    )
    return jax.shard_map(
        per_device,
        mesh=split,
        in_specs=(
            P("group", SEQ, "mp"),
            P(None, SEQ),
            P(SEQ, "group", "mp"),
            P("mp", None),
            P("group"),
            P("group", SEQ, None),
            P(None, "mp"),
            P(None, None, "mp"),
            P(SEQ, "mp"),
            P("mp", SEQ),
            P(None, "mp", None),
            P(),
            P(),
            P("group", None),
        ),
        out_specs=(P("group", SEQ, None), P("group", None, SEQ), P("group", SEQ, None)),
        check_vma=False,
    )
```

```python
import functools
import math

import jax
import jax.numpy as jnp
from jax import lax
from jax.experimental import pallas as pl
from jax.experimental.pallas import tpu as pltpu
from jax.sharding import Mesh
from jax.sharding import PartitionSpec as P


GRID_W = 64
EPSILON = 1e-06
GELU_COEF = 0.7978845608028654
INTERPRET = False

F32 = jnp.float32
BF16 = jnp.bfloat16
HIGHEST = lax.Precision.HIGHEST


def contract(left, right, left_dim, right_dim, precision=None):
    return lax.dot_general(
        left,
        right,
        (((left_dim,), (right_dim,)), ((), ())),
        precision=precision,
        preferred_element_type=F32,
    )


def gelu_tanh(values):
    inner = GELU_COEF * (values + 0.044715 * values * values * values)
    return 0.5 * values * (1.0 + jnp.tanh(inner))


def gelu_slope(values):
    inner = GELU_COEF * (values + 0.044715 * values * values * values)
    tangent = jnp.tanh(inner)
    return 0.5 * (1.0 + tangent) + 0.5 * values * (1.0 - tangent * tangent) * GELU_COEF * (
        1.0 + 3.0 * 0.044715 * values * values
    )


def time_features(timestep, width):
    half_width = width // 2
    index = jnp.arange(half_width, dtype=F32)
    freqs = jnp.exp(-math.log(10000.0) * index / half_width)
    angles = timestep.astype(F32)[:, None] * freqs[None, :]
    return jnp.concatenate([jnp.cos(angles), jnp.sin(angles)], axis=-1)


SEQ = ("plane", "core")


def seq_index():
    return lax.axis_index("plane") * 2 + lax.axis_index("core")


def exchange(value, axes):
    return lax.all_to_all(value, axes, 0, 0, tiled=False)


def call(body, outs, scalars, arrays, scratch=(), loose=(), distant=(), plain=(), away=()):
    smem = pl.BlockSpec(memory_space=pltpu.SMEM)
    vmem = pl.BlockSpec(memory_space=pltpu.VMEM)
    if INTERPRET:
        shapes = [jax.ShapeDtypeStruct(shape, dtype) for shape, dtype in outs]
    else:
        shapes = [
            jax.ShapeDtypeStruct(*out) if place in loose + away else pltpu.VMEM(*out)
            for place, out in enumerate(outs)
        ]
        arrays = [
            value if place in plain else pltpu.with_memory_space_constraint(value, pltpu.VMEM)
            for place, value in enumerate(arrays)
        ]
    return pl.pallas_call(
        body,
        in_specs=[smem] * len(scalars)
        + [vmem] * len(arrays)
        + [pl.BlockSpec(memory_space=pl.ANY)] * len(distant),
        out_specs=[
            pl.BlockSpec(memory_space=pl.ANY) if place in away else vmem for place in range(len(outs))
        ],
        out_shape=shapes,
        scratch_shapes=[pltpu.VMEM(shape, dtype) for shape, dtype in scratch]
        + [pltpu.SemaphoreType.DMA] * (len(distant) + len(away)),
        interpret=INTERPRET,
    )(*scalars, *arrays, *distant)


def pick_heads(disc_ref):
    picks = [disc_ref[0, k] for k in range(4)]
    pairs = []
    for layer in (1, 0):
        first = jnp.where(picks[0] == layer, 0, jnp.where(picks[1] == layer, 1, 2))
        last = jnp.where(picks[3] == layer, 3, jnp.where(picks[2] == layer, 2, 1))
        pairs.append((first, last))
    return pairs


def level_of(time_ref):
    return time_ref[0:1] / 1000.0


def open_body(
    disc_ref,
    cond_ref,
    mod_ref,
    tmod_ref,
    embed_ref,
    proj_ref,
    taps_in_ref,
    head_out_ref,
    noise_in_ref,
    sent_ref,
    mods_ref,
    cross_ref,
    taps_ref,
    noise_ref,
    queries_ref,
    turned_ref,
    terms_ref,
    noise_sem,
    terms_sem,
):
    fetch = pltpu.make_async_copy(noise_in_ref, noise_ref, noise_sem)
    fetch.start()
    block, other = pick_heads(disc_ref)
    channels = proj_ref.shape[2]
    latent, width = embed_ref.shape

    groups = cond_ref.shape[0]
    copies, pieces, lanes = mods_ref.shape
    seqs = copies // groups
    half = contract(cond_ref[...], mod_ref[...].astype(F32), 1, 0, HIGHEST)
    for group in range(groups):
        row = half[group : group + 1]
        pieces_of = jnp.concatenate(
            [row[:, lanes * p : lanes * (p + 1)] for p in range(pieces)], axis=0
        )
        terms_ref[seqs * group : seqs * (group + 1)] = jnp.broadcast_to(
            pieces_of.astype(BF16)[None], (seqs, pieces, lanes)
        )
    store = pltpu.make_async_copy(terms_ref, mods_ref, terms_sem)
    store.start()

    rows = sent_ref.shape[0]
    start = pl.multiple_of((lax.axis_index("plane") % (width // rows)) * rows, rows)
    embed = embed_ref[...]
    gain = 1.0 + tmod_ref[1:2]
    queries = jnp.concatenate(
        [
            embed.astype(F32) * gain,
            gain,
            tmod_ref[0:1],
            jnp.zeros((128 - latent - 2, width), F32),
        ],
        axis=0,
    )
    queries_ref[...] = queries.T
    sent_ref[:, 2 * channels :] = queries_ref[pl.ds(start, rows), :].astype(BF16)
    for place, head in enumerate(block):
        sent_ref[:, channels * place : channels * (place + 1)] = proj_ref[head, pl.ds(start, rows), :]

    _, share, pair_lanes = cross_ref.shape
    per_head = channels // share
    begin = lax.axis_index("mp") * share
    slot = begin // channels
    offset = pl.multiple_of(begin % channels, 8)
    for place in range(2):
        both = jnp.concatenate(
            [contract(proj_ref[head], embed, 0, 1) for head in (block[place], other[place])], axis=1
        )
        cross_ref[per_head * place : per_head * (place + 1)] = (
            both.astype(BF16).reshape(per_head, share, pair_lanes)
        )
    for place, pair in enumerate((block, other)):
        head = jnp.where(slot == 0, pair[0], pair[1])
        table = jnp.concatenate(
            [taps_in_ref[tap, pl.ds(head, 1), :] for tap in range(9)]
            + [head_out_ref[pl.ds(head, 1), :], jnp.zeros((6, channels), F32)],
            axis=0,
        )
        turned_ref[...] = table.T
        taps_ref[share * place : share * (place + 1)] = turned_ref[pl.ds(offset, share), :]
    store.wait()
    fetch.wait()


def weight_body(got_ref, pair_ref, order_ref, out_ref, *, latent):
    del order_ref
    copies, all_rows, lanes = out_ref.shape
    rows = all_rows - 8
    depth = got_ref.shape[0] // 2
    half = pl.ds(pl.multiple_of(lax.axis_index("core") * (copies * rows), 128), copies * rows)
    down = jnp.concatenate([pair_ref[0:depth, half], pair_ref[2 * depth : 3 * depth, half]], axis=0)
    up = jnp.concatenate([pair_ref[depth : 2 * depth, half], pair_ref[3 * depth :, half]], axis=0)
    value = contract(down, got_ref[:, :lanes], 0, 0)
    query = contract(up, got_ref[:, lanes:], 0, 0).reshape(copies, rows, 128)
    pieces = [query[:, 8 * fold : 8 * (fold + 1)] for fold in range(rows // 8)]
    tail = jnp.concatenate(
        [piece[:, :, :latent] for piece in pieces]
        + [piece[:, :, latent : latent + 2] for piece in pieces]
        + [jnp.zeros((copies, 8, lanes - len(pieces) * (latent + 2)), F32)],
        axis=2,
    )
    out_ref[:, :rows] = value.astype(BF16).reshape(copies, rows, lanes)
    out_ref[:, rows:] = tail.astype(BF16)


def gather_body(parts_ref, order_ref, out_ref):
    del order_ref
    total = jnp.sum(parts_ref[...].astype(F32), axis=0).astype(BF16)
    out_ref[...] = jnp.broadcast_to(total[None], out_ref.shape)


def sums_body(hidden_ref, out_w_ref, embed_ref, mod_ref, sums_ref):
    copies, pieces, _ = mod_ref.shape
    latent, width = out_w_ref.shape
    tokens = hidden_ref.shape[0]
    halves = []
    for half in range(2):
        total = jnp.sum(mod_ref[copies // 2 * half : copies // 2 * (half + 1)].astype(F32), axis=0)
        halves.append(jnp.concatenate([total[p : p + 1] for p in range(pieces)], axis=1))
    shift, scale = halves
    hidden = hidden_ref[...]
    embed = embed_ref[...]
    out_w = out_w_ref[...].astype(F32)
    scaled = (out_w * (1.0 + scale)).astype(BF16)
    ones = jnp.ones((8, width), BF16)
    square = jnp.square(hidden.astype(F32))
    high = square.astype(BF16)
    low = (square - high.astype(F32)).astype(BF16)
    sums_ref[0:latent] = contract(scaled, hidden, 1, 1)
    gram = contract(embed, embed, 1, 1)
    fold = latent // 2
    sums_ref[latent : latent + fold] = jnp.concatenate([gram[:fold], gram[fold:]], axis=1)
    row = lax.broadcasted_iota(jnp.int32, (8, tokens), 0)
    firsts = contract(ones, hidden, 1, 1)
    squares = contract(ones, high, 1, 1) + contract(ones, low, 1, 1)
    pairs = jnp.concatenate([contract(ones, embed, 1, 1), contract(ones, scaled, 1, 1)], axis=1)
    shifted = contract(jnp.broadcast_to(shift, (8, width)), out_w, 1, 1, HIGHEST)
    shifted = jnp.concatenate([shifted, shifted], axis=1)
    sums_ref[latent + fold :] = jnp.where(
        row == 0, firsts, jnp.where(row == 1, squares, jnp.where(row == 2, pairs, shifted))
    )


def noise_body(time_ref, sums_ref, noise_ref, latents_ref, noised_ref, *, width):
    latent, tokens = noise_ref.shape
    base = latent + latent // 2
    mean = sums_ref[base : base + 1] / width
    var = sums_ref[base + 1 : base + 2] / width - mean * mean
    inv_std = lax.rsqrt(jnp.maximum(var, 0.0) + EPSILON)
    scaled_sum = sums_ref[base + 2 : base + 3, latent:]
    shifted_sum = sums_ref[base + 3 : base + 4, :latent]
    ones = jnp.ones((1, tokens), F32)
    centered = sums_ref[0:latent] - contract(scaled_sum, mean, 0, 0, HIGHEST)
    latents = inv_std * centered + contract(shifted_sum, ones, 0, 0, HIGHEST)
    latents = latents.astype(BF16)
    latents_ref[...] = latents
    level = level_of(time_ref)
    noised_ref[...] = (
        (1.0 - level) * latents.astype(F32) + level * noise_ref[...].astype(F32)
    ).astype(BF16)


def act_body(
    sums_ref,
    cross_noised_ref,
    pair_ref,
    weights_ref,
    cross_ref,
    out_ref,
    pre_ref,
    query_ref,
    side_ref,
    wide_ref,
    values_ref,
    act_ref,
    *,
    width,
):
    latent, extent = wide_ref.shape
    tokens = extent // 3
    chunks, all_rows, split = weights_ref.shape
    unit_rows = all_rows - 8
    copies, share, _ = out_ref.shape
    edge = cross_noised_ref[...]
    first = pair_ref[0:latent]
    second = pair_ref[latent:]
    noised_f = jnp.where(
        lax.axis_index("core") == 0,
        jnp.concatenate([edge, first, second], axis=1).astype(F32),
        jnp.concatenate([first, second, edge], axis=1).astype(F32),
    )
    noised = noised_f.astype(BF16)
    wide_ref[...] = noised
    base = latent + latent // 2
    center_row = sums_ref[base + 2 : base + 3, :latent] / width
    gram = jnp.concatenate([sums_ref[latent:base, :latent], sums_ref[latent:base, latent:]], axis=0)
    gram = gram - width * contract(center_row, center_row, 0, 0, HIGHEST)
    gram_noised = contract(gram, noised_f, 1, 0, HIGHEST)
    var = jnp.sum(noised_f * gram_noised, axis=0, keepdims=True) / width
    inv_std = lax.rsqrt(jnp.maximum(var, 0.0) + EPSILON)
    side_ref[0:latent] = gram_noised[:, tokens : 2 * tokens]
    side_ref[latent:] = jnp.broadcast_to(inv_std[:, tokens : 2 * tokens], (8, tokens))
    folds = unit_rows // 8
    base = folds * latent
    step = 4
    for begin in range(0, chunks, step):
        rows = slice(begin * unit_rows, (begin + step) * unit_rows)
        tail = weights_ref[begin : begin + step, unit_rows:].astype(F32)

        def unfold(start, stride, size):
            parts = [tail[:, :, start + stride * f : start + stride * f + size] for f in range(folds)]
            return jnp.concatenate(parts, axis=1).reshape(step * unit_rows, size)

        query = (unfold(0, latent, latent) - unfold(base, 2, 1) * center_row).astype(BF16)
        query_ref[rows] = query
        pre = contract(query, noised, 1, 0) * inv_std + unfold(base + 1, 2, 1)
        pre_ref[rows] = pre[:, tokens : 2 * tokens]
        act_ref[rows] = gelu_tanh(pre).astype(BF16)
        values_ref[rows] = weights_ref[begin : begin + step, :unit_rows].reshape(
            step * unit_rows, split
        )
    part = contract(values_ref[...], act_ref[...], 0, 0).astype(BF16)
    out_ref[:, :, :extent] = part.reshape(copies, share, extent)
    out_ref[:, :, extent:] = cross_ref[...]


def conv_body(
    parts_ref, wide_ref, taps_ref, pay_ref, back_ref, *, count
):
    _, share, _ = parts_ref.shape
    latent, extent = wide_ref.shape
    own = extent // 3
    channels = 2 * share
    noised = wide_ref[...]
    total = jnp.sum(parts_ref[...].astype(F32), axis=0)
    cross = jnp.concatenate(
        [total[:, extent : extent + latent], total[:, extent + latent :]], axis=0
    ).astype(BF16)
    embed = contract(cross, noised, 1, 0)
    field_in = jnp.concatenate([embed[:share] + total[:, :extent], embed[share:]], axis=0)
    lane = lax.broadcasted_iota(jnp.int32, (channels, extent), 1)
    at = seq_index()
    first = jnp.where(at == 0, own, 0)
    last = jnp.where(at == count - 1, 2 * own, extent)
    inside = (lane >= first) & (lane < last)
    column = lane % GRID_W
    left_ok = column > 0
    right_ok = column < GRID_W - 1

    def tap(row, col):
        place = 3 * row + col
        return taps_ref[:, place : place + 1]

    def convolve(grid, flip):
        before = jnp.where(left_ok, pltpu.roll(grid, 1, 1), 0.0)
        after = jnp.where(right_ok, pltpu.roll(grid, extent - 1, 1), 0.0)
        rows = []
        for row in range(3):
            if flip:
                rows.append(tap(row, 2) * before + tap(row, 1) * grid + tap(row, 0) * after)
            else:
                rows.append(tap(row, 0) * before + tap(row, 1) * grid + tap(row, 2) * after)
        if flip:
            rows = rows[::-1]
        return pltpu.roll(rows[0], GRID_W, 1) + rows[1] + pltpu.roll(rows[2], extent - GRID_W, 1)

    field = convolve(jnp.where(inside, field_in, 0.0), False)
    gating = jax.nn.sigmoid(field)
    scale = taps_ref[:, 9:10]
    terms = field * gating * scale
    slope = -scale * gating * (1.0 + field * (1.0 - gating))
    grad = convolve(jnp.where(inside, slope, 0.0), True)[:, own : 2 * own]
    block_sum = jnp.sum(terms[:share, own : 2 * own], axis=0, keepdims=True)
    embed_sum = jnp.sum(terms[share:, own : 2 * own], axis=0, keepdims=True)
    sums = jnp.concatenate([block_sum, embed_sum], axis=0)
    high = sums.astype(BF16).astype(F32)
    low = sums - high
    tail = jnp.concatenate([high, low, jnp.zeros((12, own), F32)], axis=0)
    pay = jnp.concatenate([grad[:share], tail], axis=0).astype(BF16)
    pay_ref[...] = jnp.broadcast_to(pay[None], pay_ref.shape)
    back_ref[...] = contract(cross, grad.astype(BF16), 0, 0)


def back_body(
    disc_ref,
    pay_ref,
    values_ref,
    query_ref,
    pre_ref,
    side_ref,
    noised_ref,
    back_ref,
    out_ref,
    logits_ref,
    *,
    width,
):
    copies, rows, tokens = pay_ref.shape
    share = rows - 16
    latent = noised_ref.shape[0]
    grads = jnp.concatenate([pay_ref[copy, :share] for copy in range(copies)], axis=0)
    hidden_grad = contract(values_ref[...], grads, 1, 0)
    preact_grad = (hidden_grad * gelu_slope(pre_ref[...])).astype(BF16)
    query_grad = contract(query_ref[...], preact_grad, 0, 0)
    inv_std = side_ref[latent : latent + 1]
    along = jnp.sum(noised_ref[...].astype(F32) * query_grad, axis=0, keepdims=True)
    result = (
        inv_std * (query_grad - (inv_std * inv_std / width) * along * side_ref[0:latent])
        + back_ref[...]
    )
    out_ref[...] = jnp.broadcast_to(result.astype(BF16)[None], out_ref.shape)
    sums = []
    for place in range(2):
        total = jnp.zeros((16, tokens), F32)
        for copy in range(copies // 2 * place, copies // 2 * (place + 1)):
            total = total + pay_ref[copy, share:].astype(F32)
        sums.append(total[0:2] + total[2:4])
    block, other = pick_heads(disc_ref)
    for k in range(4):
        chosen = jnp.where(block[0] == k, 0, jnp.where(block[1] == k, 1, jnp.where(other[0] == k, 2, 3)))
        options = [sums[0][0:1], sums[1][0:1], sums[0][1:2], sums[1][1:2]]
        value = options[3]
        for place in range(3):
            value = jnp.where(chosen == place, options[place], value)
        logits_ref[k : k + 1] = value


def final_body(time_ref, parts_ref, latents_ref, logits_ref, out_ref, latents_out_ref, logits_out_ref):
    retain = 1.0 - level_of(time_ref)
    out_ref[...] = retain * jnp.sum(parts_ref[...].astype(F32), axis=0)
    latents_out_ref[...] = latents_ref[...]
    logits_out_ref[...] = logits_ref[...]


def per_device(
    student_hidden,
    student_cond,
    student_mod,
    student_out,
    timestep,
    noise,
    teacher_embed,
    teacher_mod,
    up_weight,
    down_weight,
    head_proj,
    head_kernel,
    head_out,
    disc_layer,
):
    groups = lax.axis_size("group")
    planes = lax.axis_size("plane")
    seqs = 2 * planes
    mps = lax.axis_size("mp")
    _, tokens, local_width = student_hidden.shape
    width = local_width * mps
    latent = teacher_embed.shape[0]
    units = down_weight.shape[0]
    channels = head_proj.shape[2]
    share = 2 * channels // mps
    lanes = 2 * channels + 128
    extent = 3 * tokens

    tmod = jnp.einsum(
        "sf,fjd->sjd",
        time_features(timestep, teacher_mod.shape[0]),
        teacher_mod.astype(F32),
        precision=HIGHEST,
    )[0]
    time_row = jnp.broadcast_to(timestep.astype(F32)[:, None], (8, tokens))
    ratio = seqs // mps
    rows = 2 * local_width // ratio
    pieces = local_width // 128
    sent, mods, cross, taps, noise_t = call(
        open_body,
        [
            ((rows, lanes), BF16),
            ((groups * seqs, pieces, 128), BF16),
            ((mps, share, 2 * latent), BF16),
            ((2 * share, 16), F32),
            ((latent, tokens), BF16),
        ],
        [disc_layer],
        [
            student_cond,
            student_mod[:, 0],
            tmod,
            teacher_embed,
            head_proj,
            jnp.transpose(head_kernel, (1, 2, 0, 3)).reshape(9, 4, channels),
            head_out,
        ],
        [
            ((local_width, 128), F32),
            ((channels, 16), F32),
            ((groups * seqs, pieces, 128), BF16),
        ],
        away=(1,),
        distant=[noise[0].T],
        plain=(0, 1, 3, 5, 6),
    )

    swap = [
        (at * mps + m, (ratio * m + at % ratio) * mps + at // ratio)
        for at in range(seqs)
        for m in range(mps)
    ]
    got = lax.ppermute(sent, SEQ + ("mp",), swap)

    mods = exchange(mods, ("group",) + SEQ)
    slices = jnp.concatenate([down_weight.T, up_weight], axis=0)
    slices = lax.all_gather(slices, "core", axis=0, tiled=True)
    (terms,) = call(
        functools.partial(weight_body, latent=latent),
        [((planes, units // seqs + 8, 2 * channels), BF16)],
        [],
        [got, slices, mods],
    )
    terms = exchange(terms, "plane")
    (sums,) = call(
        sums_body,
        [((latent + latent // 2 + 8, tokens), F32)],
        [],
        [student_hidden[0], student_out.T, teacher_embed, mods],
    )
    stages = [sums]
    step = 1
    while step < mps:
        sums = sums + lax.ppermute(sums, "mp", [(i, i ^ step) for i in range(mps)])
        step *= 2
        stages.append(sums)
    halfway = stages[-2]
    (terms,) = call(gather_body, [((planes, units // seqs + 8, 2 * channels), BF16)], [], [terms, halfway])
    weights = exchange(terms, "plane")
    weights = lax.all_gather(weights, "core", axis=0, tiled=True)

    latents, noised = call(
        functools.partial(noise_body, width=float(width)),
        [((latent, tokens), BF16), ((latent, tokens), BF16)],
        [],
        [time_row, sums, noise_t],
    )
    swap = [(i, i + 1 if i % 2 else i - 1) for i in range(1, seqs - 1)]
    edge = lax.ppermute(noised, SEQ, swap)
    pair = lax.all_gather(noised, "core", axis=0, tiled=True)

    parts, preact, query, side, wide, values = call(
        functools.partial(act_body, width=float(width)),
        [
            ((mps, share, extent + 2 * latent), BF16),
            ((units, tokens), F32),
            ((units, latent), BF16),
            ((latent + 8, tokens), F32),
            ((latent, extent), BF16),
            ((units, 2 * channels), BF16),
        ],
        [],
        [sums, edge, pair, weights, cross],
        [((units, extent), BF16)],
    )
    parts = exchange(parts, "mp")
    pay, back = call(
        functools.partial(conv_body, count=seqs),
        [((mps, share + 16, tokens), BF16), ((latent, tokens), F32)],
        [],
        [parts, wide, taps],
    )
    pay = exchange(pay, "mp")
    back, logits = call(
        functools.partial(back_body, width=float(width)),
        [((mps, latent, tokens), BF16), ((4, tokens), F32)],
        [disc_layer],
        [pay, values, query, preact, side, noised, back],
    )
    back = exchange(back, "mp")
    latent_grad, latents, logits = call(
        final_body,
        [((latent, tokens), F32), ((latent, tokens), BF16), ((4, tokens), F32)],
        [],
        [time_row, back, latents, logits],
        loose=(0, 1, 2),
    )
    return (latents.T[None], logits[None], latent_grad.T[None])


def solution(mesh):
    groups, seqs, mps = mesh.devices.shape
    split = Mesh(
        mesh.devices.reshape(groups, seqs // 2, 2, mps), ("group", "plane", "core", "mp")
    )
    return jax.shard_map(
        per_device,
        mesh=split,
        in_specs=(
            P("group", SEQ, "mp"),
            P(None, SEQ),
            P(SEQ, "group", "mp"),
            P("mp", None),
            P("group"),
            P("group", SEQ, None),
            P(None, "mp"),
            P(None, None, "mp"),
            P(SEQ, "mp"),
            P("mp", SEQ),
            P(None, "mp", None),
            P(),
            P(),
            P("group", None),
        ),
        out_specs=(P("group", SEQ, None), P("group", None, SEQ), P("group", SEQ, None)),
        check_vma=False,
    )
```

```python
import functools
import math

import jax
import jax.numpy as jnp
from jax import lax
from jax.experimental import pallas as pl
from jax.experimental.pallas import tpu as pltpu
from jax.sharding import Mesh
from jax.sharding import PartitionSpec as P


GRID_W = 64
EPSILON = 1e-06
GELU_COEF = 0.7978845608028654
INTERPRET = False

F32 = jnp.float32
BF16 = jnp.bfloat16
HIGHEST = lax.Precision.HIGHEST


def contract(left, right, left_dim, right_dim, precision=None):
    return lax.dot_general(
        left,
        right,
        (((left_dim,), (right_dim,)), ((), ())),
        precision=precision,
        preferred_element_type=F32,
    )


def gelu_tanh(values):
    inner = GELU_COEF * (values + 0.044715 * values * values * values)
    return 0.5 * values * (1.0 + jnp.tanh(inner))


def gelu_slope(values):
    inner = GELU_COEF * (values + 0.044715 * values * values * values)
    tangent = jnp.tanh(inner)
    return 0.5 * (1.0 + tangent) + 0.5 * values * (1.0 - tangent * tangent) * GELU_COEF * (
        1.0 + 3.0 * 0.044715 * values * values
    )


def time_features(timestep, width):
    half_width = width // 2
    index = jnp.arange(half_width, dtype=F32)
    freqs = jnp.exp(-math.log(10000.0) * index / half_width)
    angles = timestep.astype(F32)[:, None] * freqs[None, :]
    return jnp.concatenate([jnp.cos(angles), jnp.sin(angles)], axis=-1)


SEQ = ("plane", "core")


def seq_index():
    return lax.axis_index("plane") * 2 + lax.axis_index("core")


def exchange(value, axes):
    return lax.all_to_all(value, axes, 0, 0, tiled=False)


def call(body, outs, scalars, arrays, scratch=(), loose=(), distant=(), plain=(), away=()):
    smem = pl.BlockSpec(memory_space=pltpu.SMEM)
    vmem = pl.BlockSpec(memory_space=pltpu.VMEM)
    if INTERPRET:
        shapes = [jax.ShapeDtypeStruct(shape, dtype) for shape, dtype in outs]
    else:
        shapes = [
            jax.ShapeDtypeStruct(*out) if place in loose + away else pltpu.VMEM(*out)
            for place, out in enumerate(outs)
        ]
        arrays = [
            value if place in plain else pltpu.with_memory_space_constraint(value, pltpu.VMEM)
            for place, value in enumerate(arrays)
        ]
    return pl.pallas_call(
        body,
        in_specs=[smem] * len(scalars)
        + [vmem] * len(arrays)
        + [pl.BlockSpec(memory_space=pl.ANY)] * len(distant),
        out_specs=[
            pl.BlockSpec(memory_space=pl.ANY) if place in away else vmem for place in range(len(outs))
        ],
        out_shape=shapes,
        scratch_shapes=[pltpu.VMEM(shape, dtype) for shape, dtype in scratch]
        + [pltpu.SemaphoreType.DMA] * (len(distant) + len(away)),
        interpret=INTERPRET,
    )(*scalars, *arrays, *distant)


def pick_heads(disc_ref):
    picks = [disc_ref[0, k] for k in range(4)]
    pairs = []
    for layer in (1, 0):
        first = jnp.where(picks[0] == layer, 0, jnp.where(picks[1] == layer, 1, 2))
        last = jnp.where(picks[3] == layer, 3, jnp.where(picks[2] == layer, 2, 1))
        pairs.append((first, last))
    return pairs


def level_of(time_ref):
    return time_ref[0:1] / 1000.0


def open_body(
    disc_ref,
    cond_ref,
    mod_ref,
    tmod_ref,
    embed_ref,
    proj_ref,
    taps_in_ref,
    head_out_ref,
    noise_in_ref,
    sent_ref,
    mods_ref,
    cross_ref,
    taps_ref,
    noise_ref,
    queries_ref,
    turned_ref,
    terms_ref,
    noise_sem,
    terms_sem,
):
    fetch = pltpu.make_async_copy(noise_in_ref, noise_ref, noise_sem)
    fetch.start()
    block, other = pick_heads(disc_ref)
    channels = proj_ref.shape[2]
    latent, width = embed_ref.shape

    groups = cond_ref.shape[0]
    copies, pieces, lanes = mods_ref.shape
    seqs = copies // groups
    half = contract(cond_ref[...], mod_ref[...].astype(F32), 1, 0, HIGHEST)
    for group in range(groups):
        row = half[group : group + 1]
        pieces_of = jnp.concatenate(
            [row[:, lanes * p : lanes * (p + 1)] for p in range(pieces)], axis=0
        )
        terms_ref[seqs * group : seqs * (group + 1)] = jnp.broadcast_to(
            pieces_of.astype(BF16)[None], (seqs, pieces, lanes)
        )
    store = pltpu.make_async_copy(terms_ref, mods_ref, terms_sem)
    store.start()

    rows = sent_ref.shape[0]
    start = pl.multiple_of((lax.axis_index("plane") % (width // rows)) * rows, rows)
    embed = embed_ref[...]
    gain = 1.0 + tmod_ref[1:2]
    queries = jnp.concatenate(
        [
            embed.astype(F32) * gain,
            gain,
            tmod_ref[0:1],
            jnp.zeros((128 - latent - 2, width), F32),
        ],
        axis=0,
    )
    queries_ref[...] = queries.T
    sent_ref[:, 2 * channels :] = queries_ref[pl.ds(start, rows), :].astype(BF16)
    for place, head in enumerate(block):
        sent_ref[:, channels * place : channels * (place + 1)] = proj_ref[head, pl.ds(start, rows), :]

    _, share, pair_lanes = cross_ref.shape
    per_head = channels // share
    begin = lax.axis_index("mp") * share
    slot = begin // channels
    offset = pl.multiple_of(begin % channels, 8)
    for place in range(2):
        both = jnp.concatenate(
            [contract(proj_ref[head], embed, 0, 1) for head in (block[place], other[place])], axis=1
        )
        cross_ref[per_head * place : per_head * (place + 1)] = (
            both.astype(BF16).reshape(per_head, share, pair_lanes)
        )
    for place, pair in enumerate((block, other)):
        head = jnp.where(slot == 0, pair[0], pair[1])
        table = jnp.concatenate(
            [taps_in_ref[tap, pl.ds(head, 1), :] for tap in range(9)]
            + [head_out_ref[pl.ds(head, 1), :], jnp.zeros((6, channels), F32)],
            axis=0,
        )
        turned_ref[...] = table.T
        taps_ref[share * place : share * (place + 1)] = turned_ref[pl.ds(offset, share), :]
    store.wait()
    fetch.wait()


def weight_body(got_ref, pair_ref, order_ref, out_ref, *, latent):
    del order_ref
    copies, all_rows, lanes = out_ref.shape
    rows = all_rows - 8
    depth = got_ref.shape[0] // 2
    half = pl.ds(pl.multiple_of(lax.axis_index("core") * (copies * rows), 128), copies * rows)
    down = jnp.concatenate([pair_ref[0:depth, half], pair_ref[2 * depth : 3 * depth, half]], axis=0)
    up = jnp.concatenate([pair_ref[depth : 2 * depth, half], pair_ref[3 * depth :, half]], axis=0)
    value = contract(down, got_ref[:, :lanes], 0, 0)
    query = contract(up, got_ref[:, lanes:], 0, 0).reshape(copies, rows, 128)
    pieces = [query[:, 8 * fold : 8 * (fold + 1)] for fold in range(rows // 8)]
    tail = jnp.concatenate(
        [piece[:, :, :latent] for piece in pieces]
        + [piece[:, :, latent : latent + 2] for piece in pieces]
        + [jnp.zeros((copies, 8, lanes - len(pieces) * (latent + 2)), F32)],
        axis=2,
    )
    out_ref[:, :rows] = value.astype(BF16).reshape(copies, rows, lanes)
    out_ref[:, rows:] = tail.astype(BF16)


def gather_body(parts_ref, order_ref, out_ref):
    del order_ref
    total = jnp.sum(parts_ref[...].astype(F32), axis=0).astype(BF16)
    out_ref[...] = jnp.broadcast_to(total[None], out_ref.shape)


def sums_body(hidden_ref, out_w_ref, embed_ref, mod_ref, sums_ref):
    copies, pieces, _ = mod_ref.shape
    latent, width = out_w_ref.shape
    tokens = hidden_ref.shape[0]
    halves = []
    for half in range(2):
        total = jnp.sum(mod_ref[copies // 2 * half : copies // 2 * (half + 1)].astype(F32), axis=0)
        halves.append(jnp.concatenate([total[p : p + 1] for p in range(pieces)], axis=1))
    shift, scale = halves
    hidden = hidden_ref[...]
    embed = embed_ref[...]
    out_w = out_w_ref[...].astype(F32)
    scaled = (out_w * (1.0 + scale)).astype(BF16)
    ones = jnp.ones((8, width), BF16)
    square = jnp.square(hidden.astype(F32))
    high = square.astype(BF16)
    low = (square - high.astype(F32)).astype(BF16)
    sums_ref[0:latent] = contract(scaled, hidden, 1, 1)
    gram = contract(embed, embed, 1, 1)
    fold = latent // 2
    sums_ref[latent : latent + fold] = jnp.concatenate([gram[:fold], gram[fold:]], axis=1)
    row = lax.broadcasted_iota(jnp.int32, (8, tokens), 0)
    firsts = contract(ones, hidden, 1, 1)
    squares = contract(ones, high, 1, 1) + contract(ones, low, 1, 1)
    pairs = jnp.concatenate([contract(ones, embed, 1, 1), contract(ones, scaled, 1, 1)], axis=1)
    shifted = contract(jnp.broadcast_to(shift, (8, width)), out_w, 1, 1, HIGHEST)
    shifted = jnp.concatenate([shifted, shifted], axis=1)
    sums_ref[latent + fold :] = jnp.where(
        row == 0, firsts, jnp.where(row == 1, squares, jnp.where(row == 2, pairs, shifted))
    )


def noise_body(time_ref, sums_ref, noise_ref, latents_ref, noised_ref, *, width):
    latent, tokens = noise_ref.shape
    base = latent + latent // 2
    mean = sums_ref[base : base + 1] / width
    var = sums_ref[base + 1 : base + 2] / width - mean * mean
    inv_std = lax.rsqrt(jnp.maximum(var, 0.0) + EPSILON)
    scaled_sum = sums_ref[base + 2 : base + 3, latent:]
    shifted_sum = sums_ref[base + 3 : base + 4, :latent]
    ones = jnp.ones((1, tokens), F32)
    centered = sums_ref[0:latent] - contract(scaled_sum, mean, 0, 0, HIGHEST)
    latents = inv_std * centered + contract(shifted_sum, ones, 0, 0, HIGHEST)
    latents = latents.astype(BF16)
    latents_ref[...] = latents
    level = level_of(time_ref)
    noised_ref[...] = (
        (1.0 - level) * latents.astype(F32) + level * noise_ref[...].astype(F32)
    ).astype(BF16)


def act_body(
    sums_ref,
    cross_noised_ref,
    pair_ref,
    weights_ref,
    cross_ref,
    out_ref,
    pre_ref,
    query_ref,
    side_ref,
    wide_ref,
    values_ref,
    act_ref,
    *,
    width,
):
    latent, extent = wide_ref.shape
    tokens = extent // 3
    chunks, all_rows, split = weights_ref.shape
    unit_rows = all_rows - 8
    copies, share, _ = out_ref.shape
    edge = cross_noised_ref[...]
    first = pair_ref[0:latent]
    second = pair_ref[latent:]
    noised_f = jnp.where(
        lax.axis_index("core") == 0,
        jnp.concatenate([edge, first, second], axis=1).astype(F32),
        jnp.concatenate([first, second, edge], axis=1).astype(F32),
    )
    noised = noised_f.astype(BF16)
    wide_ref[...] = noised
    base = latent + latent // 2
    center_row = sums_ref[base + 2 : base + 3, :latent] / width
    gram = jnp.concatenate([sums_ref[latent:base, :latent], sums_ref[latent:base, latent:]], axis=0)
    gram = gram - width * contract(center_row, center_row, 0, 0, HIGHEST)
    gram_noised = contract(gram, noised_f, 1, 0, HIGHEST)
    var = jnp.sum(noised_f * gram_noised, axis=0, keepdims=True) / width
    inv_std = lax.rsqrt(jnp.maximum(var, 0.0) + EPSILON)
    side_ref[0:latent] = gram_noised[:, tokens : 2 * tokens]
    side_ref[latent:] = jnp.broadcast_to(inv_std[:, tokens : 2 * tokens], (8, tokens))
    folds = unit_rows // 8
    base = folds * latent
    step = 4
    for begin in range(0, chunks, step):
        rows = slice(begin * unit_rows, (begin + step) * unit_rows)
        tail = weights_ref[begin : begin + step, unit_rows:].astype(F32)

        def unfold(start, stride, size):
            parts = [tail[:, :, start + stride * f : start + stride * f + size] for f in range(folds)]
            return jnp.concatenate(parts, axis=1).reshape(step * unit_rows, size)

        query = (unfold(0, latent, latent) - unfold(base, 2, 1) * center_row).astype(BF16)
        query_ref[rows] = query
        pre = contract(query, noised, 1, 0) * inv_std + unfold(base + 1, 2, 1)
        pre_ref[rows] = pre[:, tokens : 2 * tokens]
        act_ref[rows] = gelu_tanh(pre).astype(BF16)
        values_ref[rows] = weights_ref[begin : begin + step, :unit_rows].reshape(
            step * unit_rows, split
        )
    part = contract(values_ref[...], act_ref[...], 0, 0).astype(BF16)
    out_ref[:, :, :extent] = part.reshape(copies, share, extent)
    out_ref[:, :, extent:] = cross_ref[...]


def conv_body(
    parts_ref, wide_ref, taps_ref, pay_ref, back_ref, *, count
):
    _, share, _ = parts_ref.shape
    latent, extent = wide_ref.shape
    own = extent // 3
    channels = 2 * share
    noised = wide_ref[...]
    total = jnp.sum(parts_ref[...].astype(F32), axis=0)
    cross = jnp.concatenate(
        [total[:, extent : extent + latent], total[:, extent + latent :]], axis=0
    ).astype(BF16)
    embed = contract(cross, noised, 1, 0)
    field_in = jnp.concatenate([embed[:share] + total[:, :extent], embed[share:]], axis=0)
    lane = lax.broadcasted_iota(jnp.int32, (channels, extent), 1)
    at = seq_index()
    first = jnp.where(at == 0, own, 0)
    last = jnp.where(at == count - 1, 2 * own, extent)
    inside = (lane >= first) & (lane < last)
    column = lane % GRID_W
    left_ok = column > 0
    right_ok = column < GRID_W - 1

    def tap(row, col):
        place = 3 * row + col
        return taps_ref[:, place : place + 1]

    def convolve(grid, flip):
        before = jnp.where(left_ok, pltpu.roll(grid, 1, 1), 0.0)
        after = jnp.where(right_ok, pltpu.roll(grid, extent - 1, 1), 0.0)
        rows = []
        for row in range(3):
            if flip:
                rows.append(tap(row, 2) * before + tap(row, 1) * grid + tap(row, 0) * after)
            else:
                rows.append(tap(row, 0) * before + tap(row, 1) * grid + tap(row, 2) * after)
        if flip:
            rows = rows[::-1]
        return pltpu.roll(rows[0], GRID_W, 1) + rows[1] + pltpu.roll(rows[2], extent - GRID_W, 1)

    field = convolve(jnp.where(inside, field_in, 0.0), False)
    gating = jax.nn.sigmoid(field)
    scale = taps_ref[:, 9:10]
    terms = field * gating * scale
    slope = -scale * gating * (1.0 + field * (1.0 - gating))
    grad = convolve(jnp.where(inside, slope, 0.0), True)[:, own : 2 * own]
    block_sum = jnp.sum(terms[:share, own : 2 * own], axis=0, keepdims=True)
    embed_sum = jnp.sum(terms[share:, own : 2 * own], axis=0, keepdims=True)
    sums = jnp.concatenate([block_sum, embed_sum], axis=0)
    high = sums.astype(BF16).astype(F32)
    low = sums - high
    tail = jnp.concatenate([high, low, jnp.zeros((12, own), F32)], axis=0)
    pay = jnp.concatenate([grad[:share], tail], axis=0).astype(BF16)
    pay_ref[...] = jnp.broadcast_to(pay[None], pay_ref.shape)
    back_ref[...] = contract(cross, grad.astype(BF16), 0, 0)


def back_body(
    disc_ref,
    pay_ref,
    values_ref,
    query_ref,
    pre_ref,
    side_ref,
    noised_ref,
    back_ref,
    out_ref,
    logits_ref,
    *,
    width,
):
    copies, rows, tokens = pay_ref.shape
    share = rows - 16
    latent = noised_ref.shape[0]
    grads = jnp.concatenate([pay_ref[copy, :share] for copy in range(copies)], axis=0)
    hidden_grad = contract(values_ref[...], grads, 1, 0)
    preact_grad = (hidden_grad * gelu_slope(pre_ref[...])).astype(BF16)
    query_grad = contract(query_ref[...], preact_grad, 0, 0)
    inv_std = side_ref[latent : latent + 1]
    along = jnp.sum(noised_ref[...].astype(F32) * query_grad, axis=0, keepdims=True)
    result = (
        inv_std * (query_grad - (inv_std * inv_std / width) * along * side_ref[0:latent])
        + back_ref[...]
    )
    out_ref[...] = jnp.broadcast_to(result.astype(BF16)[None], out_ref.shape)
    sums = []
    for place in range(2):
        total = jnp.zeros((16, tokens), F32)
        for copy in range(copies // 2 * place, copies // 2 * (place + 1)):
            total = total + pay_ref[copy, share:].astype(F32)
        sums.append(total[0:2] + total[2:4])
    block, other = pick_heads(disc_ref)
    for k in range(4):
        chosen = jnp.where(block[0] == k, 0, jnp.where(block[1] == k, 1, jnp.where(other[0] == k, 2, 3)))
        options = [sums[0][0:1], sums[1][0:1], sums[0][1:2], sums[1][1:2]]
        value = options[3]
        for place in range(3):
            value = jnp.where(chosen == place, options[place], value)
        logits_ref[k : k + 1] = value


def final_body(time_ref, parts_ref, latents_ref, logits_ref, out_ref, latents_out_ref, logits_out_ref):
    retain = 1.0 - level_of(time_ref)
    out_ref[...] = retain * jnp.sum(parts_ref[...].astype(F32), axis=0)
    latents_out_ref[...] = latents_ref[...]
    logits_out_ref[...] = logits_ref[...]


def per_device(
    student_hidden,
    student_cond,
    student_mod,
    student_out,
    timestep,
    noise,
    teacher_embed,
    teacher_mod,
    up_weight,
    down_weight,
    head_proj,
    head_kernel,
    head_out,
    disc_layer,
):
    groups = lax.axis_size("group")
    planes = lax.axis_size("plane")
    seqs = 2 * planes
    mps = lax.axis_size("mp")
    _, tokens, local_width = student_hidden.shape
    width = local_width * mps
    latent = teacher_embed.shape[0]
    units = down_weight.shape[0]
    channels = head_proj.shape[2]
    share = 2 * channels // mps
    lanes = 2 * channels + 128
    extent = 3 * tokens

    tmod = jnp.einsum(
        "sf,fjd->sjd",
        time_features(timestep, teacher_mod.shape[0]),
        teacher_mod.astype(F32),
        precision=HIGHEST,
    )[0]
    time_row = jnp.broadcast_to(timestep.astype(F32)[:, None], (8, tokens))
    ratio = seqs // mps
    rows = 2 * local_width // ratio
    pieces = local_width // 128
    sent, mods, cross, taps, noise_t = call(
        open_body,
        [
            ((rows, lanes), BF16),
            ((groups * seqs, pieces, 128), BF16),
            ((mps, share, 2 * latent), BF16),
            ((2 * share, 16), F32),
            ((latent, tokens), BF16),
        ],
        [disc_layer],
        [
            student_cond,
            student_mod[:, 0],
            tmod,
            teacher_embed,
            head_proj,
            jnp.transpose(head_kernel, (1, 2, 0, 3)).reshape(9, 4, channels),
            head_out,
        ],
        [
            ((local_width, 128), F32),
            ((channels, 16), F32),
            ((groups * seqs, pieces, 128), BF16),
        ],
        away=(1,),
        distant=[noise[0].T],
        plain=(0, 1, 3, 5, 6),
    )

    swap = [
        (at * mps + m, (ratio * m + at % ratio) * mps + at // ratio)
        for at in range(seqs)
        for m in range(mps)
    ]
    got = lax.ppermute(sent, SEQ + ("mp",), swap)

    mods = exchange(mods, ("group",) + SEQ)
    slices = jnp.concatenate([down_weight.T, up_weight], axis=0)
    slices = lax.all_gather(slices, "core", axis=0, tiled=True)
    (terms,) = call(
        functools.partial(weight_body, latent=latent),
        [((planes, units // seqs + 8, 2 * channels), BF16)],
        [],
        [got, slices, mods],
    )
    terms = exchange(terms, "plane")
    (sums,) = call(
        sums_body,
        [((latent + latent // 2 + 8, tokens), F32)],
        [],
        [student_hidden[0], student_out.T, teacher_embed, mods],
    )
    stages = [sums]
    hops = [1 << bit for bit in range(mps.bit_length() - 1)]
    hops[:2] = hops[:2][::-1]
    for hop in hops:
        sums = sums + lax.ppermute(sums, "mp", [(i, i ^ hop) for i in range(mps)])
        stages.append(sums)
    halfway = stages[-2]
    (terms,) = call(gather_body, [((planes, units // seqs + 8, 2 * channels), BF16)], [], [terms, halfway])
    weights = exchange(terms, "plane")
    weights = lax.all_gather(weights, "core", axis=0, tiled=True)

    latents, noised = call(
        functools.partial(noise_body, width=float(width)),
        [((latent, tokens), BF16), ((latent, tokens), BF16)],
        [],
        [time_row, sums, noise_t],
    )
    swap = [(i, i + 1 if i % 2 else i - 1) for i in range(1, seqs - 1)]
    edge = lax.ppermute(noised, SEQ, swap)
    pair = lax.all_gather(noised, "core", axis=0, tiled=True)

    parts, preact, query, side, wide, values = call(
        functools.partial(act_body, width=float(width)),
        [
            ((mps, share, extent + 2 * latent), BF16),
            ((units, tokens), F32),
            ((units, latent), BF16),
            ((latent + 8, tokens), F32),
            ((latent, extent), BF16),
            ((units, 2 * channels), BF16),
        ],
        [],
        [sums, edge, pair, weights, cross],
        [((units, extent), BF16)],
    )
    parts = exchange(parts, "mp")
    pay, back = call(
        functools.partial(conv_body, count=seqs),
        [((mps, share + 16, tokens), BF16), ((latent, tokens), F32)],
        [],
        [parts, wide, taps],
    )
    pay = exchange(pay, "mp")
    back, logits = call(
        functools.partial(back_body, width=float(width)),
        [((mps, latent, tokens), BF16), ((4, tokens), F32)],
        [disc_layer],
        [pay, values, query, preact, side, noised, back],
    )
    back = exchange(back, "mp")
    latent_grad, latents, logits = call(
        final_body,
        [((latent, tokens), F32), ((latent, tokens), BF16), ((4, tokens), F32)],
        [],
        [time_row, back, latents, logits],
        loose=(0, 1, 2),
    )
    return (latents.T[None], logits[None], latent_grad.T[None])


def solution(mesh):
    groups, seqs, mps = mesh.devices.shape
    split = Mesh(
        mesh.devices.reshape(groups, seqs // 2, 2, mps), ("group", "plane", "core", "mp")
    )
    return jax.shard_map(
        per_device,
        mesh=split,
        in_specs=(
            P("group", SEQ, "mp"),
            P(None, SEQ),
            P(SEQ, "group", "mp"),
            P("mp", None),
            P("group"),
            P("group", SEQ, None),
            P(None, "mp"),
            P(None, None, "mp"),
            P(SEQ, "mp"),
            P("mp", SEQ),
            P(None, "mp", None),
            P(),
            P(),
            P("group", None),
        ),
        out_specs=(P("group", SEQ, None), P("group", None, SEQ), P("group", SEQ, None)),
        check_vma=False,
    )
```

```python
import functools
import math

import jax
import jax.numpy as jnp
from jax import lax
from jax.experimental import pallas as pl
from jax.experimental.pallas import tpu as pltpu
from jax.sharding import Mesh
from jax.sharding import PartitionSpec as P


GRID_W = 64
EPSILON = 1e-06
GELU_COEF = 0.7978845608028654
INTERPRET = False

F32 = jnp.float32
BF16 = jnp.bfloat16
HIGHEST = lax.Precision.HIGHEST


def contract(left, right, left_dim, right_dim, precision=None):
    return lax.dot_general(
        left,
        right,
        (((left_dim,), (right_dim,)), ((), ())),
        precision=precision,
        preferred_element_type=F32,
    )


def gelu_tanh(values):
    inner = GELU_COEF * (values + 0.044715 * values * values * values)
    return 0.5 * values * (1.0 + jnp.tanh(inner))


def gelu_slope(values):
    inner = GELU_COEF * (values + 0.044715 * values * values * values)
    tangent = jnp.tanh(inner)
    return 0.5 * (1.0 + tangent) + 0.5 * values * (1.0 - tangent * tangent) * GELU_COEF * (
        1.0 + 3.0 * 0.044715 * values * values
    )


def time_features(timestep, width):
    half_width = width // 2
    index = jnp.arange(half_width, dtype=F32)
    freqs = jnp.exp(-math.log(10000.0) * index / half_width)
    angles = timestep.astype(F32) * freqs[None, :]
    return jnp.concatenate([jnp.cos(angles), jnp.sin(angles)], axis=-1)


SEQ = ("plane", "core")


def seq_index():
    return lax.axis_index("plane") * 2 + lax.axis_index("core")


def exchange(value, axes):
    return lax.all_to_all(value, axes, 0, 0, tiled=False)


def call(body, outs, scalars, arrays, scratch=(), loose=(), distant=(), plain=(), away=()):
    smem = pl.BlockSpec(memory_space=pltpu.SMEM)
    vmem = pl.BlockSpec(memory_space=pltpu.VMEM)
    if INTERPRET:
        shapes = [jax.ShapeDtypeStruct(shape, dtype) for shape, dtype in outs]
    else:
        shapes = [
            jax.ShapeDtypeStruct(*out) if place in loose + away else pltpu.VMEM(*out)
            for place, out in enumerate(outs)
        ]
        arrays = [
            value if place in plain else pltpu.with_memory_space_constraint(value, pltpu.VMEM)
            for place, value in enumerate(arrays)
        ]
    return pl.pallas_call(
        body,
        in_specs=[smem] * len(scalars)
        + [vmem] * len(arrays)
        + [pl.BlockSpec(memory_space=pl.ANY)] * len(distant),
        out_specs=[
            pl.BlockSpec(memory_space=pl.ANY) if place in away else vmem for place in range(len(outs))
        ],
        out_shape=shapes,
        scratch_shapes=[pltpu.VMEM(shape, dtype) for shape, dtype in scratch]
        + [pltpu.SemaphoreType.DMA] * (len(distant) + len(away)),
        interpret=INTERPRET,
    )(*scalars, *arrays, *distant)


def pick_heads(disc_ref):
    picks = [disc_ref[0, k] for k in range(4)]
    pairs = []
    for layer in (1, 0):
        first = jnp.where(picks[0] == layer, 0, jnp.where(picks[1] == layer, 1, 2))
        last = jnp.where(picks[3] == layer, 3, jnp.where(picks[2] == layer, 2, 1))
        pairs.append((first, last))
    return pairs


def level_of(time_ref):
    return time_ref[0:1] / 1000.0


def open_body(
    disc_ref,
    cond_ref,
    mod_ref,
    tmod_ref,
    embed_ref,
    proj_ref,
    taps_in_ref,
    head_out_ref,
    noise_in_ref,
    sent_ref,
    mods_ref,
    cross_ref,
    taps_ref,
    noise_ref,
    queries_ref,
    turned_ref,
    terms_ref,
    noise_sem,
    terms_sem,
):
    fetch = pltpu.make_async_copy(noise_in_ref, noise_ref, noise_sem)
    fetch.start()
    block, other = pick_heads(disc_ref)
    channels = proj_ref.shape[2]
    latent, width = embed_ref.shape

    groups = cond_ref.shape[0]
    copies, pieces, lanes = mods_ref.shape
    seqs = copies // groups
    half = contract(cond_ref[...], mod_ref[...].astype(F32), 1, 0, HIGHEST)
    for group in range(groups):
        row = half[group : group + 1]
        pieces_of = jnp.concatenate(
            [row[:, lanes * p : lanes * (p + 1)] for p in range(pieces)], axis=0
        )
        terms_ref[seqs * group : seqs * (group + 1)] = jnp.broadcast_to(
            pieces_of.astype(BF16)[None], (seqs, pieces, lanes)
        )
    store = pltpu.make_async_copy(terms_ref, mods_ref, terms_sem)
    store.start()

    rows = sent_ref.shape[0]
    start = pl.multiple_of((lax.axis_index("plane") % (width // rows)) * rows, rows)
    embed = embed_ref[...]
    gain = 1.0 + tmod_ref[1:2]
    queries = jnp.concatenate(
        [
            embed.astype(F32) * gain,
            gain,
            tmod_ref[0:1],
            jnp.zeros((128 - latent - 2, width), F32),
        ],
        axis=0,
    )
    queries_ref[...] = queries.T
    sent_ref[:, 2 * channels :] = queries_ref[pl.ds(start, rows), :].astype(BF16)
    for place, head in enumerate(block):
        sent_ref[:, channels * place : channels * (place + 1)] = proj_ref[head, pl.ds(start, rows), :]

    _, share, pair_lanes = cross_ref.shape
    per_head = channels // share
    begin = lax.axis_index("mp") * share
    slot = begin // channels
    offset = pl.multiple_of(begin % channels, 8)
    for place in range(2):
        both = jnp.concatenate(
            [contract(proj_ref[head], embed, 0, 1) for head in (block[place], other[place])], axis=1
        )
        cross_ref[per_head * place : per_head * (place + 1)] = (
            both.astype(BF16).reshape(per_head, share, pair_lanes)
        )
    for place, pair in enumerate((block, other)):
        head = jnp.where(slot == 0, pair[0], pair[1])
        table = jnp.concatenate(
            [taps_in_ref[tap, pl.ds(head, 1), :] for tap in range(9)]
            + [head_out_ref[pl.ds(head, 1), :], jnp.zeros((6, channels), F32)],
            axis=0,
        )
        turned_ref[...] = table.T
        taps_ref[share * place : share * (place + 1)] = turned_ref[pl.ds(offset, share), :]
    store.wait()
    fetch.wait()


def weight_body(got_ref, pair_ref, order_ref, out_ref, *, latent):
    del order_ref
    copies, all_rows, lanes = out_ref.shape
    rows = all_rows - 8
    depth = got_ref.shape[0] // 2
    half = pl.ds(pl.multiple_of(lax.axis_index("core") * (copies * rows), 128), copies * rows)
    down = jnp.concatenate([pair_ref[0:depth, half], pair_ref[2 * depth : 3 * depth, half]], axis=0)
    up = jnp.concatenate([pair_ref[depth : 2 * depth, half], pair_ref[3 * depth :, half]], axis=0)
    value = contract(down, got_ref[:, :lanes], 0, 0)
    query = contract(up, got_ref[:, lanes:], 0, 0).reshape(copies, rows, 128)
    pieces = [query[:, 8 * fold : 8 * (fold + 1)] for fold in range(rows // 8)]
    tail = jnp.concatenate(
        [piece[:, :, :latent] for piece in pieces]
        + [piece[:, :, latent : latent + 2] for piece in pieces]
        + [jnp.zeros((copies, 8, lanes - len(pieces) * (latent + 2)), F32)],
        axis=2,
    )
    out_ref[:, :rows] = value.astype(BF16).reshape(copies, rows, lanes)
    out_ref[:, rows:] = tail.astype(BF16)


def gather_body(parts_ref, order_ref, out_ref):
    del order_ref
    total = jnp.sum(parts_ref[...].astype(F32), axis=0).astype(BF16)
    out_ref[...] = jnp.broadcast_to(total[None], out_ref.shape)


def sums_body(hidden_ref, out_w_ref, embed_ref, mod_ref, sums_ref):
    copies, pieces, _ = mod_ref.shape
    latent, width = out_w_ref.shape
    tokens = hidden_ref.shape[0]
    halves = []
    for half in range(2):
        total = jnp.sum(mod_ref[copies // 2 * half : copies // 2 * (half + 1)].astype(F32), axis=0)
        halves.append(jnp.concatenate([total[p : p + 1] for p in range(pieces)], axis=1))
    shift, scale = halves
    hidden = hidden_ref[...]
    embed = embed_ref[...]
    out_w = out_w_ref[...].astype(F32)
    scaled = (out_w * (1.0 + scale)).astype(BF16)
    ones = jnp.ones((8, width), BF16)
    square = jnp.square(hidden.astype(F32))
    high = square.astype(BF16)
    low = (square - high.astype(F32)).astype(BF16)
    sums_ref[0:latent] = contract(scaled, hidden, 1, 1)
    gram = contract(embed, embed, 1, 1)
    fold = latent // 2
    sums_ref[latent : latent + fold] = jnp.concatenate([gram[:fold], gram[fold:]], axis=1)
    row = lax.broadcasted_iota(jnp.int32, (8, tokens), 0)
    firsts = contract(ones, hidden, 1, 1)
    squares = contract(ones, high, 1, 1) + contract(ones, low, 1, 1)
    pairs = jnp.concatenate([contract(ones, embed, 1, 1), contract(ones, scaled, 1, 1)], axis=1)
    shifted = contract(jnp.broadcast_to(shift, (8, width)), out_w, 1, 1, HIGHEST)
    shifted = jnp.concatenate([shifted, shifted], axis=1)
    sums_ref[latent + fold :] = jnp.where(
        row == 0, firsts, jnp.where(row == 1, squares, jnp.where(row == 2, pairs, shifted))
    )


def noise_body(time_ref, sums_ref, noise_ref, latents_ref, noised_ref, *, width):
    latent, tokens = noise_ref.shape
    base = latent + latent // 2
    mean = sums_ref[base : base + 1] / width
    var = sums_ref[base + 1 : base + 2] / width - mean * mean
    inv_std = lax.rsqrt(jnp.maximum(var, 0.0) + EPSILON)
    scaled_sum = sums_ref[base + 2 : base + 3, latent:]
    shifted_sum = sums_ref[base + 3 : base + 4, :latent]
    ones = jnp.ones((1, tokens), F32)
    centered = sums_ref[0:latent] - contract(scaled_sum, mean, 0, 0, HIGHEST)
    latents = inv_std * centered + contract(shifted_sum, ones, 0, 0, HIGHEST)
    latents = latents.astype(BF16)
    latents_ref[...] = latents
    level = level_of(time_ref)
    noised_ref[...] = (
        (1.0 - level) * latents.astype(F32) + level * noise_ref[...].astype(F32)
    ).astype(BF16)


def act_body(
    sums_ref,
    cross_noised_ref,
    pair_ref,
    weights_ref,
    cross_ref,
    out_ref,
    pre_ref,
    query_ref,
    side_ref,
    wide_ref,
    values_ref,
    act_ref,
    *,
    width,
):
    latent, extent = wide_ref.shape
    tokens = extent // 3
    chunks, all_rows, split = weights_ref.shape
    unit_rows = all_rows - 8
    copies, share, _ = out_ref.shape
    edge = cross_noised_ref[...]
    first = pair_ref[0:latent]
    second = pair_ref[latent:]
    noised_f = jnp.where(
        lax.axis_index("core") == 0,
        jnp.concatenate([edge, first, second], axis=1).astype(F32),
        jnp.concatenate([first, second, edge], axis=1).astype(F32),
    )
    noised = noised_f.astype(BF16)
    wide_ref[...] = noised
    base = latent + latent // 2
    center_row = sums_ref[base + 2 : base + 3, :latent] / width
    gram = jnp.concatenate([sums_ref[latent:base, :latent], sums_ref[latent:base, latent:]], axis=0)
    gram = gram - width * contract(center_row, center_row, 0, 0, HIGHEST)
    gram_noised = contract(gram, noised_f, 1, 0, HIGHEST)
    var = jnp.sum(noised_f * gram_noised, axis=0, keepdims=True) / width
    inv_std = lax.rsqrt(jnp.maximum(var, 0.0) + EPSILON)
    side_ref[0:latent] = gram_noised[:, tokens : 2 * tokens]
    side_ref[latent:] = jnp.broadcast_to(inv_std[:, tokens : 2 * tokens], (8, tokens))
    folds = unit_rows // 8
    base = folds * latent
    step = 4
    for begin in range(0, chunks, step):
        rows = slice(begin * unit_rows, (begin + step) * unit_rows)
        tail = weights_ref[begin : begin + step, unit_rows:].astype(F32)

        def unfold(start, stride, size):
            parts = [tail[:, :, start + stride * f : start + stride * f + size] for f in range(folds)]
            return jnp.concatenate(parts, axis=1).reshape(step * unit_rows, size)

        query = (unfold(0, latent, latent) - unfold(base, 2, 1) * center_row).astype(BF16)
        query_ref[rows] = query
        pre = contract(query, noised, 1, 0) * inv_std + unfold(base + 1, 2, 1)
        pre_ref[rows] = pre[:, tokens : 2 * tokens]
        act_ref[rows] = gelu_tanh(pre).astype(BF16)
        values_ref[rows] = weights_ref[begin : begin + step, :unit_rows].reshape(
            step * unit_rows, split
        )
    part = contract(values_ref[...], act_ref[...], 0, 0).astype(BF16)
    out_ref[:, :, :extent] = part.reshape(copies, share, extent)
    out_ref[:, :, extent:] = cross_ref[...]


def conv_body(
    parts_ref, wide_ref, taps_ref, pay_ref, back_ref, *, count
):
    _, share, _ = parts_ref.shape
    latent, extent = wide_ref.shape
    own = extent // 3
    channels = 2 * share
    noised = wide_ref[...]
    total = jnp.sum(parts_ref[...].astype(F32), axis=0)
    cross = jnp.concatenate(
        [total[:, extent : extent + latent], total[:, extent + latent :]], axis=0
    ).astype(BF16)
    embed = contract(cross, noised, 1, 0)
    field_in = jnp.concatenate([embed[:share] + total[:, :extent], embed[share:]], axis=0)
    lane = lax.broadcasted_iota(jnp.int32, (channels, extent), 1)
    at = seq_index()
    first = jnp.where(at == 0, own, 0)
    last = jnp.where(at == count - 1, 2 * own, extent)
    inside = (lane >= first) & (lane < last)
    column = lane % GRID_W
    left_ok = column > 0
    right_ok = column < GRID_W - 1

    def tap(row, col):
        place = 3 * row + col
        return taps_ref[:, place : place + 1]

    def convolve(grid, flip):
        before = jnp.where(left_ok, pltpu.roll(grid, 1, 1), 0.0)
        after = jnp.where(right_ok, pltpu.roll(grid, extent - 1, 1), 0.0)
        rows = []
        for row in range(3):
            if flip:
                rows.append(tap(row, 2) * before + tap(row, 1) * grid + tap(row, 0) * after)
            else:
                rows.append(tap(row, 0) * before + tap(row, 1) * grid + tap(row, 2) * after)
        if flip:
            rows = rows[::-1]
        return pltpu.roll(rows[0], GRID_W, 1) + rows[1] + pltpu.roll(rows[2], extent - GRID_W, 1)

    field = convolve(jnp.where(inside, field_in, 0.0), False)
    gating = jax.nn.sigmoid(field)
    scale = taps_ref[:, 9:10]
    terms = field * gating * scale
    slope = -scale * gating * (1.0 + field * (1.0 - gating))
    grad = convolve(jnp.where(inside, slope, 0.0), True)[:, own : 2 * own]
    block_sum = jnp.sum(terms[:share, own : 2 * own], axis=0, keepdims=True)
    embed_sum = jnp.sum(terms[share:, own : 2 * own], axis=0, keepdims=True)
    sums = jnp.concatenate([block_sum, embed_sum], axis=0)
    high = sums.astype(BF16).astype(F32)
    low = sums - high
    tail = jnp.concatenate([high, low, jnp.zeros((12, own), F32)], axis=0)
    pay = jnp.concatenate([grad[:share], tail], axis=0).astype(BF16)
    pay_ref[...] = jnp.broadcast_to(pay[None], pay_ref.shape)
    back_ref[...] = contract(cross, grad.astype(BF16), 0, 0)


def back_body(
    disc_ref,
    pay_ref,
    values_ref,
    query_ref,
    pre_ref,
    side_ref,
    noised_ref,
    back_ref,
    out_ref,
    logits_ref,
    *,
    width,
):
    copies, rows, tokens = pay_ref.shape
    share = rows - 16
    latent = noised_ref.shape[0]
    grads = jnp.concatenate([pay_ref[copy, :share] for copy in range(copies)], axis=0)
    hidden_grad = contract(values_ref[...], grads, 1, 0)
    preact_grad = (hidden_grad * gelu_slope(pre_ref[...])).astype(BF16)
    query_grad = contract(query_ref[...], preact_grad, 0, 0)
    inv_std = side_ref[latent : latent + 1]
    along = jnp.sum(noised_ref[...].astype(F32) * query_grad, axis=0, keepdims=True)
    result = (
        inv_std * (query_grad - (inv_std * inv_std / width) * along * side_ref[0:latent])
        + back_ref[...]
    )
    out_ref[...] = jnp.broadcast_to(result.astype(BF16)[None], out_ref.shape)
    sums = []
    for place in range(2):
        total = jnp.zeros((16, tokens), F32)
        for copy in range(copies // 2 * place, copies // 2 * (place + 1)):
            total = total + pay_ref[copy, share:].astype(F32)
        sums.append(total[0:2] + total[2:4])
    block, other = pick_heads(disc_ref)
    for k in range(4):
        chosen = jnp.where(block[0] == k, 0, jnp.where(block[1] == k, 1, jnp.where(other[0] == k, 2, 3)))
        options = [sums[0][0:1], sums[1][0:1], sums[0][1:2], sums[1][1:2]]
        value = options[3]
        for place in range(3):
            value = jnp.where(chosen == place, options[place], value)
        logits_ref[k : k + 1] = value


def final_body(time_ref, parts_ref, latents_ref, logits_ref, out_ref, latents_out_ref, logits_out_ref):
    retain = 1.0 - level_of(time_ref)
    out_ref[...] = retain * jnp.sum(parts_ref[...].astype(F32), axis=0)
    latents_out_ref[...] = latents_ref[...]
    logits_out_ref[...] = logits_ref[...]


def per_device(
    student_hidden,
    student_cond,
    student_mod,
    student_out,
    timestep,
    noise,
    teacher_embed,
    teacher_mod,
    up_weight,
    down_weight,
    head_proj,
    head_kernel,
    head_out,
    disc_layer,
):
    groups = lax.axis_size("group")
    planes = lax.axis_size("plane")
    seqs = 2 * planes
    mps = lax.axis_size("mp")
    _, tokens, local_width = student_hidden.shape
    width = local_width * mps
    latent = teacher_embed.shape[0]
    units = down_weight.shape[0]
    channels = head_proj.shape[2]
    share = 2 * channels // mps
    lanes = 2 * channels + 128
    extent = 3 * tokens

    half_freqs = teacher_mod.shape[0] // 2
    time = lax.optimization_barrier(jnp.broadcast_to(timestep[:, None], (1, half_freqs)))
    tmod = jnp.einsum(
        "sf,fjd->sjd",
        time_features(time, 2 * half_freqs),
        teacher_mod.astype(F32),
        precision=HIGHEST,
    )[0]
    time_row = jnp.broadcast_to(time[:, :tokens].astype(F32), (8, tokens))
    ratio = seqs // mps
    rows = 2 * local_width // ratio
    pieces = local_width // 128
    sent, mods, cross, taps, noise_t = call(
        open_body,
        [
            ((rows, lanes), BF16),
            ((groups * seqs, pieces, 128), BF16),
            ((mps, share, 2 * latent), BF16),
            ((2 * share, 16), F32),
            ((latent, tokens), BF16),
        ],
        [disc_layer],
        [
            student_cond,
            student_mod[:, 0],
            tmod,
            teacher_embed,
            head_proj,
            jnp.transpose(head_kernel, (1, 2, 0, 3)).reshape(9, 4, channels),
            head_out,
        ],
        [
            ((local_width, 128), F32),
            ((channels, 16), F32),
            ((groups * seqs, pieces, 128), BF16),
        ],
        away=(1,),
        distant=[noise[0].T],
        plain=(0, 1, 3, 5, 6),
    )

    swap = [
        (at * mps + m, (ratio * m + at % ratio) * mps + at // ratio)
        for at in range(seqs)
        for m in range(mps)
    ]
    got = lax.ppermute(sent, SEQ + ("mp",), swap)

    mods = exchange(mods, ("group",) + SEQ)
    slices = jnp.concatenate([down_weight.T, up_weight], axis=0)
    slices = lax.all_gather(slices, "core", axis=0, tiled=True)
    (terms,) = call(
        functools.partial(weight_body, latent=latent),
        [((planes, units // seqs + 8, 2 * channels), BF16)],
        [],
        [got, slices, mods],
    )
    terms = exchange(terms, "plane")
    (sums,) = call(
        sums_body,
        [((latent + latent // 2 + 8, tokens), F32)],
        [],
        [student_hidden[0], student_out.T, teacher_embed, mods],
    )
    stages = [sums]
    hops = [1 << bit for bit in range(mps.bit_length() - 1)]
    hops[:2] = hops[:2][::-1]
    for hop in hops:
        sums = sums + lax.ppermute(sums, "mp", [(i, i ^ hop) for i in range(mps)])
        stages.append(sums)
    halfway = stages[-2]
    (terms,) = call(gather_body, [((planes, units // seqs + 8, 2 * channels), BF16)], [], [terms, halfway])
    weights = exchange(terms, "plane")
    weights = lax.all_gather(weights, "core", axis=0, tiled=True)

    latents, noised = call(
        functools.partial(noise_body, width=float(width)),
        [((latent, tokens), BF16), ((latent, tokens), BF16)],
        [],
        [time_row, sums, noise_t],
    )
    swap = [(i, i + 1 if i % 2 else i - 1) for i in range(1, seqs - 1)]
    edge = lax.ppermute(noised, SEQ, swap)
    pair = lax.all_gather(noised, "core", axis=0, tiled=True)

    parts, preact, query, side, wide, values = call(
        functools.partial(act_body, width=float(width)),
        [
            ((mps, share, extent + 2 * latent), BF16),
            ((units, tokens), F32),
            ((units, latent), BF16),
            ((latent + 8, tokens), F32),
            ((latent, extent), BF16),
            ((units, 2 * channels), BF16),
        ],
        [],
        [sums, edge, pair, weights, cross],
        [((units, extent), BF16)],
    )
    parts = exchange(parts, "mp")
    pay, back = call(
        functools.partial(conv_body, count=seqs),
        [((mps, share + 16, tokens), BF16), ((latent, tokens), F32)],
        [],
        [parts, wide, taps],
    )
    pay = exchange(pay, "mp")
    back, logits = call(
        functools.partial(back_body, width=float(width)),
        [((mps, latent, tokens), BF16), ((4, tokens), F32)],
        [disc_layer],
        [pay, values, query, preact, side, noised, back],
    )
    back = exchange(back, "mp")
    latent_grad, latents, logits = call(
        final_body,
        [((latent, tokens), F32), ((latent, tokens), BF16), ((4, tokens), F32)],
        [],
        [time_row, back, latents, logits],
        loose=(0, 1, 2),
    )
    return (latents.T[None], logits[None], latent_grad.T[None])


def solution(mesh):
    groups, seqs, mps = mesh.devices.shape
    split = Mesh(
        mesh.devices.reshape(groups, seqs // 2, 2, mps), ("group", "plane", "core", "mp")
    )
    return jax.shard_map(
        per_device,
        mesh=split,
        in_specs=(
            P("group", SEQ, "mp"),
            P(None, SEQ),
            P(SEQ, "group", "mp"),
            P("mp", None),
            P("group"),
            P("group", SEQ, None),
            P(None, "mp"),
            P(None, None, "mp"),
            P(SEQ, "mp"),
            P("mp", SEQ),
            P(None, "mp", None),
            P(),
            P(),
            P("group", None),
        ),
        out_specs=(P("group", SEQ, None), P("group", None, SEQ), P("group", SEQ, None)),
        check_vma=False,
    )
```
